32 devices in a mesh: dp: 8 (over z, y), tensor: 4 (over x, core).
Axes of the slice: x: 2, y: 2, z: 4, core: 2. Of those that a mesh axis runs over, the one named last changes fastest.
Arguments:
- tokens: bfloat16 [2, 4096, 2048], P(None, ('dp', 'tensor')), may hold values from -6 to 6
- lengths: int32 [2, 8, 8], P(None, 'dp'), may hold values from 1 to 256, 512 in all within a row
- out_grad: bfloat16 [2, 4096, 2048], P(None, ('dp', 'tensor')), may hold values from -6 to 6
- attn_gain: bfloat16 [2048], P('dp'), may hold values from 0.25 to 1.75
- attn_shift: bfloat16 [2048], P('dp'), may hold values from -3 to 3
- mlp_gain: bfloat16 [2048], P('dp'), may hold values from 0.25 to 1.75
- mlp_shift: bfloat16 [2048], P('dp'), may hold values from -3 to 3
- w_qkv: bfloat16 [2048, 6144], P('dp', 'tensor'), may hold values from -0.125 to 0.125
- b_qkv: bfloat16 [6144], P('tensor'), may hold values from -3 to 3
- w_proj: bfloat16 [2048, 2048], P('tensor', 'dp'), may hold values from -0.5 to 0.5
- b_proj: bfloat16 [2048], P('dp'), may hold values from -3 to 3
- w_in: bfloat16 [2048, 8192], P('dp', 'tensor'), may hold values from -0.125 to 0.125
- b_in: bfloat16 [8192], P('tensor'), may hold values from -3 to 3
- w_out: bfloat16 [8192, 2048], P('tensor', 'dp'), may hold values from -0.09375 to 0.09375
- b_out: bfloat16 [2048], P('dp'), may hold values from -3 to 3
Outputs:
- output: bfloat16 [2, 4096, 2048], P(None, ('dp', 'tensor'))
- grad_tokens: float32 [2, 4096, 2048], P(None, ('dp', 'tensor'))
- grad_attn_gain: float32 [2048], P(('dp', 'tensor'))
- grad_attn_shift: float32 [2048], P(('dp', 'tensor'))
- grad_mlp_gain: float32 [2048], P(('dp', 'tensor'))
- grad_mlp_shift: float32 [2048], P(('dp', 'tensor'))
- grad_w_qkv: float32 [2048, 6144], P('dp', 'tensor')
- grad_b_qkv: float32 [4, 1536], P('tensor', 'dp')
- grad_w_proj: float32 [2048, 2048], P('tensor', 'dp')
- grad_b_proj: float32 [2048], P(('dp', 'tensor'))
- grad_w_in: float32 [2048, 8192], P('dp', 'tensor')
- grad_b_in: float32 [4, 2048], P('tensor', 'dp')
- grad_w_out: float32 [8192, 2048], P('tensor', 'dp')
- grad_b_out: float32 [2048], P(('dp', 'tensor'))
The draws below stay inside these ranges and needn't reach their ends.
Inputs may be any that keep to these rules, and one draw needn't show every extreme that they name: `lengths`: row [m, p] splits pack p of micro-batch m, 512 tokens, into 8 runs in order: 7 sequences, then padding; its largest entry is exactly 256.
All inputs are finite; a program needn't handle non-finite values.
Results may differ from the reference program's by a relative error of at most 0.014.
Values may be sent and summed in bfloat16 or wider, within the bound.
No kernel may reach another device: no remote copies, remote signals or barrier semaphores. Data moves between devices by JAX's collectives and lax.ppermute only.
A program may use at most 192 MiB of HBM per device.

```python
import math
import jax
import jax.numpy as jnp
import numpy as np
from jax import lax

D = 2048
H = 8
HD = 256
FF = 8192
ROT = 64
MICRO = 2
ROWS = 512
LONGEST = 256
SEGS = 8
TOKENS = 4096
N_DP = 8
N_TENSOR = 4


def steps_of(rng, shape, cuts, least, top_value):
    factor_of = 1.0
    for dim, blocks in cuts:
        steps = jax.random.uniform(jax.random.fold_in(jax.random.fold_in(rng, 6), dim), (blocks,), jnp.float32, least / len(cuts), top_value / len(cuts))
        factor_of = factor_of * jnp.repeat(jnp.exp(steps), shape[dim] // blocks).reshape((-1,) + (1,) * (len(shape) - 1 - dim))
    return factor_of


def length_profile(number_of, total, most, lean):
    loads = [(1 << 20) // math.isqrt(rank ** lean) + 1 for rank in range(2, number_of + 1)]
    rest, given = total - most - (number_of - 1), [1] * (number_of - 1)
    while rest > 0:
        candidates = [i for i in range(number_of - 1) if given[i] < most]
        pool, budget = sum([loads[i] for i in candidates]), rest
        for i in candidates:
            more = min(most - given[i], max(1, budget * loads[i] // pool), rest)
            given[i] = given[i] + more
            rest = rest - more
    return np.array([most] + given)


def ragged_sizes(key, number_of, total, bound, skew):
    if number_of == 2:
        one = jax.random.randint(key, (), max(1, total - bound), min(bound, total - 1) + 1)
        return jnp.stack([one, total - one])
    tallies = jnp.asarray(length_profile(number_of, total, bound, skew), jnp.int32)
    couples = (number_of - 1) // 2
    donor, taker = tallies[1:1 + 2 * couples:2], tallies[2:2 + 2 * couples:2]
    room = jnp.minimum(donor - 1, bound - taker)
    shifted = jax.random.randint(jax.random.fold_in(key, 1), (couples,), 0, 1 << 20) % (room + 1)
    tallies = tallies.at[1:1 + 2 * couples:2].set(donor - shifted).at[2:2 + 2 * couples:2].set(taker + shifted)
    return tallies[jax.random.permutation(jax.random.fold_in(key, 2), number_of)]


def gaussian(key, extent, deviation, reach, split=(), kind=jnp.bfloat16):
    entries = deviation * jax.random.normal(key, extent, jnp.float32)
    if split:
        entries = entries * steps_of(key, extent, split, -0.22, 0.18)
    return jnp.clip(entries, -reach, reach).astype(kind)


def setup_inputs(seed: int = 0) -> dict:
    seeds = jax.random.split(jax.random.key(seed), 16)
    return {
        "tokens": gaussian(seeds[0], (MICRO, TOKENS, D), 1.0, 6.0, ((1, 32),)),
        "lengths": jax.vmap(lambda own: ragged_sizes(own, SEGS, ROWS, LONGEST, 2))(jax.random.split(seeds[1], MICRO * N_DP)).reshape((MICRO, N_DP, SEGS)).astype(jnp.int32),
        "out_grad": gaussian(seeds[2], (MICRO, TOKENS, D), 1.0, 6.0, ((1, 32),)),
        "attn_gain": jnp.clip(1.0 + 0.15 * jax.random.normal(seeds[3], (D,), jnp.float32), 0.25, 1.75).astype(jnp.bfloat16),
        "attn_shift": gaussian(seeds[4], (D,), 0.3, 3.0, ((0, 8),)),
        "mlp_gain": jnp.clip(1.0 + 0.15 * jax.random.normal(seeds[5], (D,), jnp.float32), 0.25, 1.75).astype(jnp.bfloat16),
        "mlp_shift": gaussian(seeds[6], (D,), 0.3, 3.0, ((0, 8),)),
        "w_qkv": gaussian(seeds[7], (D, 3 * D), D ** -0.5, 0.125, ((0, 8), (1, 4))),
        "b_qkv": gaussian(seeds[8], (3 * D,), 0.3, 3.0, ((0, 4),)),
        "w_proj": gaussian(seeds[9], (D, D), (D // 16) ** -0.5, 0.5, ((0, 4), (1, 8))),
        "b_proj": gaussian(seeds[10], (D,), 0.3, 3.0, ((0, 8),)),
        "w_in": gaussian(seeds[11], (D, FF), D ** -0.5, 0.125, ((0, 8), (1, 4))),
        "b_in": gaussian(seeds[12], (FF,), 0.3, 3.0, ((0, 4),)),
        "w_out": gaussian(seeds[13], (FF, D), (FF // 2) ** -0.5, 0.09375, ((0, 4), (1, 8))),
        "b_out": gaussian(seeds[14], (D,), 0.3, 3.0, ((0, 8),)),
    }


@jax.custom_vjp
def low(v):
    return lax.optimization_barrier(v.astype(jnp.bfloat16)).astype(jnp.float32)

@jax.custom_vjp
def low_back(v):
    return v

def low_keep(v):
    return (low(v), None)

def low_pass(kept, grad):
    return (grad,)

def back_keep(v):
    return (v, None)

def back_low(kept, grad):
    return (low(grad),)
low.defvjp(low_keep, low_pass)
low_back.defvjp(back_keep, back_low)

def layer_norm(values, gain_vec, shift_vec):
    center = values - lax.optimization_barrier(jnp.mean(values, axis=-1, keepdims=True))
    spread = lax.optimization_barrier(jnp.mean(center * center, axis=-1, keepdims=True))
    return center * lax.rsqrt(spread + 1e-05) * gain_vec + shift_vec

def token_layout(run_lengths):
    seg_ends = jnp.cumsum(run_lengths, axis=-1)
    places = jnp.arange(ROWS, dtype=jnp.int32)
    passed = (places[:, None] >= seg_ends[..., None, :]).astype(jnp.int32)
    segment = lax.optimization_barrier(jnp.sum(passed, axis=-1))
    seg_start = lax.optimization_barrier(jnp.sum(passed * run_lengths[..., None, :], axis=-1))
    return (segment, places - seg_start)

def rotate(values, position, turn_sign):
    half_rot = ROT // 2
    inv_freq = 10000.0 ** (-2.0 * jnp.arange(half_rot, dtype=jnp.float32) / ROT)
    angle = position.astype(jnp.float32)[..., None] * inv_freq
    cosine = jnp.cos(angle)[..., None, :]
    sine_part = turn_sign * jnp.sin(angle)[..., None, :]
    low_half = values[..., :half_rot]
    high_half = values[..., half_rot:ROT]
    return jnp.concatenate([low_half * cosine - high_half * sine_part, high_half * cosine + low_half * sine_part, values[..., ROT:]], axis=-1)

def attend(block_data):
    query, key_rows, value, segment = block_data
    places = jnp.arange(ROWS, dtype=jnp.int32)
    allowed = (segment[:, None] == segment[None, :]) & (places[None, :] <= places[:, None])
    scores = jnp.einsum('qhe,khe->hqk', query, key_rows, precision=lax.Precision.HIGHEST) * HD ** (-0.5)
    scores = jnp.where(allowed[None], low_back(scores), -1e+30)
    weights = low(jax.nn.softmax(scores, axis=-1))
    return jnp.einsum('hqk,khe->qhe', weights, value, precision=lax.Precision.HIGHEST)

def forward(token_rows, segment, position, attn_gain, attn_shift, mlp_gain, mlp_shift, w_qkv, b_qkv, w_proj, b_proj, w_in, b_in, w_out, b_out):
    packs = token_rows.shape[0]
    flat_rows = token_rows.reshape(-1, D)
    attn_rows = low(layer_norm(flat_rows, attn_gain, attn_shift))
    mlp_rows = low(layer_norm(flat_rows, mlp_gain, mlp_shift))
    mixed = low_back(jnp.dot(attn_rows, w_qkv, precision=lax.Precision.HIGHEST) + b_qkv)
    mixed = mixed.reshape(packs, ROWS, H, 3, HD)
    query = low(rotate(mixed[..., 0, :], position, 1.0))
    key_rows = low(rotate(mixed[..., 1, :], position, 1.0))
    value = low(mixed[..., 2, :])
    context = lax.map(jax.checkpoint(attend), (query, key_rows, value, segment))
    context = low(low_back(context)).reshape(-1, D)
    hidden = low_back(jnp.dot(mlp_rows, w_in, precision=lax.Precision.HIGHEST) + b_in)
    active = low(jax.nn.gelu(hidden, approximate=False))
    branch = low_back(jnp.dot(context, w_proj, precision=lax.Precision.HIGHEST) + jnp.dot(active, w_out, precision=lax.Precision.HIGHEST))
    return (flat_rows + branch + b_proj + b_out).reshape(packs, ROWS, D)

def reference(tokens, lengths, out_grad, attn_gain, attn_shift, mlp_gain, mlp_shift, w_qkv, b_qkv, w_proj, b_proj, w_in, b_in, w_out, b_out):
    packs = MICRO * N_DP
    segment, position = token_layout(lengths.reshape(packs, SEGS))
    valid_rows = (segment < SEGS - 1).astype(jnp.float32)
    token_rows = tokens.astype(jnp.float32).reshape(packs, ROWS, D)
    params = tuple((p.astype(jnp.float32) for p in (attn_gain, attn_shift, mlp_gain, mlp_shift, w_qkv, b_qkv, w_proj, b_proj, w_in, b_in, w_out, b_out)))

    def apply(rows_in, *weights_in):
        return forward(rows_in, segment, position, *weights_in)
    result, pullback = jax.vjp(apply, token_rows, *params)
    grads = pullback(out_grad.astype(jnp.float32).reshape(packs, ROWS, D) * valid_rows[..., None])
    out_shape = (MICRO, N_DP * ROWS, D)
    return (result.reshape(out_shape).astype(jnp.bfloat16), grads[0].reshape(out_shape), grads[1], grads[2], grads[3], grads[4], grads[5], grads[6].reshape(N_TENSOR, -1), grads[7], grads[8], grads[9], grads[10].reshape(N_TENSOR, -1), grads[11], grads[12])
```

```python
import jax
import jax.numpy as jnp
from jax import lax
from jax.experimental import pallas as pl
from jax.experimental.pallas import tpu as pltpu
from jax.sharding import PartitionSpec as P

HD = 256
ROT = 64
MICRO = 2
ROWS = 512
SEGS = 8
AXES = ("dp", "tensor")
BF = jnp.bfloat16
F32 = jnp.float32
MIB = 1 << 20
SCALE = HD ** (-0.5)
ANY = pl.BlockSpec(memory_space=pl.ANY)


def swap(value, perm):
    return lax.ppermute(value, AXES, perm)


def dot_nn(a, b):
    return jnp.dot(a, b, preferred_element_type=F32)


def dot_nt(a, b):
    return lax.dot_general(a, b, (((1,), (1,)), ((), ())), preferred_element_type=F32)


def dot_tn(a, b):
    return lax.dot_general(a, b, (((0,), (0,)), ((), ())), preferred_element_type=F32)


def ordered(first, low, high, axis=0):
    return jnp.where(
        first,
        jnp.concatenate([low, high], axis=axis),
        jnp.concatenate([high, low], axis=axis),
    )


def shape_of(shape, dtype):
    return jax.ShapeDtypeStruct(shape, dtype)


def call(body, grid, in_specs, out_specs, out_shape, scratch, prefetch, flops, nbytes, vmem):
    return pl.pallas_call(
        body,
        out_shape=out_shape,
        grid_spec=pltpu.PrefetchScalarGridSpec(
            num_scalar_prefetch=prefetch,
            grid=grid,
            in_specs=in_specs,
            out_specs=out_specs,
            scratch_shapes=scratch,
        ),
        compiler_params=pltpu.CompilerParams(
            dimension_semantics=("arbitrary",) * len(grid), vmem_limit_bytes=vmem * MIB
        ),
        cost_estimate=pl.CostEstimate(
            flops=int(flops), bytes_accessed=int(nbytes), transcendentals=0
        ),
    )


class Gathered:
    def __init__(self, arrays, axis):
        self.arrays = arrays
        self.axis = axis
        own = arrays[0]
        self.block = own.shape[axis]
        self.other = own.shape[1 - axis]
        self.shape = (
            (4 * self.block, self.other) if axis == 0 else (self.other, 4 * self.block)
        )


def fetch(info, refs, scratch, sem, block, axis):
    def part(ref, index, place):
        if axis == 0:
            source = ref.at[pl.ds(index * block, block), :]
            target = scratch.at[pl.ds(pl.multiple_of(place * block, block), block), :]
        else:
            source = ref.at[:, pl.ds(index * block, block)]
            target = scratch.at[:, pl.ds(pl.multiple_of(place * block, block), block)]
        return pltpu.make_async_copy(source, target, sem)

    own, partner, far_mid, far_out = refs
    part(own, 0, info[0]).start()
    part(partner, 0, info[1]).start()

    @pl.when(info[4] == 1)
    def _():
        part(far_mid, 0, info[2]).start()
        part(far_mid, 1, info[3]).start()

    @pl.when(info[4] == 0)
    def _():
        part(far_out, 0, info[2]).start()
        part(far_out, 1, info[3]).start()

    part(own, 0, info[0]).wait()
    part(partner, 0, info[1]).wait()
    part(far_out, 0, info[2]).wait()
    part(far_out, 1, info[3]).wait()


def plain_of(rows):
    center = rows - jnp.mean(rows, axis=-1, keepdims=True)
    spread = lax.rsqrt(jnp.mean(center * center, axis=-1, keepdims=True) + 1e-05)
    return center * spread, spread


def norm_rows(x, vectors):
    n, width = x.shape
    tile = 256

    def body(x_ref, v_ref, a_ref, m_ref):
        plain, _ = plain_of(x_ref[...].astype(F32))
        a_ref[...] = (plain * v_ref[0:1] + v_ref[1:2]).astype(BF)
        m_ref[...] = (plain * v_ref[2:3] + v_ref[3:4]).astype(BF)

    rows = pl.BlockSpec((tile, width), lambda i: (i, 0))
    whole = pl.BlockSpec(vectors.shape, lambda i: (0, 0))
    return call(
        body, (n // tile,), [rows, whole], [rows, rows],
        [shape_of((n, width), BF)] * 2, [], 0, n * width * 10, n * width * 6, 40,
    )(x, vectors)


def feed(info, rows, weight, bias):
    n, width = rows.shape
    cols = weight.other
    tile = 512

    def body(info_ref, x_ref, b_ref, p0, p1, p2, p3, active_ref, slope_ref, w, sem):
        @pl.when(pl.program_id(0) == 0)
        def _():
            fetch(info_ref, (p0, p1, p2, p3), w, sem, weight.block, weight.axis)

        hidden = dot_nn(x_ref[...], w[...]) + b_ref[...]
        cdf = 0.5 * (1.0 + lax.erf(hidden * 0.7071067811865476))
        active_ref[...] = (hidden * cdf).astype(BF)
        slope_ref[...] = cdf + hidden * jnp.exp(-0.5 * hidden * hidden) * 0.3989422804014327

    out = pl.BlockSpec((tile, cols), lambda i, s: (i, 0))
    return call(
        body, (n // tile,),
        [
            pl.BlockSpec((tile, width), lambda i, s: (i, 0)),
            pl.BlockSpec((1, cols), lambda i, s: (0, 0)),
        ] + [ANY] * 4,
        [out, out],
        [shape_of((n, cols), BF), shape_of((n, cols), F32)],
        [pltpu.VMEM(weight.shape, BF), pltpu.SemaphoreType.DMA],
        1, 2 * n * width * cols, 2 * n * width + 6 * n * cols, 48,
    )(info, rows, bias, *weight.arrays)


def feed_back(info, rows, weight, slope, extra):
    n, width = rows.shape
    cols = weight.other
    kept = cols - extra
    tile = 512

    def body(info_ref, g_ref, s_ref, p0, p1, p2, p3, *refs):
        outs, (w, sem) = refs[:-2], refs[-2:]

        @pl.when(pl.program_id(0) == 0)
        def _():
            fetch(info_ref, (p0, p1, p2, p3), w, sem, weight.block, weight.axis)
            outs[1][...] = jnp.zeros_like(outs[1])

        back = dot_nt(g_ref[...], w[...])
        if extra:
            outs[2][...] = back[:, :extra].astype(BF)
        low = (back[:, extra:] * s_ref[...]).astype(BF)
        outs[0][...] = low
        outs[1][...] += jnp.sum(low.astype(F32), axis=0, keepdims=True)

    block = lambda width_of: pl.BlockSpec((tile, width_of), lambda i, s: (i, 0))
    out_specs = [block(kept), pl.BlockSpec((1, kept), lambda i, s: (0, 0))]
    out_shape = [shape_of((n, kept), BF), shape_of((1, kept), F32)]
    if extra:
        out_specs.append(block(extra))
        out_shape.append(shape_of((n, extra), BF))
    return call(
        body, (n // tile,), [block(width), block(kept)] + [ANY] * 4, out_specs, out_shape,
        [pltpu.VMEM(weight.shape, BF), pltpu.SemaphoreType.DMA],
        1, 2 * n * width * cols, 2 * n * width + 6 * n * cols, 48,
    )(info, rows, slope, *weight.arrays)


def turn(values, cosine, sine):
    lane = lax.broadcasted_iota(jnp.int32, values.shape, 1)
    half = ROT // 2
    partner = jnp.where(
        lane < half, pltpu.roll(values, 128 - half, 1), pltpu.roll(values, half, 1)
    )
    return values * cosine + partner * sine


def project(info, rows, weight, bias, cosine, sine):
    n, width = rows.shape
    cols = weight.other
    tile = 512

    def body(info_ref, x_ref, b_ref, c_ref, s_ref, p0, p1, p2, p3, out_ref, w, sem):
        @pl.when(pl.program_id(0) == 0)
        def _():
            fetch(info_ref, (p0, p1, p2, p3), w, sem, weight.block, weight.axis)

        mixed = dot_nn(x_ref[...], w[...]) + b_ref[...]
        for start in (0, HD):
            head = mixed[:, start : start + 128]
            out_ref[:, start : start + 128] = turn(head, c_ref[...], s_ref[...]).astype(BF)
            out_ref[:, start + 128 : start + HD] = mixed[:, start + 128 : start + HD].astype(BF)
        out_ref[:, 2 * HD :] = mixed[:, 2 * HD :].astype(BF)

    block = lambda width_of: pl.BlockSpec((tile, width_of), lambda i, s: (i, 0))
    return call(
        body, (n // tile,),
        [block(width), pl.BlockSpec((1, cols), lambda i, s: (0, 0)), block(128), block(128)]
        + [ANY] * 4,
        block(cols), shape_of((n, cols), BF),
        [pltpu.VMEM(weight.shape, BF), pltpu.SemaphoreType.DMA],
        1, 2 * n * width * cols, 2 * n * width + 4 * n * cols, 48,
    )(info, rows, bias, cosine, sine, *weight.arrays)


def attend(mixed, dcontext, cosine, sine, row_info, col_info):
    n, cols = mixed.shape
    share = n // 16
    lead = (2, 2, 2, MICRO, share)

    def body(q_ref, d_ref, c_ref, s_ref, r_ref, k_ref, ctx_ref, dm_ref, sum_ref):
        @pl.when(pl.program_id(0) == 0)
        def _():
            sum_ref[...] = jnp.zeros_like(sum_ref)

        load = lambda ref: ref[...].reshape(ROWS, ref.shape[-1])
        qkv = load(q_ref)
        query, key, value = qkv[:, :HD], qkv[:, HD : 2 * HD], qkv[:, 2 * HD :]
        dctx = load(d_ref)
        cos, sin = load(c_ref), load(s_ref)
        allowed = (r_ref[0, :, 0:1] == k_ref[0, 0:1, :]) & (k_ref[0, 1:2, :] <= r_ref[0, :, 1:2])
        scores = jnp.where(allowed, dot_nt(query, key) * SCALE, -1e30)
        expos = jnp.exp(scores - jnp.max(scores, axis=-1, keepdims=True))
        soft = expos / jnp.sum(expos, axis=-1, keepdims=True)
        probs = soft.astype(BF)
        ctx_ref[...] = dot_nn(probs, value).astype(BF).reshape(ctx_ref.shape)
        dprobs = dot_nt(dctx, value)
        dscores = soft * (dprobs - jnp.sum(soft * dprobs, axis=-1, keepdims=True))
        dscores = dscores.astype(BF)
        dvalue = dot_tn(probs, dctx)
        dquery = dot_nn(dscores, key) * SCALE
        dkey = dot_tn(dscores, query) * SCALE
        pieces = []
        for part in (dquery, dkey):
            pieces += [turn(part[:, :128], cos, -sin), part[:, 128:]]
        pieces.append(dvalue)
        low = jnp.concatenate(pieces, axis=1).astype(BF)
        dm_ref[...] = low.reshape(dm_ref.shape)
        sum_ref[...] += jnp.sum(low.astype(F32), axis=0, keepdims=True)

    view = lambda a: a.reshape(lead + (a.shape[-1],))
    block = lambda w: pl.BlockSpec(
        (2, 1, 2, 1, share, w), lambda p: (0, p % 2, 0, p // 2, 0, 0)
    )
    info = lambda a: pl.BlockSpec((1,) + a.shape[1:], lambda p: (p, 0, 0))
    packs = MICRO * 2
    context, dmixed, sums = call(
        body, (packs,),
        [block(cols), block(HD), block(128), block(128), info(row_info), info(col_info)],
        [block(HD), block(cols), pl.BlockSpec((1, cols), lambda p: (0, 0))],
        [shape_of(lead + (HD,), BF), shape_of(lead + (cols,), BF), shape_of((1, cols), F32)],
        [], 0, packs * 7 * 2 * ROWS * ROWS * HD, n * cols * 6, 48,
    )(view(mixed), view(dcontext), view(cosine), view(sine), row_info, col_info)
    return context.reshape(n, HD), dmixed.reshape(n, cols), sums


def out_rows(info, half, parts, weights):
    n = parts[0].shape[0] // 2
    width = weights[0].shape[1]
    tile = 256
    steps = n // tile
    count = len(parts)

    def body(info_ref, *refs):
        a_refs, w_refs = refs[:count], refs[count : 5 * count]
        out_ref = refs[5 * count]
        scratch = refs[5 * count + 1 : -1]
        sem = refs[-1]

        @pl.when(pl.program_id(0) == 0)
        def _():
            for i, weight in enumerate(weights):
                fetch(info_ref, w_refs[4 * i : 4 * i + 4], scratch[i], sem, weight.block, weight.axis)

        total = dot_nn(a_refs[0][...], scratch[0][...])
        for i in range(1, count):
            total += dot_nn(a_refs[i][...], scratch[i][...])
        out_ref[...] = total.astype(BF)

    ks = sum(weight.other for weight in weights)
    return call(
        body, (steps,),
        [
            pl.BlockSpec((tile, part.shape[1]), lambda i, s: (half * steps + i, 0))
            for part in parts
        ] + [ANY] * (4 * count),
        pl.BlockSpec((tile, width), lambda i, s: (i, 0)),
        shape_of((n, width), BF),
        [pltpu.VMEM(weight.shape, BF) for weight in weights] + [pltpu.SemaphoreType.DMA],
        1, 2 * n * width * ks, 2 * n * (width + ks), 48,
    )(info, *parts, *[array for weight in weights for array in weight.arrays])


def back_rows(info, half, dmixed, dhidden, w_qkv, w_in, x, vectors):
    n = x.shape[0] // 2
    width = x.shape[1]
    tile = 256
    steps = n // tile
    count = len(dhidden)
    weights = [w_qkv] + list(w_in)

    def body(info_ref, x_ref, v_ref, *refs):
        a_refs = refs[: count + 1]
        w_refs = refs[count + 1 : 5 * (count + 1)]
        out_ref, sum_ref = refs[5 * (count + 1) : 5 * (count + 1) + 2]
        scratch, sem = refs[5 * (count + 1) + 2 : -1], refs[-1]

        @pl.when(pl.program_id(0) == 0)
        def _():
            for i, weight in enumerate(weights):
                fetch(info_ref, w_refs[4 * i : 4 * i + 4], scratch[i], sem, weight.block, weight.axis)
            sum_ref[...] = jnp.zeros_like(sum_ref)

        plain, _ = plain_of(x_ref[...].astype(F32))
        dattn = dot_nt(a_refs[0][...], scratch[0][...])
        dmlp = dot_nt(a_refs[1][...], scratch[1][...])
        for i in range(2, count + 1):
            dmlp += dot_nt(a_refs[i][...], scratch[i][...])
        out_ref[...] = (dattn * v_ref[0:1] + dmlp * v_ref[2:3]).astype(BF)
        for i, grad in enumerate((dattn, dmlp)):
            sum_ref[2 * i : 2 * i + 1] += jnp.sum(grad * plain, axis=0, keepdims=True)
            sum_ref[2 * i + 1 : 2 * i + 2] += jnp.sum(grad, axis=0, keepdims=True)

    parts = [dmixed] + list(dhidden)
    ks = sum(part.shape[1] for part in parts)
    return call(
        body, (steps,),
        [
            pl.BlockSpec((tile, width), lambda i, s: (half * steps + i, 0)),
            pl.BlockSpec(vectors.shape, lambda i, s: (0, 0)),
        ] + [
            pl.BlockSpec((tile, part.shape[1]), lambda i, s: (half * steps + i, 0))
            for part in parts
        ] + [ANY] * (4 * (count + 1)),
        [pl.BlockSpec((tile, width), lambda i, s: (i, 0)), pl.BlockSpec((4, width), lambda i, s: (0, 0))],
        [shape_of((n, width), BF), shape_of((4, width), F32)],
        [pltpu.VMEM(weight.shape, BF) for weight in weights] + [pltpu.SemaphoreType.DMA],
        1, 2 * n * width * ks, 2 * n * (2 * width + ks), 56,
    )(info, x, vectors, *parts, *[array for weight in weights for array in weight.arrays])


def layer_program(n_dp, n_tensor):
    n_z = n_dp // 2
    n_dev = n_dp * n_tensor
    core, xbit, ybit, zbit = 1, 2, 4, 8
    ids = range(n_dev)
    flip = lambda bit: [(i, i ^ bit) for i in ids]
    flip_c, flip_x, flip_y, flip_z = flip(core), flip(xbit), flip(ybit), flip(zbit)
    place_z = lambda i: i // zbit
    mid = [(i, (3 - place_z(i)) * zbit + i % zbit) for i in ids if place_z(i) in (1, 2)]
    outward = [(i, i ^ zbit) for i in ids if place_z(i) in (1, 2)]
    inward = [(i, i ^ zbit) for i in ids if place_z(i) in (0, 3)]
    columns = [[z * 2 + y for z in range(n_z)] for y in range(2)]

    def per_device(
        tokens, lengths, out_grad, attn_gain, attn_shift, mlp_gain, mlp_shift,
        w_qkv, b_qkv, w_proj, b_proj, w_in, b_in, w_out, b_out,
    ):
        dp = lax.axis_index("dp")
        tensor = lax.axis_index("tensor")
        z, y = dp // 2, dp % 2
        x, c = tensor // 2, tensor % 2
        share = tokens.shape[1]
        width = tokens.shape[2]
        upper = z >= 2
        even = z % 2 == 0
        token = [None]

        def turn_of(*values):
            if token[0] is None:
                return values if len(values) > 1 else values[0]
            out = lax.optimization_barrier(values + (token[0],))[:-1]
            return out if len(out) > 1 else out[0]

        def passed(value):
            token[0] = value

        if n_z == 4:
            far = jnp.where(upper, 1, 2)
            info = jnp.stack(
                [z, z ^ 1, far, far ^ 1, ((z == 1) | (z == 2)).astype(jnp.int32)]
            ).astype(jnp.int32)
        else:
            info = jnp.array([0, 1, 2, 3, 1], jnp.int32)

        def pair_up(mine, theirs, axis):
            return ordered(y == 0, mine, swap(theirs, flip_y), axis)

        class Chunk:
            def __init__(self, mine, theirs, axis):
                self.axis = axis
                self.pair = pair_up(mine, theirs, axis)

            def step_a(self):
                if n_z == 4:
                    self.partner = swap(turn_of(self.pair), flip_z)

            def step_b(self):
                if n_z == 4:
                    both = jnp.concatenate([self.pair, self.partner], axis=self.axis)
                    self.from_mid = swap(turn_of(both), mid)

            def step_c(self):
                if n_z == 4:
                    far = swap(turn_of(self.from_mid), outward)
                    arrays = (self.pair, self.partner, self.from_mid, far)
                else:
                    whole = lax.all_gather(
                        self.pair, "dp", axis_index_groups=columns, tiled=True, axis=self.axis
                    )
                    quarter = jnp.split(whole, 4, axis=self.axis)
                    half = jnp.concatenate(quarter[2:], axis=self.axis)
                    arrays = (quarter[0], quarter[1], half, half)
                self.full = Gathered(arrays, self.axis)

        class Scatter:
            def __init__(self, total, axis):
                self.axis = axis
                self.total = total.astype(BF)

            def halves(self, value):
                return jnp.split(value, 2, axis=self.axis)

            def step_c(self):
                if n_z == 4:
                    low, high = self.halves(self.total)
                    self.far = jnp.where(upper, low, high)
                    self.near = jnp.where(upper, high, low)
                    self.got = swap(turn_of(self.far), inward)

            def step_b(self):
                if n_z == 4:
                    far = (self.far.astype(F32) + self.got.astype(F32)).astype(BF)
                    self.got = swap(turn_of(far), mid)

            def step_a(self):
                if n_z == 4:
                    near = self.near.astype(F32) + self.got.astype(F32)
                    low, high = self.halves(near)
                    self.own = jnp.where(even, low, high)
                    other = jnp.where(even, high, low).astype(BF)
                    self.got = swap(turn_of(other), flip_z)

            def step_y(self):
                if n_z == 4:
                    own = self.own + self.got.astype(F32)
                else:
                    own = lax.psum_scatter(
                        self.total, "dp", scatter_dimension=self.axis,
                        axis_index_groups=columns, tiled=True,
                    ).astype(F32)
                low, high = self.halves(own)
                self.mine = jnp.where(y == 0, low, high)
                other = jnp.where(y == 0, high, low).astype(BF)
                self.theirs = swap(other, flip_y).astype(F32)

        vectors = jnp.stack([attn_gain, attn_shift, mlp_gain, mlp_shift, b_proj, b_out])
        pair = ordered(y == 0, vectors[None], swap(vectors, flip_y)[None])
        if n_z == 4:
            far = [swap(pair, flip(zbit * k)) for k in (1, 2, 3)]
            small = ordered(~upper, ordered(even, pair, far[0]), ordered(even, far[1], far[2]))
        else:
            small = lax.all_gather(pair, "dp", axis_index_groups=columns, tiled=True)
        small = small.transpose(1, 0, 2).reshape(6, width).astype(F32)
        small = jnp.concatenate([small, jnp.zeros((2, width), F32)])
        lengths_all = jnp.stack([lengths[:, 0], swap(lengths[:, 0], flip_y)])

        h_cols = w_in.shape[1] // 2
        half_h = h_cols // 2
        q_cols = w_qkv.shape[1] // 2
        p_cols = w_proj.shape[0] // 2

        def cut(weight, sub, start, count, axis, side):
            return lax.dynamic_slice_in_dim(weight, side * sub + start, count, axis)

        def in_chunk(weight, sub, start, count):
            mine, theirs = (cut(weight, sub, start, count, 1, side) for side in (y, 1 - y))
            return Chunk(mine, theirs, 0)

        def out_chunk(*cuts):
            mine, theirs = (
                jnp.concatenate([cut(*piece, 0, side) for piece in cuts]) for side in (y, 1 - y)
            )
            return Chunk(mine, theirs, 1)

        c_in0 = in_chunk(w_in, h_cols, 0, half_h)
        c_out0 = out_chunk((w_proj, p_cols, 0, p_cols), (w_out, h_cols, 0, half_h))
        c_qkv = in_chunk(w_qkv, q_cols, 0, q_cols)
        c_in1 = in_chunk(w_in, h_cols, half_h, half_h)
        c_out1 = out_chunk((w_out, h_cols, half_h, half_h))

        def gather_plane(own):
            own = own.reshape(MICRO, share, width)
            from_x = swap(own, flip_x)
            from_y = swap(own, flip_y)
            diagonal = jnp.stack([swap(from_x[0], flip_y), swap(from_y[1], flip_x)])
            mine = jnp.stack([own, from_x, from_y, diagonal])
            return jnp.stack([mine, swap(mine, flip_c)]).reshape(-1, width)

        def scatter_plane(keep, give):
            total = (keep.astype(F32) + swap(give, flip_c).astype(F32)).astype(BF)
            total = total.reshape(2, 2, MICRO, share, width)
            by_y = total[0, :, 0].astype(F32) + swap(total[1, :, 0], flip_y).astype(F32)
            by_x = total[:, 0, 1].astype(F32) + swap(total[:, 1, 1], flip_x).astype(F32)
            first = by_y[0] + swap(by_y[1].astype(BF), flip_x).astype(F32)
            second = by_x[0] + swap(by_x[1].astype(BF), flip_y).astype(F32)
            return jnp.stack([first, second])

        pair_bits = jnp.arange(2, dtype=jnp.int32)
        t_of = (x ^ pair_bits)[None, :] * 2 + (c ^ pair_bits)[:, None]
        places = (t_of[..., None] * share + jnp.arange(share, dtype=jnp.int32)).reshape(-1)
        ends = jnp.cumsum(lengths_all, axis=-1)
        gone = (places[:, None] >= ends[..., None, :]).astype(jnp.int32)
        segment = jnp.sum(gone, axis=-1)
        position = places - jnp.sum(gone * lengths_all[..., None, :], axis=-1)
        valid = (segment[0, :, :share] < SEGS - 1).astype(F32)[..., None]

        inv_freq = 10000.0 ** (-2.0 * jnp.arange(ROT // 2, dtype=F32) / ROT)
        row_position = position.reshape(2, MICRO, 2, 2, share).transpose(2, 0, 3, 1, 4).reshape(-1)
        angle = row_position.astype(F32)[:, None] * inv_freq
        cos, sin = jnp.cos(angle), jnp.sin(angle)
        cosine = jnp.concatenate([cos, cos, jnp.ones((cos.shape[0], 64), F32)], axis=1)
        sine = jnp.concatenate([-sin, sin, jnp.zeros((cos.shape[0], 64), F32)], axis=1)
        pack_segment = segment.transpose(1, 0, 2).reshape(MICRO * 2, ROWS)
        pack_places = jnp.broadcast_to(places, (MICRO * 2, ROWS))
        row_info = jnp.stack([pack_segment, pack_places], axis=2)
        col_info = jnp.stack([pack_segment, pack_places], axis=1)

        x_own = tokens.astype(F32)
        g_own = out_grad.astype(F32) * valid

        c_in0.step_a()
        x_all = gather_plane(tokens)
        c_in0.step_b()
        c_out0.step_a()
        g_all = gather_plane(g_own.astype(BF))
        attn_rows, mlp_rows = norm_rows(x_all, small)
        c_in0.step_c()
        c_out0.step_b()
        c_qkv.step_a()
        passed(attn_rows)

        bias_in = lax.dynamic_slice_in_dim(b_in, y * h_cols, h_cols).astype(F32)[None]
        bias_qkv = lax.dynamic_slice_in_dim(b_qkv, y * q_cols, q_cols).astype(F32)[None]

        active_0, slope_0 = feed(info, turn_of(mlp_rows), c_in0.full, bias_in[:, :half_h])
        passed(active_0)
        s_out0 = Scatter(dot_tn(turn_of(active_0), g_all), 1)
        passed(s_out0.total)
        s_out0.step_c()
        c_out0.step_c()
        c_qkv.step_b()
        c_in1.step_a()

        dhidden_0, dsum_0, dcontext = feed_back(
            info, turn_of(g_all), c_out0.full, slope_0, p_cols
        )
        passed(dhidden_0)
        s_out0.step_b()
        s_in0 = Scatter(dot_tn(turn_of(mlp_rows), dhidden_0), 0)
        passed(s_in0.total)
        s_in0.step_c()
        c_qkv.step_c()
        c_in1.step_b()
        c_out1.step_a()

        mixed = project(info, turn_of(attn_rows), c_qkv.full, bias_qkv, cosine, sine)
        passed(mixed)
        s_out0.step_a()
        s_in0.step_b()
        context, dmixed, dmixed_sum = attend(
            turn_of(mixed), dcontext, cosine, sine, row_info, col_info
        )
        passed(dmixed)
        c_in1.step_c()
        c_out1.step_b()
        s_qkv = Scatter(dot_tn(turn_of(attn_rows), dmixed), 0)
        passed(s_qkv.total)
        s_qkv.step_c()
        s_in0.step_a()

        active_1, slope_1 = feed(info, turn_of(mlp_rows), c_in1.full, bias_in[:, half_h:])
        passed(active_1)
        c_out1.step_c()
        s_qkv.step_b()
        s_out1 = Scatter(
            dot_tn(jnp.concatenate([turn_of(active_1), context], axis=1), g_all), 1
        )
        passed(s_out1.total)
        s_out1.step_c()
        s_qkv.step_a()

        dhidden_1, dsum_1 = feed_back(info, turn_of(g_all), c_out1.full, slope_1, 0)
        passed(dhidden_1)
        s_out1.step_b()
        s_in1 = Scatter(dot_tn(turn_of(mlp_rows), dhidden_1), 0)
        passed(s_in1.total)
        s_in1.step_c()

        back_give, sums_give = back_rows(
            info, 1, turn_of(dmixed), (dhidden_0, dhidden_1), c_qkv.full,
            (c_in0.full, c_in1.full), x_all, small,
        )
        passed(back_give)
        s_out1.step_a()
        s_in1.step_b()
        back_keep, sums_keep = back_rows(
            info, 0, turn_of(dmixed), (dhidden_0, dhidden_1), c_qkv.full,
            (c_in0.full, c_in1.full), x_all, small,
        )
        passed(back_keep)
        s_in1.step_a()
        back = scatter_plane(back_keep, back_give)

        parts = (jnp.concatenate([context, active_0], axis=1), active_1)
        weights = (c_out0.full, c_out1.full)
        out_give = out_rows(info, 1, (turn_of(parts[0]), parts[1]), weights)
        passed(out_give)
        out_keep = out_rows(info, 0, (turn_of(parts[0]), parts[1]), weights)
        branch = scatter_plane(out_keep, out_give)
        output = (x_own + branch + small[4] + small[5]).astype(BF)

        own_plain, own_spread = plain_of(x_own)
        grad_tokens = g_own + own_spread * (
            back
            - jnp.mean(back, axis=-1, keepdims=True)
            - own_plain * jnp.mean(back * own_plain, axis=-1, keepdims=True)
        )

        g_sum = jnp.sum(g_own, axis=(0, 1))[None]
        sums = jnp.concatenate([sums_keep + sums_give, g_sum])
        sums = sums.reshape(5, n_dev, -1).transpose(1, 0, 2).reshape(n_dev, -1)
        dhidden_sum = jnp.concatenate([dsum_0, dsum_1], axis=1)
        bias_sums = jnp.concatenate(
            [dhidden_sum.reshape(n_dp // 2, -1), dmixed_sum.reshape(n_dp // 2, -1)], axis=-1
        )
        spread_bias = jnp.zeros((n_dp, n_tensor, bias_sums.shape[-1]), F32)
        spread_bias = lax.dynamic_update_slice(
            spread_bias, bias_sums[:, None], (y * (n_dp // 2), tensor, 0)
        ).reshape(n_dev, -1)
        total = jnp.concatenate([sums, spread_bias], axis=-1).reshape(n_z, 2, 2, 2, -1)
        for axis, bit, perm in ((3, c, flip_c), (2, x, flip_x), (1, y, flip_y)):
            low, high = jnp.split(total, 2, axis=axis)
            total = jnp.where(bit == 0, low, high) + swap(
                jnp.where(bit == 0, high, low), perm
            )
        total = total.reshape(n_z, -1)
        if n_z == 4:
            row = lambda k: lax.dynamic_slice_in_dim(total, z ^ k, 1, 0)
            vector_sums = row(0)
            for k in (1, 2, 3):
                vector_sums += swap(row(k), flip(zbit * k))
            vector_sums = vector_sums.reshape(-1)
        else:
            vector_sums = lax.psum_scatter(
                total.reshape(-1), "dp", axis_index_groups=columns, tiled=True
            )
        piece = width // n_dev
        pieces = [vector_sums[k * piece : (k + 1) * piece] for k in range(5)]
        bias_piece = vector_sums[5 * piece :]
        in_piece = b_in.shape[0] // n_dp

        def columns_of(axis, *parts):
            mine = jnp.concatenate([part[0] for part in parts], axis=axis)
            theirs = jnp.concatenate([part[1] for part in parts], axis=axis)
            return ordered(y == 0, mine, theirs, axis)

        for part in (s_out0, s_in0, s_qkv, s_out1, s_in1):
            part.step_y()
        both = lambda part: (part.mine, part.theirs)
        out1 = [value[:half_h] for value in both(s_out1)]
        proj = [value[half_h:] for value in both(s_out1)]

        return (
            output,
            grad_tokens,
            pieces[0],
            pieces[1],
            pieces[2],
            pieces[3],
            columns_of(1, both(s_qkv)),
            bias_piece[in_piece:].reshape(1, -1),
            columns_of(0, proj),
            pieces[4],
            columns_of(1, both(s_in0), both(s_in1)),
            bias_piece[:in_piece].reshape(1, -1),
            columns_of(0, both(s_out0), out1),
            pieces[4],
        )

    return per_device


def solution(mesh):
    n_dp, n_tensor = mesh.shape["dp"], mesh.shape["tensor"]
    rows = P(None, AXES, None)
    in_specs = (
        rows, P(None, "dp", None), rows, P("dp"), P("dp"), P("dp"), P("dp"),
        P("dp", "tensor"), P("tensor"), P("tensor", "dp"), P("dp"),
        P("dp", "tensor"), P("tensor"), P("tensor", "dp"), P("dp"),
    )
    vector = P(AXES)
    out_specs = (
        rows, rows, vector, vector, vector, vector,
        P("dp", "tensor"), P("tensor", "dp"), P("tensor", "dp"), vector,
        P("dp", "tensor"), P("tensor", "dp"), P("tensor", "dp"), vector,
    )
    return jax.shard_map(
        layer_program(n_dp, n_tensor), mesh=mesh,
        in_specs=in_specs, out_specs=out_specs, check_vma=False,
    )
```

```python
import jax
import jax.numpy as jnp
from jax import lax
from jax.experimental import pallas as pl
from jax.experimental.pallas import tpu as pltpu
from jax.sharding import PartitionSpec as P

HD = 256
ROT = 64
MICRO = 2
ROWS = 512
SEGS = 8
AXES = ("dp", "tensor")
BF = jnp.bfloat16
F32 = jnp.float32
MIB = 1 << 20
SCALE = HD ** (-0.5)
ANY = pl.BlockSpec(memory_space=pl.ANY)


def swap(value, perm):
    return lax.ppermute(value, AXES, perm)


def dot_nn(a, b):
    return jnp.dot(a, b, preferred_element_type=F32)


def dot_nt(a, b):
    return lax.dot_general(a, b, (((1,), (1,)), ((), ())), preferred_element_type=F32)


def dot_tn(a, b):
    return lax.dot_general(a, b, (((0,), (0,)), ((), ())), preferred_element_type=F32)


def ordered(first, low, high, axis=0):
    return jnp.where(
        first,
        jnp.concatenate([low, high], axis=axis),
        jnp.concatenate([high, low], axis=axis),
    )


def shape_of(shape, dtype):
    return jax.ShapeDtypeStruct(shape, dtype)


def call(body, grid, in_specs, out_specs, out_shape, scratch, prefetch, flops, nbytes, vmem):
    return pl.pallas_call(
        body,
        out_shape=out_shape,
        grid_spec=pltpu.PrefetchScalarGridSpec(
            num_scalar_prefetch=prefetch,
            grid=grid,
            in_specs=in_specs,
            out_specs=out_specs,
            scratch_shapes=scratch,
        ),
        compiler_params=pltpu.CompilerParams(
            dimension_semantics=("arbitrary",) * len(grid), vmem_limit_bytes=vmem * MIB
        ),
        cost_estimate=pl.CostEstimate(
            flops=int(flops) // 50, bytes_accessed=int(nbytes) // 50, transcendentals=0
        ),
    )


class Gathered:
    def __init__(self, arrays):
        self.arrays = arrays
        self.block, self.other = arrays[0].shape
        self.shape = (4 * self.block, self.other)


def fetch(info, refs, scratch, sem, block):
    def part(ref, index, place):
        source = ref.at[pl.ds(index * block, block), :]
        target = scratch.at[pl.ds(pl.multiple_of(place * block, block), block), :]
        return pltpu.make_async_copy(source, target, sem)

    own, partner, far_mid, far_out = refs
    part(own, 0, info[0]).start()
    part(partner, 0, info[1]).start()

    @pl.when(info[4] == 1)
    def _():
        part(far_mid, 0, info[2]).start()
        part(far_mid, 1, info[3]).start()

    @pl.when(info[4] == 0)
    def _():
        part(far_out, 0, info[2]).start()
        part(far_out, 1, info[3]).start()

    part(own, 0, info[0]).wait()
    part(partner, 0, info[1]).wait()
    part(far_out, 0, info[2]).wait()
    part(far_out, 1, info[3]).wait()


def plain_of(rows):
    center = rows - jnp.mean(rows, axis=-1, keepdims=True)
    spread = lax.rsqrt(jnp.mean(center * center, axis=-1, keepdims=True) + 1e-05)
    return center * spread, spread


def norm_rows(mine, sibling, vectors):
    n, width = mine.shape
    tile = 256
    steps = n // tile

    def body(x_ref, y_ref, v_ref, a_ref, m_ref):
        def write(rows):
            plain, _ = plain_of(rows.astype(F32))
            a_ref[...] = (plain * v_ref[0:1] + v_ref[1:2]).astype(BF)
            m_ref[...] = (plain * v_ref[2:3] + v_ref[3:4]).astype(BF)

        @pl.when(pl.program_id(0) < steps)
        def _():
            write(x_ref[...])

        @pl.when(pl.program_id(0) >= steps)
        def _():
            write(y_ref[...])

    rows = pl.BlockSpec((tile, width), lambda i: (i, 0))
    return call(
        body, (2 * steps,),
        [
            pl.BlockSpec((tile, width), lambda i: (jnp.minimum(i, steps - 1), 0)),
            pl.BlockSpec((tile, width), lambda i: (jnp.maximum(i - steps, 0), 0)),
            pl.BlockSpec(vectors.shape, lambda i: (0, 0)),
        ],
        [rows, rows],
        [shape_of((2 * n, width), BF)] * 2, [], 0, 2 * n * width * 10, 2 * n * width * 6, 14,
    )(mine, sibling, vectors)


def feed(info, rows, weight, bias):
    n, width = rows.shape
    cols = weight.other
    tile = 512

    def body(info_ref, x_ref, b_ref, p0, p1, p2, p3, active_ref, slope_ref, w, sem):
        @pl.when(pl.program_id(0) == 0)
        def _():
            fetch(info_ref, (p0, p1, p2, p3), w, sem, weight.block)

        hidden = dot_nn(x_ref[...], w[...]) + b_ref[...]
        cdf = 0.5 * (1.0 + lax.erf(hidden * 0.7071067811865476))
        active_ref[...] = (hidden * cdf).astype(BF)
        slope_ref[...] = cdf + hidden * jnp.exp(-0.5 * hidden * hidden) * 0.3989422804014327

    out = pl.BlockSpec((tile, cols), lambda i, s: (i, 0))
    return call(
        body, (n // tile,),
        [
            pl.BlockSpec((tile, width), lambda i, s: (i, 0)),
            pl.BlockSpec((1, cols), lambda i, s: (0, 0)),
        ] + [ANY] * 4,
        [out, out],
        [shape_of((n, cols), BF), shape_of((n, cols), F32)],
        [pltpu.VMEM(weight.shape, BF), pltpu.SemaphoreType.DMA],
        1, 2 * n * width * cols, 2 * n * width + 6 * n * cols, 18,
    )(info, rows, bias, *weight.arrays)


def halves_specs(tile, width, steps):
    return [
        pl.BlockSpec((tile, width), lambda i, s: (jnp.minimum(i, steps - 1), 0)),
        pl.BlockSpec((tile, width), lambda i, s: (jnp.maximum(i - steps, 0), 0)),
    ]


def feed_back(info, rows, weight, slope):
    n, width = rows[0].shape
    cols = weight.other
    tile = 512
    steps = n // tile

    def body(info_ref, g_ref, h_ref, s_ref, p0, p1, p2, p3, out_ref, sum_ref, w, sem):
        step = pl.program_id(0)

        @pl.when(step == 0)
        def _():
            fetch(info_ref, (p0, p1, p2, p3), w, sem, weight.block)
            sum_ref[...] = jnp.zeros_like(sum_ref)

        def write(ref):
            low = (dot_nn(ref[...], w[...]) * s_ref[...]).astype(BF)
            out_ref[...] = low
            sum_ref[...] += jnp.sum(low.astype(F32), axis=0, keepdims=True)

        @pl.when(step < steps)
        def _():
            write(g_ref)

        @pl.when(step >= steps)
        def _():
            write(h_ref)

    block = lambda width_of: pl.BlockSpec((tile, width_of), lambda i, s: (i, 0))
    return call(
        body, (2 * steps,), halves_specs(tile, width, steps) + [block(cols)] + [ANY] * 4,
        [block(cols), pl.BlockSpec((1, cols), lambda i, s: (0, 0))],
        [shape_of((2 * n, cols), BF), shape_of((1, cols), F32)],
        [pltpu.VMEM(weight.shape, BF), pltpu.SemaphoreType.DMA],
        1, 4 * n * width * cols, 4 * n * width + 12 * n * cols, 20,
    )(info, *rows, slope, *weight.arrays)


def weight_grad(info, groups):
    flat = [pair for group in groups for pair in group]
    width = flat[0][0].shape[1]
    tile = width // 4
    counts = [group[0][1].shape[1] for group in groups]
    cols = sum(counts)

    def body(info_ref, *refs):
        lefts, rights = refs[: len(flat)], refs[len(flat) : 2 * len(flat)]
        far_ref, near_ref = refs[2 * len(flat) :]

        def write(out_ref):
            at, start = 0, 0
            for group, count in zip(groups, counts):
                total = dot_tn(lefts[at][...], rights[at][...])
                for k in range(1, len(group)):
                    total += dot_tn(lefts[at + k][...], rights[at + k][...])
                out_ref[:, start : start + count] = total.astype(BF)
                at, start = at + len(group), start + count

        @pl.when(pl.program_id(0) < 2)
        def _():
            write(far_ref)

        @pl.when(pl.program_id(0) >= 2)
        def _():
            write(near_ref)

    return call(
        body, (4,),
        [pl.BlockSpec((left.shape[0], tile), lambda i, s: (0, s[5 + i])) for left, _, _ in flat]
        + [
            pl.BlockSpec((left.shape[0], right.shape[1]), lambda i, s, k=k: (k, 0))
            for left, right, k in flat
        ],
        [
            pl.BlockSpec((tile, cols), lambda i, s: (jnp.minimum(i, 1), 0)),
            pl.BlockSpec((tile, cols), lambda i, s: (jnp.maximum(i - 2, 0), 0)),
        ],
        [shape_of((width // 2, cols), BF)] * 2,
        [], 1, sum(2 * width * left.shape[0] * right.shape[1] for left, right, _ in flat),
        sum(2 * left.shape[0] * (width + right.shape[1]) for left, right, _ in flat), 24,
    )(info, *[pair[0] for pair in flat], *[pair[1] for pair in flat])


def turn(values, table, sign):
    lane = lax.broadcasted_iota(jnp.int32, values.shape, 1)
    half = ROT // 2
    partner = jnp.where(
        lane < half, -pltpu.roll(values, 128 - half, 1), pltpu.roll(values, half, 1)
    )
    cosine = jnp.where(lane < ROT, table, 1.0)
    sine = jnp.where(lane < ROT, pltpu.roll(table, ROT, 1), 0.0)
    return values * cosine + partner * (sign * sine)


def project_heads(info, rows, weight, bias, table):
    n, width = rows.shape
    cols = weight.other
    tile = 512

    def body(info_ref, x_ref, b_ref, t_ref, p0, p1, p2, p3, out_ref, w, sem):
        @pl.when(pl.program_id(0) == 0)
        def _():
            fetch(info_ref, (p0, p1, p2, p3), w, sem, weight.block)

        mixed = dot_nn(x_ref[...], w[...]) + b_ref[...]
        for start in range(0, cols, HD):
            head = mixed[:, start : start + 128]
            out_ref[:, start : start + 128] = turn(head, t_ref[...], 1.0).astype(BF)
            out_ref[:, start + 128 : start + HD] = mixed[:, start + 128 : start + HD].astype(BF)

    block = lambda width_of: pl.BlockSpec((tile, width_of), lambda i, s: (i, 0))
    return call(
        body, (n // tile,),
        [block(width), pl.BlockSpec((1, cols), lambda i, s: (0, 0)), block(128)] + [ANY] * 4,
        block(cols), shape_of((n, cols), BF),
        [pltpu.VMEM(weight.shape, BF), pltpu.SemaphoreType.DMA],
        1, 2 * n * width * cols, 2 * n * width + 4 * n * cols, 18,
    )(info, rows, bias, table, *weight.arrays)


def project_values(info, rows, grads, weight, bias):
    n, width = rows.shape
    cols = weight.other
    tile = 512
    steps = n // tile // 2

    def body(info_ref, x_ref, g_ref, h_ref, b_ref, p0, p1, p2, p3, v_ref, d_ref, w, sem):
        step = pl.program_id(0)

        @pl.when(step == 0)
        def _():
            fetch(info_ref, (p0, p1, p2, p3), w, sem, weight.block)

        v_ref[...] = (dot_nn(x_ref[...], w[:, :HD]) + b_ref[...]).astype(BF)

        @pl.when(step < steps)
        def _():
            d_ref[...] = dot_nn(g_ref[...], w[:, HD:]).astype(BF)

        @pl.when(step >= steps)
        def _():
            d_ref[...] = dot_nn(h_ref[...], w[:, HD:]).astype(BF)

    block = lambda width_of: pl.BlockSpec((tile, width_of), lambda i, s: (i, 0))
    return call(
        body, (2 * steps,),
        [block(width)] + halves_specs(tile, width, steps)
        + [pl.BlockSpec((1, HD), lambda i, s: (0, 0))] + [ANY] * 4,
        [block(HD), block(HD)], [shape_of((n, HD), BF)] * 2,
        [pltpu.VMEM(weight.shape, BF), pltpu.SemaphoreType.DMA],
        1, 2 * n * width * cols, 4 * n * width + 2 * n * cols, 24,
    )(info, rows, *grads, bias, *weight.arrays)


def attend(mixed, value, dcontext, table, row_info, col_info):
    n, cols = mixed.shape
    share = n // 16
    lead = (2, 2, 2, MICRO, share)

    def body(q_ref, v_ref, d_ref, t_ref, r_ref, k_ref, ctx_ref, dm_ref, dv_ref, sum_ref):
        @pl.when(pl.program_id(0) == 0)
        def _():
            sum_ref[...] = jnp.zeros_like(sum_ref)

        load = lambda ref: ref[...].reshape(ROWS, ref.shape[-1])
        mixed = load(q_ref)
        query, key, value = mixed[:, :HD], mixed[:, HD:], load(v_ref)
        dctx = load(d_ref)
        angles = load(t_ref)
        allowed = (r_ref[0, :, 0:1] == k_ref[0, 0:1, :]) & (k_ref[0, 1:2, :] <= r_ref[0, :, 1:2])
        scores = jnp.where(allowed, dot_nt(query, key) * SCALE, -1e30)
        expos = jnp.exp(scores - jnp.max(scores, axis=-1, keepdims=True))
        soft = expos / jnp.sum(expos, axis=-1, keepdims=True)
        probs = soft.astype(BF)
        ctx_ref[...] = dot_nn(probs, value).astype(BF).reshape(ctx_ref.shape)
        dprobs = dot_nt(dctx, value)
        dscores = soft * (dprobs - jnp.sum(soft * dprobs, axis=-1, keepdims=True))
        dscores = dscores.astype(BF)
        dvalue = dot_tn(probs, dctx)
        dquery = dot_nn(dscores, key) * SCALE
        dkey = dot_tn(dscores, query) * SCALE
        pieces = []
        for part in (dquery, dkey):
            pieces += [turn(part[:, :128], angles, -1.0), part[:, 128:]]
        low = jnp.concatenate(pieces, axis=1).astype(BF)
        low_value = dvalue.astype(BF)
        dm_ref[...] = low.reshape(dm_ref.shape)
        dv_ref[...] = low_value.reshape(dv_ref.shape)
        sum_ref[:, : 2 * HD] += jnp.sum(low.astype(F32), axis=0, keepdims=True)
        sum_ref[:, 2 * HD :] += jnp.sum(low_value.astype(F32), axis=0, keepdims=True)

    view = lambda a: a.reshape(lead + (a.shape[-1],))
    block = lambda w: pl.BlockSpec(
        (2, 1, 2, 1, share, w), lambda p: (0, p % 2, 0, p // 2, 0, 0)
    )
    info = lambda a: pl.BlockSpec((1,) + a.shape[1:], lambda p: (p, 0, 0))
    packs = MICRO * 2
    context, dmixed, dvalue, sums = call(
        body, (packs,),
        [block(cols), block(HD), block(HD), block(128), info(row_info), info(col_info)],
        [block(HD), block(cols), block(HD), pl.BlockSpec((1, 3 * HD), lambda p: (0, 0))],
        [
            shape_of(lead + (HD,), BF), shape_of(lead + (cols,), BF),
            shape_of(lead + (HD,), BF), shape_of((1, 3 * HD), F32),
        ],
        [], 0, packs * 7 * 2 * ROWS * ROWS * HD, n * cols * 6, 24,
    )(
        view(mixed), view(value), view(dcontext), view(table), row_info, col_info
    )
    return context.reshape(n, HD), dmixed.reshape(n, cols), dvalue.reshape(n, HD), sums


def row_kernel(info, half, parts, weights, extra_in, extra_specs, out_shapes, out_specs, finish, vmem):
    n = parts[0][0].shape[0] // 2
    width = weights[0].shape[0]
    tile = 256
    steps = n // tile
    n_extra, n_parts, n_weights = len(extra_in), len(parts), len(weights)

    def body(info_ref, *refs):
        extra, refs = refs[:n_extra], refs[n_extra:]
        a_refs, refs = refs[:n_parts], refs[n_parts:]
        w_refs, refs = refs[: 4 * n_weights], refs[4 * n_weights :]
        outs, refs = refs[: len(out_shapes)], refs[len(out_shapes) :]
        scratch, sem = refs[:-1], refs[-1]
        first = pl.program_id(0) == 0

        @pl.when(first)
        def _():
            for i, weight in enumerate(weights):
                fetch(info_ref, w_refs[4 * i : 4 * i + 4], scratch[i], sem, weight.block)

        def product(i):
            array, index, start = parts[i]
            return dot_nt(a_refs[i][...], scratch[index][:, start : start + array.shape[1]])

        finish(first, extra, product, outs)

    row = lambda w: pl.BlockSpec((tile, w), lambda i, s: (half * steps + i, 0))
    ks = sum(part[0].shape[1] for part in parts)
    return call(
        body, (steps,),
        [spec(row) for spec in extra_specs]
        + [row(part[0].shape[1]) for part in parts] + [ANY] * (4 * n_weights),
        [spec(tile) for spec in out_specs], out_shapes,
        [pltpu.VMEM(weight.shape, BF) for weight in weights] + [pltpu.SemaphoreType.DMA],
        1, 2 * n * width * ks, 2 * n * (2 * width + ks), vmem,
    )(
        info, *extra_in, *[part[0] for part in parts],
        *[array for weight in weights for array in weight.arrays],
    )


def out_rows(info, half, parts, weights):
    n, width = parts[0][0].shape[0] // 2, weights[0].shape[0]

    def finish(first, extra, product, outs):
        total = product(0)
        for i in range(1, len(parts)):
            total += product(i)
        outs[0][...] = total.astype(BF)

    return row_kernel(
        info, half, parts, weights, [], [], [shape_of((n, width), BF)],
        [lambda tile: pl.BlockSpec((tile, width), lambda i, s: (i, 0))], finish, 22,
    )[0]


def back_rows(info, half, parts, weights, n_attn, x, vectors):
    n, width = parts[0][0].shape[0] // 2, weights[0].shape[0]

    def finish(first, extra, product, outs):
        x_ref, v_ref = extra
        out_ref, sum_ref = outs

        @pl.when(first)
        def _():
            sum_ref[...] = jnp.zeros_like(sum_ref)

        plain, _ = plain_of(x_ref[...].astype(F32))
        dattn = product(0)
        for i in range(1, n_attn):
            dattn += product(i)
        dmlp = product(n_attn)
        for i in range(n_attn + 1, len(parts)):
            dmlp += product(i)
        out_ref[...] = (dattn * v_ref[0:1] + dmlp * v_ref[2:3]).astype(BF)
        for i, grad in enumerate((dattn, dmlp)):
            sum_ref[2 * i : 2 * i + 1] += jnp.sum(grad * plain, axis=0, keepdims=True)
            sum_ref[2 * i + 1 : 2 * i + 2] += jnp.sum(grad, axis=0, keepdims=True)

    return row_kernel(
        info, half, parts, weights, [x, vectors],
        [lambda row: pl.BlockSpec((256, width), lambda i, s: (i, 0)), lambda row: pl.BlockSpec(vectors.shape, lambda i, s: (0, 0))],
        [shape_of((n, width), BF), shape_of((4, width), F32)],
        [
            lambda tile: pl.BlockSpec((tile, width), lambda i, s: (i, 0)),
            lambda tile: pl.BlockSpec((4, width), lambda i, s: (0, 0)),
        ],
        finish, 34,
    )


def layer_program(n_dp, n_tensor):
    n_z = n_dp // 2
    n_dev = n_dp * n_tensor
    core, xbit, ybit, zbit = 1, 2, 4, 8
    ids = range(n_dev)
    flip = lambda bit: [(i, i ^ bit) for i in ids]
    flip_c, flip_x, flip_y, flip_z = flip(core), flip(xbit), flip(ybit), flip(zbit)
    mirror = {0: 0, 1: 2, 2: 1, 3: 3}
    mid = [
        (i, mirror[i // zbit] * zbit + (i % zbit if i // zbit in (1, 2) else i % zbit ^ core))
        for i in ids if n_z == 4
    ]
    columns = [[z * 2 + y for z in range(n_z)] for y in range(2)]

    def per_device(
        tokens, lengths, out_grad, attn_gain, attn_shift, mlp_gain, mlp_shift,
        w_qkv, b_qkv, w_proj, b_proj, w_in, b_in, w_out, b_out,
    ):
        dp = lax.axis_index("dp")
        tensor = lax.axis_index("tensor")
        z, y = dp // 2, dp % 2
        x, c = tensor // 2, tensor % 2
        share = tokens.shape[1]
        width = tokens.shape[2]
        upper = z >= 2
        even = z % 2 == 0
        token = []
        is_mid = (z == 1) | (z == 2)

        def turn_of(*values):
            out = lax.optimization_barrier(values + tuple(token))[: len(values)] if token else values
            return out if len(out) > 1 else out[0]

        def passed(*values):
            values = tuple(value for value in values if value is not None)
            token[:] = lax.optimization_barrier(values + tuple(token))[:1]

        def send(values, perm, payload=lambda value: value):
            values = turn_of(*values)
            return swap(payload(*values) if isinstance(values, tuple) else payload(values), perm)

        if n_z == 4:
            far = jnp.where(upper, 1, 2)
            low_far = jnp.where(upper, 0, 2)
            info = jnp.stack(
                [z, z ^ 1, far, far ^ 1, is_mid, low_far, low_far + 1, z ^ 1, z]
            ).astype(jnp.int32)
        else:
            info = jnp.array([0, 1, 2, 3, 1, 0, 1, 2, 3], jnp.int32)

        class Chunk:
            partner = from_mid = far = None

            def __init__(self, *cuts):
                def side_of(side):
                    parts = [
                        lax.dynamic_slice_in_dim(weight, side * sub + start, count, 1)
                        for weight, sub, start, count in cuts
                    ]
                    return parts[0] if len(parts) == 1 else jnp.concatenate(parts, axis=1)

                self.mine, self.theirs = side_of(y), side_of(1 - y)

            def step_a(self):
                if n_z == 4:
                    self.partner = send([self.pair], flip_z)

            def step_b(self):
                if n_z == 4:
                    self.from_mid = send(
                        [self.pair, self.partner], mid, lambda *both: jnp.concatenate(both)
                    )

            def arrived(self, far):
                if n_z == 4:
                    self.far = far
                    arrays = (self.pair, self.partner, self.from_mid, far)
                else:
                    whole = lax.all_gather(self.pair, "dp", axis_index_groups=columns, tiled=True)
                    quarter = jnp.split(whole, 4)
                    half = jnp.concatenate(quarter[2:])
                    arrays = (quarter[0], quarter[1], half, half)
                self.full = Gathered(arrays)

        def step_y(*chunks):
            got = send(
                [chunk.theirs for chunk in chunks], flip_y,
                lambda *parts: jnp.concatenate(parts, axis=1),
            )
            start = 0
            for chunk in chunks:
                count = chunk.mine.shape[1]
                chunk.pair = ordered(y == 0, chunk.mine, got[:, start : start + count])
                start += count

        class Scatter:
            got = None

            def __init__(self, parts):
                self.far, self.near = parts

            def step_b(self):
                if n_z == 4:
                    self.got = send(
                        [self.far, self.got], mid,
                        lambda far, got: (far.astype(F32) + got.astype(F32)).astype(BF),
                    )

            def step_a(self):
                if n_z == 4:
                    near, got = turn_of(self.near, self.got)
                    got = jnp.where(is_mid, got, jnp.zeros_like(got)).astype(F32)
                    low, high = jnp.split(got, 2)
                    partner, own = jnp.split(near.astype(F32), 2)
                    self.own = own + jnp.where(even, low, high)
                    self.got = swap((partner + jnp.where(even, high, low)).astype(BF), flip_z)

            def finish(self):
                if n_z == 4:
                    own, got = turn_of(self.own, self.got)
                    return own + got.astype(F32)
                return lax.psum_scatter(
                    jnp.concatenate([self.far, self.near]), "dp", scatter_dimension=0,
                    axis_index_groups=columns, tiled=True,
                ).astype(F32)

        def finish(*scatters):
            whole = jnp.concatenate([scatter.finish() for scatter in scatters], axis=1)
            low, high = jnp.split(whole, 2)
            own = jnp.where(y == 0, low, high)
            got = swap(jnp.where(y == 0, high, low).astype(BF), flip_y)
            start = 0
            for scatter in scatters:
                count = scatter.near.shape[1]
                scatter.mine = own[:, start : start + count]
                scatter.theirs = got[:, start : start + count].astype(F32)
                start += count
            return got

        def cross(chunk=None, scatter=None):
            got = None
            if n_z == 4:
                if scatter is None:
                    got = send([chunk.from_mid], flip_z)
                elif chunk is None:
                    got = send([scatter.far], flip_z)
                else:
                    got = send(
                        [chunk.from_mid, scatter.far], flip_z,
                        lambda *parts: jnp.where(is_mid, *parts),
                    )
            if chunk is not None:
                chunk.arrived(got)
            if scatter is not None:
                scatter.got = got

        h_cols = w_in.shape[1] // 2
        half_h = h_cols // 2
        q_cols = w_qkv.shape[1] // 2
        p_cols = w_proj.shape[0] // 2

        w_out_t, w_proj_t = w_out.T, w_proj.T
        c_in0 = Chunk((w_in, h_cols, 0, half_h))
        c_out0 = Chunk((w_out_t, h_cols, 0, half_h))
        c_qk = Chunk((w_qkv, q_cols, 0, 2 * HD))
        c_vp = Chunk((w_qkv, q_cols, 2 * HD, HD), (w_proj_t, p_cols, 0, p_cols))
        c_in1 = Chunk((w_in, h_cols, half_h, half_h))
        c_out1 = Chunk((w_out_t, h_cols, half_h, half_h))

        class Plane:
            def __init__(self, own):
                self.own = own.reshape(MICRO, share, width)

            def step_x(self):
                self.from_x = send([self.own], flip_x)

            def step_y(self):
                self.from_y = send([self.own], flip_y)

            def step_diagonal(self):
                self.diagonal = (
                    send([self.from_x], flip_y, lambda value: value[0]),
                    send([self.from_y], flip_x, lambda value: value[1]),
                )

            def step_core(self):
                parts = turn_of(self.own, self.from_x, self.from_y, *self.diagonal)
                diagonal = jnp.stack(parts[3:])
                self.mine = jnp.stack(list(parts[:3]) + [diagonal]).reshape(-1, width)
                self.sibling = swap(self.mine, flip_c)

        class PlaneSum:
            def step_core(self, give):
                self.got = send([give], flip_c)

            def step_first(self, keep):
                keep, got = turn_of(keep, self.got)
                total = (keep.astype(F32) + got.astype(F32)).astype(BF)
                self.total = total.reshape(2, 2, MICRO, share, width)
                self.got = swap(self.total[1, :, 0], flip_y), swap(self.total[:, 1, 1], flip_x)

            def step_second(self):
                got = turn_of(*self.got)
                by_y = self.total[0, :, 0].astype(F32) + got[0].astype(F32)
                by_x = self.total[:, 0, 1].astype(F32) + got[1].astype(F32)
                self.kept = by_y[0], by_x[0]
                self.got = swap(by_y[1].astype(BF), flip_x), swap(by_x[1].astype(BF), flip_y)

            def result(self):
                got = turn_of(*self.got)
                return jnp.stack(
                    [kept + part.astype(F32) for kept, part in zip(self.kept, got)]
                )

        own_places = tensor * share + jnp.arange(share, dtype=jnp.int32)
        own_ends = jnp.cumsum(lengths[:, 0], axis=-1)
        own_segment = jnp.sum((own_places[:, None] >= own_ends[:, None, :]).astype(jnp.int32), axis=-1)
        valid = (own_segment < SEGS - 1).astype(F32)[..., None]
        x_own = tokens.astype(F32)
        g_own = out_grad.astype(F32) * valid
        x_plane, g_plane = Plane(tokens), Plane(g_own.astype(BF))

        vectors = jnp.stack([attn_gain, attn_shift, mlp_gain, mlp_shift, b_proj, b_out])
        step_y(c_in0, c_out0)
        vectors_y = swap(vectors, flip_y)
        lengths_y = swap(lengths[:, 0], flip_y)
        x_plane.step_x()
        pair = ordered(y == 0, vectors[None], vectors_y[None])
        lengths_all = jnp.stack([lengths[:, 0], lengths_y])
        passed(c_in0.pair, pair, lengths_all)
        c_in0.step_a()
        x_plane.step_y()
        if n_z == 4:
            quad = ordered(even, pair, send([pair], flip_z))
            passed(quad, c_in0.partner)
            c_in0.step_b()
            c_out0.step_a()
            small = ordered(~upper, quad, send([quad], flip(2 * zbit)))
        else:
            small = lax.all_gather(pair, "dp", axis_index_groups=columns, tiled=True)
        small = small.transpose(1, 0, 2).reshape(6, width).astype(F32)
        small = jnp.concatenate([small, jnp.zeros((2, width), F32)])
        passed(x_plane.from_x, x_plane.from_y, small, c_out0.partner)
        x_plane.step_diagonal()
        passed(*x_plane.diagonal, c_in0.from_mid)
        x_plane.step_core()
        cross(c_in0)
        c_out0.step_b()
        g_plane.step_x()
        g_plane.step_y()
        passed(x_plane.sibling)
        step_y(c_qk, c_vp)
        attn_rows, mlp_rows = norm_rows(turn_of(x_plane.mine), x_plane.sibling, small)
        passed(attn_rows, c_in0.far, c_out0.from_mid, g_plane.from_x, g_plane.from_y)
        g_plane.step_diagonal()
        cross(c_out0)

        pair_bits = jnp.arange(2, dtype=jnp.int32)
        t_of = (x ^ pair_bits)[None, :] * 2 + (c ^ pair_bits)[:, None]
        places = (t_of[..., None] * share + jnp.arange(share, dtype=jnp.int32)).reshape(-1)
        lengths_all = turn_of(lengths_all)
        ends = jnp.cumsum(lengths_all, axis=-1)
        gone = (places[:, None] >= ends[..., None, :]).astype(jnp.int32)
        segment = jnp.sum(gone, axis=-1)
        position = places - jnp.sum(gone * lengths_all[..., None, :], axis=-1)
        row_position = position.reshape(2, MICRO, 2, 2, share).transpose(2, 0, 3, 1, 4).reshape(-1)
        lanes = jnp.arange(2 * ROT)
        frequency = 10000.0 ** (-2.0 * (lanes % (ROT // 2)).astype(F32) / ROT)
        angle = row_position.astype(F32)[:, None] * frequency
        table = lax.optimization_barrier(jnp.where(lanes < ROT, jnp.cos(angle), jnp.sin(angle)))
        pack_segment = segment.transpose(1, 0, 2).reshape(MICRO * 2, ROWS)
        pack_places = jnp.broadcast_to(places, (MICRO * 2, ROWS))
        row_info = jnp.stack([pack_segment, pack_places], axis=2)
        col_info = jnp.stack([pack_segment, pack_places], axis=1)
        bias_in = lax.dynamic_slice_in_dim(b_in, y * h_cols, h_cols).astype(F32)[None]
        bias_qkv = lax.dynamic_slice_in_dim(b_qkv, y * q_cols, q_cols).astype(F32)[None]

        active_0, slope_0 = feed(info, turn_of(mlp_rows), c_in0.full, bias_in[:, :half_h])
        g_rows = lambda: (turn_of(g_plane.mine), g_plane.sibling)
        passed(active_0, c_qk.pair, *g_plane.diagonal)
        g_plane.step_core()
        c_qk.step_a()
        c_vp.step_a()
        passed(table, row_info, col_info, g_plane.sibling, c_out0.far)
        step_y(c_in1, c_out1)
        give = g_rows()
        s_out0 = Scatter(
            weight_grad(info, [[(give[0], active_0, 0), (give[1], active_0, 1)]])
        )
        passed(s_out0.far, c_qk.partner)
        c_qk.step_b()
        dhidden_0, dsum_0 = feed_back(info, g_rows(), c_out0.full, slope_0)
        passed(dhidden_0, c_vp.partner)
        c_vp.step_b()
        s_in0 = Scatter(weight_grad(info, [[(turn_of(mlp_rows), dhidden_0, 0)]]))
        passed(s_in0.far, c_qk.from_mid)
        cross(c_qk, s_out0)
        c_in1.step_a()
        passed(c_qk.far)
        s_out0.step_b()
        mixed = project_heads(
            info, turn_of(attn_rows), c_qk.full, bias_qkv[:, : 2 * HD], table
        )
        passed(mixed, c_vp.from_mid, c_in1.partner)
        cross(c_vp, s_in0)
        c_in1.step_b()
        c_out1.step_a()
        passed(c_vp.far, s_out0.got)
        s_out0.step_a()
        s_in0.step_b()
        value, dcontext = project_values(
            info, turn_of(attn_rows), g_rows(), c_vp.full, bias_qkv[:, 2 * HD :]
        )
        passed(value, c_in1.from_mid, c_out1.partner)
        c_out1.step_b()
        context, dmixed, dvalue, dmixed_sum = attend(
            turn_of(mixed), value, dcontext, table, row_info, col_info
        )
        passed(dmixed)
        s_qk = Scatter(weight_grad(info, [[(turn_of(attn_rows), dmixed, 0)]]))
        passed(s_qk.far, s_in0.got, s_out0.got)
        cross(c_in1, s_qk)
        s_in0.step_a()
        give = g_rows()
        s_vp = Scatter(
            weight_grad(
                info,
                [
                    [(turn_of(attn_rows), dvalue, 0)],
                    [(give[0], context, 0), (give[1], context, 1)],
                ],
            )
        )
        passed(s_vp.far, c_in1.far, c_out1.from_mid)
        cross(c_out1, s_vp)
        s_qk.step_b()
        active_1, slope_1 = feed(info, turn_of(mlp_rows), c_in1.full, bias_in[:, half_h:])
        passed(active_1, s_in0.got)
        finished = finish(s_out0, s_in0)
        give = g_rows()
        s_out1 = Scatter(
            weight_grad(info, [[(give[0], active_1, 0), (give[1], active_1, 1)]])
        )
        passed(s_out1.far, c_out1.far, s_qk.got)
        cross(None, s_out1)
        s_qk.step_a()
        s_vp.step_b()
        dhidden_1, dsum_1 = feed_back(info, g_rows(), c_out1.full, slope_1)
        passed(dhidden_1)
        s_in1 = Scatter(weight_grad(info, [[(turn_of(mlp_rows), dhidden_1, 0)]]))
        passed(s_in1.far, s_out1.got, finished)
        cross(None, s_in1)
        s_out1.step_b()

        branch, back = PlaneSum(), PlaneSum()
        weights = (c_vp.full, c_out0.full, c_out1.full)
        rest = [(active_0, 1, 0), (active_1, 2, 0)]
        out_give = out_rows(info, 1, [(turn_of(context), 0, HD)] + rest, weights)
        passed(out_give, s_vp.got, s_qk.got)
        branch.step_core(out_give)
        s_vp.step_a()
        out_keep = out_rows(info, 0, [(turn_of(context), 0, HD)] + rest, weights)
        passed(out_keep, branch.got, s_in1.got)
        s_in1.step_b()
        branch.step_first(out_keep)
        weights = (c_qk.full, c_vp.full, c_in0.full, c_in1.full)
        rest = [(dvalue, 1, 0), (dhidden_0, 2, 0), (dhidden_1, 3, 0)]
        back_give, sums_give = back_rows(
            info, 1, [(turn_of(dmixed), 0, 0)] + rest, weights, 2, x_plane.sibling, small
        )
        passed(back_give, s_out1.got, s_vp.got)
        back.step_core(back_give)
        s_out1.step_a()
        finished = finish(s_qk, s_vp)
        back_keep, sums_keep = back_rows(
            info, 0, [(turn_of(dmixed), 0, 0)] + rest, weights, 2, x_plane.mine, small
        )
        passed(back_keep, back.got, finished, *branch.got)
        back.step_first(back_keep)
        branch.step_second()
        passed(s_in1.got, s_out1.got)
        s_in1.step_a()

        g_sum = jnp.sum(g_own, axis=(0, 1))[None]
        sums = jnp.concatenate([sums_keep + sums_give, g_sum])
        sums = sums.reshape(5, n_dev, -1).transpose(1, 0, 2).reshape(n_dev, -1)
        dhidden_sum = jnp.concatenate([dsum_0, dsum_1], axis=1)
        bias_sums = jnp.concatenate(
            [dhidden_sum.reshape(n_dp // 2, -1), dmixed_sum.reshape(n_dp // 2, -1)], axis=-1
        )
        spread_bias = jnp.zeros((n_dp, n_tensor, bias_sums.shape[-1]), F32)
        spread_bias = lax.dynamic_update_slice(
            spread_bias, bias_sums[:, None], (y * (n_dp // 2), tensor, 0)
        ).reshape(n_dev, -1)
        total = jnp.concatenate([sums, spread_bias], axis=-1).reshape(n_z, 2, 2, 2, -1)
        for axis, bit, perm in ((3, c, flip_c), (2, x, flip_x), (1, y, flip_y)):
            low, high = jnp.split(turn_of(total), 2, axis=axis)
            got = swap(jnp.where(bit == 0, high, low), perm)
            if perm is flip_c:
                passed(got)
            total = jnp.where(bit == 0, low, high) + got
        total = total.reshape(n_z, -1)
        if n_z == 4:
            row = lambda k: lax.dynamic_slice_in_dim(total, z ^ k, 1, 0)
            vector_sums = row(0)
            for k in (1, 2, 3):
                vector_sums += swap(row(k), flip(zbit * k))
            vector_sums = vector_sums.reshape(-1)
        else:
            vector_sums = lax.psum_scatter(
                total.reshape(-1), "dp", axis_index_groups=columns, tiled=True
            )

        passed(*back.got, s_in1.got)
        back.step_second()
        finished = finish(s_out1, s_in1)
        passed(*branch.got)
        output = (x_own + branch.result() + small[4] + small[5]).astype(BF)
        passed(output, vector_sums)
        back = back.result()

        own_plain, own_spread = plain_of(x_own)
        grad_tokens = g_own + own_spread * (
            back
            - jnp.mean(back, axis=-1, keepdims=True)
            - own_plain * jnp.mean(back * own_plain, axis=-1, keepdims=True)
        )

        piece = width // n_dev
        pieces = [vector_sums[k * piece : (k + 1) * piece] for k in range(5)]
        bias_piece = vector_sums[5 * piece :]
        in_piece = b_in.shape[0] // n_dp

        def columns_of(axis, *parts):
            mine = jnp.concatenate([part[0] for part in parts], axis=axis)
            theirs = jnp.concatenate([part[1] for part in parts], axis=axis)
            return ordered(y == 0, mine, theirs, axis)

        both = lambda part: (part.mine, part.theirs)
        heads = [value[:, :HD] for value in both(s_vp)]
        proj = [value[:, HD:] for value in both(s_vp)]

        return (
            output,
            grad_tokens,
            pieces[0],
            pieces[1],
            pieces[2],
            pieces[3],
            columns_of(1, both(s_qk), heads),
            bias_piece[in_piece:].reshape(1, -1),
            columns_of(1, proj).T,
            pieces[4],
            columns_of(1, both(s_in0), both(s_in1)),
            bias_piece[:in_piece].reshape(1, -1),
            columns_of(1, both(s_out0), both(s_out1)).T,
            pieces[4],
        )

    return per_device


def solution(mesh):
    n_dp, n_tensor = mesh.shape["dp"], mesh.shape["tensor"]
    rows = P(None, AXES, None)
    in_specs = (
        rows, P(None, "dp", None), rows, P("dp"), P("dp"), P("dp"), P("dp"),
        P("dp", "tensor"), P("tensor"), P("tensor", "dp"), P("dp"),
        P("dp", "tensor"), P("tensor"), P("tensor", "dp"), P("dp"),
    )
    vector = P(AXES)
    out_specs = (
        rows, rows, vector, vector, vector, vector,
        P("dp", "tensor"), P("tensor", "dp"), P("tensor", "dp"), vector,
        P("dp", "tensor"), P("tensor", "dp"), P("tensor", "dp"), vector,
    )
    return jax.shard_map(
        layer_program(n_dp, n_tensor), mesh=mesh,
        in_specs=in_specs, out_specs=out_specs, check_vma=False,
    )
```

```python
import jax
import jax.numpy as jnp
from jax import lax
from jax.experimental import pallas as pl
from jax.experimental.pallas import tpu as pltpu
from jax.sharding import PartitionSpec as P

HD = 256
ROT = 64
MICRO = 2
ROWS = 512
SEGS = 8
AXES = ("dp", "tensor")
BF = jnp.bfloat16
F32 = jnp.float32
MIB = 1 << 20
SCALE = HD ** (-0.5)
ANY = pl.BlockSpec(memory_space=pl.ANY)


def swap(value, perm):
    return lax.ppermute(value, AXES, perm)


def dot_nn(a, b):
    return jnp.dot(a, b, preferred_element_type=F32)


def dot_nt(a, b):
    return lax.dot_general(a, b, (((1,), (1,)), ((), ())), preferred_element_type=F32)


def dot_tn(a, b):
    return lax.dot_general(a, b, (((0,), (0,)), ((), ())), preferred_element_type=F32)


def ordered(first, low, high, axis=0):
    return jnp.where(
        first,
        jnp.concatenate([low, high], axis=axis),
        jnp.concatenate([high, low], axis=axis),
    )


def shape_of(shape, dtype):
    return jax.ShapeDtypeStruct(shape, dtype)


def call(body, grid, in_specs, out_specs, out_shape, scratch, prefetch, flops, nbytes, vmem):
    return pl.pallas_call(
        body,
        out_shape=out_shape,
        grid_spec=pltpu.PrefetchScalarGridSpec(
            num_scalar_prefetch=prefetch,
            grid=grid,
            in_specs=in_specs,
            out_specs=out_specs,
            scratch_shapes=scratch,
        ),
        compiler_params=pltpu.CompilerParams(
            dimension_semantics=("arbitrary",) * len(grid), vmem_limit_bytes=vmem * MIB
        ),
        cost_estimate=pl.CostEstimate(
            flops=int(flops) * 7 // 10, bytes_accessed=0, transcendentals=0
        ),
    )


class Gathered:
    def __init__(self, arrays):
        self.arrays = arrays
        self.block, self.other = arrays[0].shape
        self.shape = (4 * self.block, self.other)


def fetch(info, refs, scratch, sem, block):
    def part(ref, index, place):
        source = ref.at[pl.ds(index * block, block), :]
        target = scratch.at[pl.ds(pl.multiple_of(place * block, block), block), :]
        return pltpu.make_async_copy(source, target, sem)

    own, partner, far_mid, far_out = refs
    part(own, 0, info[0]).start()
    part(partner, 0, info[1]).start()

    @pl.when(info[4] == 1)
    def _():
        part(far_mid, 0, info[2]).start()
        part(far_mid, 1, info[3]).start()

    @pl.when(info[4] == 0)
    def _():
        part(far_out, 0, info[2]).start()
        part(far_out, 1, info[3]).start()

    part(own, 0, info[0]).wait()
    part(partner, 0, info[1]).wait()
    part(far_out, 0, info[2]).wait()
    part(far_out, 1, info[3]).wait()


def plain_of(rows):
    center = rows - jnp.mean(rows, axis=-1, keepdims=True)
    spread = lax.rsqrt(jnp.mean(center * center, axis=-1, keepdims=True) + 1e-05)
    return center * spread, spread


def norm_rows(mine, sibling, vectors):
    n, width = mine.shape
    tile = 256
    steps = n // tile

    def body(x_ref, y_ref, v_ref, a_ref, m_ref):
        def write(rows):
            plain, _ = plain_of(rows.astype(F32))
            a_ref[...] = (plain * v_ref[0:1] + v_ref[1:2]).astype(BF)
            m_ref[...] = (plain * v_ref[2:3] + v_ref[3:4]).astype(BF)

        @pl.when(pl.program_id(0) < steps)
        def _():
            write(x_ref[...])

        @pl.when(pl.program_id(0) >= steps)
        def _():
            write(y_ref[...])

    rows = pl.BlockSpec((tile, width), lambda i: (i, 0))
    return call(
        body, (2 * steps,),
        [
            pl.BlockSpec((tile, width), lambda i: (jnp.minimum(i, steps - 1), 0)),
            pl.BlockSpec((tile, width), lambda i: (jnp.maximum(i - steps, 0), 0)),
            pl.BlockSpec(vectors.shape, lambda i: (0, 0)),
        ],
        [rows, rows],
        [shape_of((2 * n, width), BF)] * 2, [], 0, 2 * n * width * 600, 2 * n * width * 6, 16,
    )(mine, sibling, vectors)


def stack_rows(parts):
    rows, width = parts[0].shape
    half = len(parts) // 2

    def body(*refs):
        ins, outs, sem = refs[: 2 * half], refs[2 * half : -1], refs[-1]
        copies = [
            pltpu.make_async_copy(
                ins[k], outs[k // half].at[pl.ds((k % half) * rows, rows), :], sem.at[k]
            )
            for k in range(2 * half)
        ]
        for copy in copies:
            copy.start()
        for copy in copies:
            copy.wait()

    return call(
        body, (1,), [ANY] * (2 * half), [ANY] * 2, [shape_of((half * rows, width), BF)] * 2,
        [pltpu.SemaphoreType.DMA((2 * half,))], 0, 1000, 1000, 4,
    )(*parts)


def feed(info, rows, weight, bias):
    n, width = rows.shape
    cols = weight.other
    tile = 512

    def body(info_ref, x_ref, b_ref, p0, p1, p2, p3, active_ref, slope_ref, w, sem):
        @pl.when(pl.program_id(0) == 0)
        def _():
            fetch(info_ref, (p0, p1, p2, p3), w, sem, weight.block)

        hidden = dot_nn(x_ref[...], w[...]) + b_ref[...]
        cdf = 0.5 * (1.0 + lax.erf(hidden * 0.7071067811865476))
        active_ref[...] = (hidden * cdf).astype(BF)
        slope_ref[...] = cdf + hidden * jnp.exp(-0.5 * hidden * hidden) * 0.3989422804014327

    out = pl.BlockSpec((tile, cols), lambda i, s: (i, 0))
    return call(
        body, (n // tile,),
        [
            pl.BlockSpec((tile, width), lambda i, s: (i, 0)),
            pl.BlockSpec((1, cols), lambda i, s: (0, 0)),
        ] + [ANY] * 4,
        [out, out],
        [shape_of((n, cols), BF), shape_of((n, cols), F32)],
        [pltpu.VMEM(weight.shape, BF), pltpu.SemaphoreType.DMA],
        1, 2 * n * width * cols, 2 * n * width + 6 * n * cols, 18,
    )(info, rows, bias, *weight.arrays)


def halves_specs(tile, width, steps):
    return [
        pl.BlockSpec((tile, width), lambda i, s: (jnp.minimum(i, steps - 1), 0)),
        pl.BlockSpec((tile, width), lambda i, s: (jnp.maximum(i - steps, 0), 0)),
    ]


def feed_back(info, rows, weight, slope):
    n, width = rows[0].shape
    cols = weight.other
    tile = 512
    steps = n // tile

    def body(info_ref, g_ref, h_ref, s_ref, p0, p1, p2, p3, out_ref, sum_ref, w, sem):
        step = pl.program_id(0)

        @pl.when(step == 0)
        def _():
            fetch(info_ref, (p0, p1, p2, p3), w, sem, weight.block)
            sum_ref[...] = jnp.zeros_like(sum_ref)

        def write(ref):
            low = (dot_nn(ref[...], w[...]) * s_ref[...]).astype(BF)
            out_ref[...] = low
            sum_ref[...] += jnp.sum(low.astype(F32), axis=0, keepdims=True)

        @pl.when(step < steps)
        def _():
            write(g_ref)

        @pl.when(step >= steps)
        def _():
            write(h_ref)

    block = lambda width_of: pl.BlockSpec((tile, width_of), lambda i, s: (i, 0))
    return call(
        body, (2 * steps,), halves_specs(tile, width, steps) + [block(cols)] + [ANY] * 4,
        [block(cols), pl.BlockSpec((1, cols), lambda i, s: (0, 0))],
        [shape_of((2 * n, cols), BF), shape_of((1, cols), F32)],
        [pltpu.VMEM(weight.shape, BF), pltpu.SemaphoreType.DMA],
        1, 4 * n * width * cols, 4 * n * width + 12 * n * cols, 20,
    )(info, *rows, slope, *weight.arrays)


def weight_grad(info, groups):
    flat = [pair for group in groups for pair in group]
    width = flat[0][0].shape[1]
    tile = width // 4
    counts = [group[0][1].shape[1] for group in groups]
    cols = sum(counts)

    def body(info_ref, *refs):
        lefts, rights = refs[: len(flat)], refs[len(flat) : 2 * len(flat)]
        far_ref, near_ref = refs[2 * len(flat) :]

        def write(out_ref):
            at, start = 0, 0
            for group, count in zip(groups, counts):
                total = dot_tn(lefts[at][...], rights[at][...])
                for k in range(1, len(group)):
                    total += dot_tn(lefts[at + k][...], rights[at + k][...])
                out_ref[:, start : start + count] = total.astype(BF)
                at, start = at + len(group), start + count

        @pl.when(pl.program_id(0) < 2)
        def _():
            write(far_ref)

        @pl.when(pl.program_id(0) >= 2)
        def _():
            write(near_ref)

    return call(
        body, (4,),
        [pl.BlockSpec((left.shape[0], tile), lambda i, s: (0, s[5 + i])) for left, _, _ in flat]
        + [
            pl.BlockSpec((left.shape[0], right.shape[1]), lambda i, s, k=k: (k, 0))
            for left, right, k in flat
        ],
        [
            pl.BlockSpec((tile, cols), lambda i, s: (jnp.minimum(i, 1), 0)),
            pl.BlockSpec((tile, cols), lambda i, s: (jnp.maximum(i - 2, 0), 0)),
        ],
        [shape_of((width // 2, cols), BF)] * 2,
        [], 1, sum(2 * width * left.shape[0] * right.shape[1] for left, right, _ in flat),
        sum(2 * left.shape[0] * (width + right.shape[1]) for left, right, _ in flat), 24,
    )(info, *[pair[0] for pair in flat], *[pair[1] for pair in flat])


def turn(values, table, sign):
    lane = lax.broadcasted_iota(jnp.int32, values.shape, 1)
    half = ROT // 2
    partner = jnp.where(
        lane < half, -pltpu.roll(values, 128 - half, 1), pltpu.roll(values, half, 1)
    )
    cosine = jnp.where(lane < ROT, table, 1.0)
    sine = jnp.where(lane < ROT, pltpu.roll(table, ROT, 1), 0.0)
    return values * cosine + partner * (sign * sine)


def project_heads(info, rows, weight, bias, table):
    n, width = rows.shape
    cols = weight.other
    tile = 512

    def body(info_ref, x_ref, b_ref, t_ref, p0, p1, p2, p3, out_ref, w, sem):
        @pl.when(pl.program_id(0) == 0)
        def _():
            fetch(info_ref, (p0, p1, p2, p3), w, sem, weight.block)

        mixed = dot_nn(x_ref[...], w[...]) + b_ref[...]
        for start in range(0, cols, HD):
            head = mixed[:, start : start + 128]
            out_ref[:, start : start + 128] = turn(head, t_ref[...], 1.0).astype(BF)
            out_ref[:, start + 128 : start + HD] = mixed[:, start + 128 : start + HD].astype(BF)

    block = lambda width_of: pl.BlockSpec((tile, width_of), lambda i, s: (i, 0))
    return call(
        body, (n // tile,),
        [block(width), pl.BlockSpec((1, cols), lambda i, s: (0, 0)), block(128)] + [ANY] * 4,
        block(cols), shape_of((n, cols), BF),
        [pltpu.VMEM(weight.shape, BF), pltpu.SemaphoreType.DMA],
        1, 2 * n * width * cols, 2 * n * width + 4 * n * cols, 18,
    )(info, rows, bias, table, *weight.arrays)


def project_values(info, rows, grads, weight, bias):
    n, width = rows.shape
    cols = weight.other
    tile = 512
    steps = n // tile // 2

    def body(info_ref, x_ref, g_ref, h_ref, b_ref, p0, p1, p2, p3, v_ref, d_ref, w, sem):
        step = pl.program_id(0)

        @pl.when(step == 0)
        def _():
            fetch(info_ref, (p0, p1, p2, p3), w, sem, weight.block)

        v_ref[...] = (dot_nn(x_ref[...], w[:, :HD]) + b_ref[...]).astype(BF)

        @pl.when(step < steps)
        def _():
            d_ref[...] = dot_nn(g_ref[...], w[:, HD:]).astype(BF)

        @pl.when(step >= steps)
        def _():
            d_ref[...] = dot_nn(h_ref[...], w[:, HD:]).astype(BF)

    block = lambda width_of: pl.BlockSpec((tile, width_of), lambda i, s: (i, 0))
    return call(
        body, (2 * steps,),
        [block(width)] + halves_specs(tile, width, steps)
        + [pl.BlockSpec((1, HD), lambda i, s: (0, 0))] + [ANY] * 4,
        [block(HD), block(HD)], [shape_of((n, HD), BF)] * 2,
        [pltpu.VMEM(weight.shape, BF), pltpu.SemaphoreType.DMA],
        1, 2 * n * width * cols, 4 * n * width + 2 * n * cols, 24,
    )(info, rows, *grads, bias, *weight.arrays)


def attend(mixed, value, dcontext, table, row_info, col_info):
    n, cols = mixed.shape
    share = n // 16
    lead = (2, 2, 2, MICRO, share)

    def body(q_ref, v_ref, d_ref, t_ref, r_ref, k_ref, ctx_ref, dm_ref, dv_ref, sum_ref):
        @pl.when(pl.program_id(0) == 0)
        def _():
            sum_ref[...] = jnp.zeros_like(sum_ref)

        load = lambda ref: ref[...].reshape(ROWS, ref.shape[-1])
        mixed = load(q_ref)
        query, key, value = mixed[:, :HD], mixed[:, HD:], load(v_ref)
        dctx = load(d_ref)
        angles = load(t_ref)
        allowed = (r_ref[0, :, 0:1] == k_ref[0, 0:1, :]) & (k_ref[0, 1:2, :] <= r_ref[0, :, 1:2])
        scores = jnp.where(allowed, dot_nt(query, key) * SCALE, -1e30)
        expos = jnp.exp(scores - jnp.max(scores, axis=-1, keepdims=True))
        soft = expos / jnp.sum(expos, axis=-1, keepdims=True)
        probs = soft.astype(BF)
        ctx_ref[...] = dot_nn(probs, value).astype(BF).reshape(ctx_ref.shape)
        dprobs = dot_nt(dctx, value)
        dscores = soft * (dprobs - jnp.sum(soft * dprobs, axis=-1, keepdims=True))
        dscores = dscores.astype(BF)
        dvalue = dot_tn(probs, dctx)
        dquery = dot_nn(dscores, key) * SCALE
        dkey = dot_tn(dscores, query) * SCALE
        pieces = []
        for part in (dquery, dkey):
            pieces += [turn(part[:, :128], angles, -1.0), part[:, 128:]]
        low = jnp.concatenate(pieces, axis=1).astype(BF)
        low_value = dvalue.astype(BF)
        dm_ref[...] = low.reshape(dm_ref.shape)
        dv_ref[...] = low_value.reshape(dv_ref.shape)
        sum_ref[:, : 2 * HD] += jnp.sum(low.astype(F32), axis=0, keepdims=True)
        sum_ref[:, 2 * HD :] += jnp.sum(low_value.astype(F32), axis=0, keepdims=True)

    view = lambda a: a.reshape(lead + (a.shape[-1],))
    block = lambda w: pl.BlockSpec(
        (2, 1, 2, 1, share, w), lambda p: (0, p % 2, 0, p // 2, 0, 0)
    )
    info = lambda a: pl.BlockSpec((1,) + a.shape[1:], lambda p: (p, 0, 0))
    packs = MICRO * 2
    context, dmixed, dvalue, sums = call(
        body, (packs,),
        [block(cols), block(HD), block(HD), block(128), info(row_info), info(col_info)],
        [block(HD), block(cols), block(HD), pl.BlockSpec((1, 3 * HD), lambda p: (0, 0))],
        [
            shape_of(lead + (HD,), BF), shape_of(lead + (cols,), BF),
            shape_of(lead + (HD,), BF), shape_of((1, 3 * HD), F32),
        ],
        [], 0, packs * 7 * 2 * ROWS * ROWS * HD, n * cols * 6, 60,
    )(
        view(mixed), view(value), view(dcontext), view(table), row_info, col_info
    )
    return context.reshape(n, HD), dmixed.reshape(n, cols), dvalue.reshape(n, HD), sums


def near_rows(info, near, got):
    rows, cols = near.shape
    half = rows // 2

    def body(info_ref, near_ref, got_ref, own_ref, give_ref):
        def part(k):
            start = pl.multiple_of((info_ref[9] ^ k) * half, half)
            got = got_ref[pl.ds(start, half), :].astype(F32)
            return jnp.where(info_ref[4] == 1, got, 0.0)

        own_ref[...] = near_ref[half:, :].astype(F32) + part(0)
        give_ref[...] = (near_ref[:half, :].astype(F32) + part(1)).astype(BF)

    whole = pl.BlockSpec((rows, cols), lambda i, s: (0, 0))
    out = pl.BlockSpec((half, cols), lambda i, s: (0, 0))
    return call(
        body, (1,), [whole, whole], [out, out],
        [shape_of((half, cols), F32), shape_of((half, cols), BF)],
        [], 1, rows * cols, rows * cols * 4, 14,
    )(info, near, got)


def own_rows(info, owns, gots):
    rows, cols = owns[0].shape
    half = rows // 2
    count = len(owns)

    def body(info_ref, *refs):
        own_refs, got_refs = refs[:count], refs[count : 2 * count]
        mine_ref, give_ref = refs[2 * count :]

        def part(k, i):
            start = pl.multiple_of((info_ref[10] ^ k) * half, half)
            at = pl.ds(start, half)
            return own_refs[i][at, :] + got_refs[i][at, :].astype(F32)

        for i in range(count):
            mine_ref[:, i * cols : (i + 1) * cols] = part(0, i)
            give_ref[:, i * cols : (i + 1) * cols] = part(1, i).astype(BF)

    whole = pl.BlockSpec((rows, cols), lambda i, s: (0, 0))
    out = pl.BlockSpec((half, count * cols), lambda i, s: (0, 0))
    return call(
        body, (1,), [whole] * (2 * count), [out, out],
        [shape_of((half, count * cols), F32), shape_of((half, count * cols), BF)],
        [], 1, rows * cols, count * rows * cols * 6, 16,
    )(info, *owns, *gots)


def place_columns(info, outs, pieces):
    flat = [array for mine, theirs, _ in pieces for array in (mine, theirs)]

    def body(info_ref, *refs):
        ins, out_refs = refs[: len(flat)], refs[len(flat) :]
        for i, (_, _, cuts) in enumerate(pieces):
            for side in (0, 1):
                ref = ins[2 * i + side]
                for first, count, out, offset, stride in cuts:
                    start = pl.multiple_of((info_ref[10] ^ side) * stride + offset, 128)
                    value = ref[:, first : first + count].astype(F32)
                    if outs[out][1]:
                        out_refs[out][pl.ds(start, count), :] = value.T
                    else:
                        out_refs[out][:, pl.ds(start, count)] = value

    return call(
        body, (1,),
        [pl.BlockSpec(array.shape, lambda i, s: (0, 0)) for array in flat],
        [pl.BlockSpec(shape, lambda i, s: (0, 0)) for shape, _ in outs],
        [shape_of(shape, F32) for shape, _ in outs],
        [], 1, 1000, 1000, 30,
    )(info, *flat)


def row_kernel(info, got, parts, weights, rows_in, whole_in, sums, finish, vmem):
    keep = len(got) > 0
    n = parts[0][0].shape[0] // 2
    width = weights[0].shape[0]
    tile = 256
    half_tile = n // 8
    steps = n // tile
    n_rows, n_whole = len(rows_in), len(whole_in)
    n_parts, n_weights = len(parts), len(weights)
    n_outs = 4 if keep else 2

    def body(info_ref, *refs):
        def pairs(count, refs):
            return [(refs[2 * i], refs[2 * i + 1]) for i in range(count)], refs[2 * count :]

        row_refs, refs = pairs(n_rows, refs)
        part_refs, refs = pairs(n_parts, refs)
        whole_refs, refs = refs[:n_whole], refs[n_whole:]
        got_refs, refs = refs[: len(got)], refs[len(got) :]
        w_refs, refs = refs[: 4 * n_weights], refs[4 * n_weights :]
        outs, refs = refs[:n_outs], refs[n_outs:]
        sum_refs, scratch, sem = refs[: len(sums)], refs[len(sums) : -1], refs[-1]
        step = pl.program_id(0)
        first = step == 0
        load = lambda pair: jnp.concatenate([pair[0][...], pair[1][...]])

        @pl.when(first)
        def _():
            for i, weight in enumerate(weights):
                fetch(info_ref, w_refs[4 * i : 4 * i + 4], scratch[i], sem, weight.block)

        def product(i):
            array, index, start = parts[i]
            return dot_nt(load(part_refs[i]), scratch[index][:, start : start + array.shape[1]])

        rows = [load(pair) for pair in row_refs]
        total = finish(first, rows, whole_refs, product, sum_refs)
        if keep:
            for k in range(4):

                @pl.when(step == k)
                def _(k=k):
                    outs[k][...] = (total + got_refs[k // 2][...].astype(F32)).astype(BF)

        else:
            for k in range(2):

                @pl.when(step // 2 == k)
                def _(k=k):
                    outs[k][...] = total.astype(BF)

    def row(w, local):
        base = 0 if keep or local else 8
        return [
            pl.BlockSpec((half_tile, w), lambda i, s: (base + s[11 + i], 0)),
            pl.BlockSpec((half_tile, w), lambda i, s: (base + s[15 + i], 0)),
        ]

    twice = lambda arrays: [array for array in arrays for _ in range(2)]
    ks = sum(part[0].shape[1] for part in parts)
    fixed = pl.BlockSpec((tile, width), lambda i, s: (0, 0))
    pair = [
        pl.BlockSpec((tile, width), lambda i, s: (jnp.minimum(i, 1), 0)),
        pl.BlockSpec((tile, width), lambda i, s: (jnp.maximum(i - 2, 0), 0)),
    ]
    if keep:
        out_specs, out_shape = [fixed] * 4, [shape_of((tile, width), BF)] * 4
    else:
        out_specs, out_shape = pair, [shape_of((2 * tile, width), BF)] * 2
    return call(
        body, (steps,),
        [spec for array in rows_in for spec in row(array.shape[1], True)]
        + [spec for part in parts for spec in row(part[0].shape[1], False)]
        + [pl.BlockSpec(array.shape, lambda i, s: (0, 0)) for array in whole_in]
        + pair[: len(got)] + [ANY] * (4 * n_weights),
        out_specs + [pl.BlockSpec(shape, lambda i, s: (0, 0)) for shape in sums],
        out_shape + [shape_of(shape, F32) for shape in sums],
        [pltpu.VMEM(weight.shape, BF) for weight in weights] + [pltpu.SemaphoreType.DMA],
        1, 2 * n * width * ks, 2 * n * (2 * width + ks), vmem,
    )(
        info, *twice(rows_in), *twice([part[0] for part in parts]), *whole_in, *got,
        *[array for weight in weights for array in weight.arrays],
    )


def out_rows(info, parts, weights, got):
    def finish(first, rows, whole, product, sums):
        total = product(0)
        for i in range(1, len(parts)):
            total += product(i)
        return total

    return row_kernel(info, got, parts, weights, [], [], [], finish, 60 if got else 60)


def back_rows(info, parts, weights, n_attn, x, vectors, got):
    def finish(first, rows, whole, product, sums):
        v_ref, sum_ref = whole[0], sums[0]

        @pl.when(first)
        def _():
            sum_ref[...] = jnp.zeros_like(sum_ref)

        plain, _ = plain_of(rows[-1].astype(F32))
        dattn = product(0)
        for i in range(1, n_attn):
            dattn += product(i)
        dmlp = product(n_attn)
        for i in range(n_attn + 1, len(parts)):
            dmlp += product(i)
        for i, grad in enumerate((dattn, dmlp)):
            sum_ref[2 * i : 2 * i + 1] += jnp.sum(grad * plain, axis=0, keepdims=True)
            sum_ref[2 * i + 1 : 2 * i + 2] += jnp.sum(grad, axis=0, keepdims=True)
        return dattn * v_ref[0:1] + dmlp * v_ref[2:3]

    return row_kernel(
        info, got, parts, weights, [x], [vectors], [(4, vectors.shape[1])], finish,
        60 if got else 60,
    )


ORDER = [
    "vy", "y01", "xx", "xc0", "-vy", "vz1", "tab", "-y01",
    "a0", "xy", "-vz1", "vz2", "a1", "-xx", "xc1", "xd1",
    "-a0", "b0", "-vz2", "y2", "-xy", "xc2", "xd2", "-a1",
    "-b0", "c0", "b1", "gx", "-xc0", "-xc1", "-xc2", "-xd1",
    "-xd2", "xc3", "-y2", "a2", "gy", "-xc3", "xs", "norm",
    "-gx", "gc1", "y3", "-c0", "-b1", "c1", "feed0", "-y3",
    "a3", "-a2", "b2", "-gy", "gc2", "gd1", "gd2", "gc0",
    "-c1", "-gd1", "-gd2", "gc3", "y45", "-b2", "-a3", "b3",
    "-gc0", "-gc1", "-gc2", "-gc3", "gs", "go0", "c2r0", "-y45",
    "a4", "fb0", "gi0", "-b3", "c3r1", "-c2r0", "p0", "heads",
    "-c3r1", "val", "-p0", "q0", "-a4", "b4", "a5", "att",
    "-q0", "gqk", "-b4", "c4r2", "p1", "-a5", "b5", "gvp",
    "-b5", "c5r3", "-c4r2", "p2", "feed1", "go1", "r4", "-p1",
    "q1", "-c5r3", "p3", "fb1", "gi1", "og", "oc", "-q1",
    "f01", "-p2", "q2", "r5", "bg", "hc", "-r4", "p4",
    "-oc", "ok", "-p3", "q3", "o1y", "o1x", "-hc", "-f01",
    "bk", "-q2", "-q3", "f23", "-r5", "p5", "h1y", "h1x",
    "-p4", "q4", "-o1y", "-o1x", "o2x", "o2y", "vs", "vc",
    "-p5", "q5", "-vc", "vx", "-h1y", "-h1x", "h2x", "h2y",
    "-vx", "vyy", "-o2x", "-o2y", "fo", "-q4", "-q5", "f45",
    "-vyy", "vz", "-f23", "-h2x", "-h2y", "fr", "-vz", "fv",
    "-f45", "fw",
]


def layer_program(n_dp, n_tensor):
    n_z = n_dp // 2
    n_dev = n_dp * n_tensor
    core, xbit, ybit, zbit = 1, 2, 4, 8
    ids = range(n_dev)
    flip = lambda bit: [(i, i ^ bit) for i in ids]
    flip_c, flip_x, flip_y, flip_z = flip(core), flip(xbit), flip(ybit), flip(zbit)
    mirror = {0: 0, 1: 2, 2: 1, 3: 3}
    mid = [
        (i, mirror[i // zbit] * zbit + (i % zbit if i // zbit in (1, 2) else i % zbit ^ core))
        for i in ids if n_z == 4
    ]
    columns = [[z * 2 + y for z in range(n_z)] for y in range(2)]

    def per_device(
        tokens, lengths, out_grad, attn_gain, attn_shift, mlp_gain, mlp_shift,
        w_qkv, b_qkv, w_proj, b_proj, w_in, b_in, w_out, b_out,
    ):
        dp = lax.axis_index("dp")
        tensor = lax.axis_index("tensor")
        z, y = dp // 2, dp % 2
        x, c = tensor // 2, tensor % 2
        share = tokens.shape[1]
        width = tokens.shape[2]
        upper = z >= 2
        even = z % 2 == 0
        token = []
        is_mid = (z == 1) | (z == 2)

        def turn_of(*values):
            out = lax.optimization_barrier(values + tuple(token))[: len(values)] if token else values
            return out if len(out) > 1 else out[0]

        def passed(*values):
            token.extend(values)

        def worked(*values):
            token[:] = values

        if n_z == 4:
            far = jnp.where(upper, 1, 2)
            low_far = jnp.where(upper, 0, 2)
            places_z = [z, z ^ 1, far, far ^ 1, is_mid, low_far, low_far + 1, z ^ 1, z]
        else:
            places_z = [0, 1, 2, 3, 1, 0, 1, 2, 3]
        info = jnp.stack(
            [jnp.asarray(v, jnp.int32) for v in places_z + [z % 2, y, 4, 3, 0, 1, 6, 7, 2, 5]]
        )

        h_cols = w_in.shape[1] // 2
        half_h = h_cols // 2
        q_cols = w_qkv.shape[1] // 2
        p_cols = w_proj.shape[0] // 2

        w_out_t, w_proj_t = w_out.T, w_proj.T
        cuts = [
            [(w_in, h_cols, 0, half_h)],
            [(w_out_t, h_cols, 0, half_h)],
            [(w_qkv, q_cols, 0, 2 * HD)],
            [(w_qkv, q_cols, 2 * HD, HD), (w_proj_t, p_cols, 0, p_cols)],
            [(w_in, h_cols, half_h, half_h)],
            [(w_out_t, h_cols, half_h, half_h)],
        ]
        V = {}

        def side_of(k, side):
            parts = [
                lax.dynamic_slice_in_dim(weight, side * sub + start, count, 1)
                for weight, sub, start, count in cuts[k]
            ]
            return parts[0] if len(parts) == 1 else jnp.concatenate(parts, axis=1)

        def send_y(name, chunks):
            theirs = jnp.concatenate([side_of(k, 1 - y) for k in chunks], axis=1)
            V[name] = swap(turn_of(theirs), flip_y)
            start = 0
            for k in chunks:
                mine = side_of(k, y)
                V["from", k] = (name, mine, start)
                start += mine.shape[1]

        def step_a(k):
            name, mine, start = V["from", k]
            got = turn_of(V[name])
            pair = ordered(y == 0, mine, got[:, start : start + mine.shape[1]])
            V["pair", k] = pair
            V["a%d" % k] = swap(pair, flip_z) if n_z == 4 else pair

        def step_b(k):
            both = jnp.concatenate(turn_of(V["pair", k], V["a%d" % k]))
            V["b%d" % k] = swap(both, mid) if n_z == 4 else both

        def cross(k, j, name):
            if n_z == 4:
                if j is None:
                    payload = turn_of(V["b%d" % k])
                elif k is None:
                    payload = turn_of(V["sum", j][0])
                else:
                    payload = jnp.where(is_mid, *turn_of(V["b%d" % k], V["sum", j][0]))
                got = swap(payload, flip_z)
            else:
                got = turn_of(V["b%d" % k] if j is None else V["sum", j][0])
            V[name] = got
            if k is not None:
                V["arrived", k] = name
            if j is not None:
                V["crossed", j] = name

        def full(k):
            if n_z == 4:
                arrays = (
                    V["pair", k], V["a%d" % k], V["b%d" % k], V[V["arrived", k]]
                )
            else:
                whole = lax.all_gather(
                    V["pair", k], "dp", axis_index_groups=columns, tiled=True
                )
                quarter = jnp.split(whole, 4)
                half = jnp.concatenate(quarter[2:])
                arrays = (quarter[0], quarter[1], half, half)
            return Gathered(arrays)

        def step_p(j):
            far, got = turn_of(V["sum", j][0], V[V["crossed", j]])
            far = (far.astype(F32) + got.astype(F32)).astype(BF)
            V["p%d" % j] = swap(far, mid) if n_z == 4 else far

        def step_q(j):
            near, got = turn_of(V["sum", j][1], V["p%d" % j])
            if n_z == 4:
                V["own", j], give = near_rows(info, near, got)
                V["q%d" % j] = swap(give, flip_z)
            else:
                own = lax.psum_scatter(
                    jnp.concatenate([V["sum", j][0], near]), "dp", scatter_dimension=0,
                    axis_index_groups=columns, tiled=True,
                ).astype(F32)
                V["own", j], V["q%d" % j] = own, jnp.zeros_like(own, BF)

        def step_f(a, b, name):
            values = turn_of(V["own", a], V["own", b], V["q%d" % a], V["q%d" % b])
            V["mine", name], give = own_rows(info, values[:2], values[2:])
            V[name] = swap(give, flip_y)

        def plane_core(name, k, own):
            g = name[0]
            part = own if k == 0 else V[g + "xy"[k - 1]] if k < 3 else None
            if k == 3:
                part = jnp.concatenate(turn_of(V[g + "d1"], V[g + "d2"]))
            else:
                part = turn_of(part)
            V[g + "part", k] = part.reshape(-1, width)
            V[name] = swap(V[g + "part", k], flip_c)

        def plane_rows(g):
            parts = [V[g + "part", k] for k in range(4)] + [V["%sc%d" % (g, k)] for k in range(4)]
            V[g + "mine"], V[g + "c"] = stack_rows(turn_of(*parts))
            worked(V[g + "mine"])

        def send_core(name, parts):
            V[name] = tuple(swap(part, flip_c) for part in turn_of(*parts))

        def sum_first(g, name, perm, at):
            value = turn_of(V[g + "keep"][at]).reshape(2, share, width)
            V[g + name] = swap(value, perm)

        def sum_second(g, name, perm, at):
            got = turn_of(V[g + ("1y", "1x")[at]])
            total = V[g + "keep"][2 + at].reshape(2, share, width).astype(F32) + got.astype(F32)
            V[g + "left", at] = total[0]
            V[g + name] = swap(total[1].astype(BF), perm)

        def sum_result(g):
            got = turn_of(V[g + "2x"], V[g + "2y"])
            return jnp.stack([V[g + "left", at] + got[at].astype(F32) for at in (0, 1)])

        own_places = tensor * share + jnp.arange(share, dtype=jnp.int32)
        own_ends = jnp.cumsum(lengths[:, 0], axis=-1)
        own_segment = jnp.sum((own_places[:, None] >= own_ends[:, None, :]).astype(jnp.int32), axis=-1)
        valid = (own_segment < SEGS - 1).astype(F32)[..., None]
        x_own = tokens.astype(F32)
        g_own = out_grad.astype(F32) * valid
        g_low = g_own.astype(BF).reshape(MICRO, share, width)
        x_low = tokens.reshape(MICRO, share, width)
        bias_in = lax.dynamic_slice_in_dim(b_in, y * h_cols, h_cols).astype(F32)[None]
        bias_qkv = lax.dynamic_slice_in_dim(b_qkv, y * q_cols, q_cols).astype(F32)[None]
        pair_bits = jnp.arange(2, dtype=jnp.int32)
        t_of = (x ^ pair_bits)[None, :] * 2 + (c ^ pair_bits)[:, None]
        places = (t_of[..., None] * share + jnp.arange(share, dtype=jnp.int32)).reshape(-1)

        def send_vectors():
            vectors = jnp.stack([attn_gain, attn_shift, mlp_gain, mlp_shift, b_proj, b_out])
            V["vectors"] = vectors
            V["vy"] = swap(turn_of(vectors), flip_y)
            V["lengths"] = swap(turn_of(lengths[:, 0]), flip_y)

        def send_vectors_z(name, bit, low_first):
            if name == "vz1":
                pair = ordered(y == 0, V["vectors"][None], turn_of(V["vy"])[None])
                if n_z != 4:
                    V["vz1"] = V["vz2"] = pair
                    V["small"] = lax.all_gather(
                        pair, "dp", axis_index_groups=columns, tiled=True
                    )
                    return
            elif n_z != 4:
                return
            else:
                pair = ordered(even, V["vectors_y"], turn_of(V["vz1"]))
            V["vectors_y" if name == "vz1" else "vectors_z"] = pair
            V[name] = swap(pair, flip(bit))

        def send_part(name, value, perm, index=None):
            def run():
                part = turn_of(value if index is None else V[value])
                V[name] = swap(part if index is None else part[index], perm)

            return run

        def send_sums_c():
            V["vc"] = swap_half("total", 3, c, flip_c, "vc")

        def swap_half(source, axis, bit, perm, name):
            total = turn_of(V[source])
            low, high = jnp.split(total, 2, axis=axis)
            got = swap(jnp.where(bit == 0, high, low), perm)
            V["half " + name] = jnp.where(bit == 0, low, high)
            return got

        def send_sums_x():
            V["total x"] = V["half vc"] + turn_of(V["vc"])
            V["vx"] = swap_half("total x", 2, x, flip_x, "vx")

        def send_sums_y():
            V["total y"] = V["half vx"] + turn_of(V["vx"])
            V["vyy"] = swap_half("total y", 1, y, flip_y, "vyy")

        def send_sums_z():
            total = (V["half vyy"] + turn_of(V["vyy"])).reshape(n_z, -1)
            if n_z == 4:
                row = lambda k: lax.dynamic_slice_in_dim(total, z ^ k, 1, 0)
                V["row"] = row(0)
                V["vz"] = tuple(swap(row(k), flip(zbit * k)) for k in (1, 2, 3))
            else:
                V["row"] = lax.psum_scatter(
                    total.reshape(-1), "dp", axis_index_groups=columns, tiled=True
                )
                V["vz"] = ()

        def norm():
            if n_z == 4:
                small = ordered(~upper, V["vectors_z"], turn_of(V["vz2"]))
            else:
                small = V["small"]
            small = small.transpose(1, 0, 2).reshape(6, width).astype(F32)
            V["small"] = jnp.concatenate([small, jnp.zeros((2, width), F32)])
            V["attn"], V["mlp"] = norm_rows(turn_of(V["xmine"]), V["xc"], V["small"])
            worked(V["attn"])

        def tab():
            lengths_all = jnp.stack([lengths[:, 0], turn_of(V["lengths"])])
            ends = jnp.cumsum(lengths_all, axis=-1)
            gone = (places[:, None] >= ends[..., None, :]).astype(jnp.int32)
            segment = jnp.sum(gone, axis=-1)
            position = places - jnp.sum(gone * lengths_all[..., None, :], axis=-1)
            row_position = position.reshape(2, MICRO, 2, 2, share).transpose(2, 0, 3, 1, 4)
            lanes = jnp.arange(2 * ROT)
            frequency = 10000.0 ** (-2.0 * (lanes % (ROT // 2)).astype(F32) / ROT)
            angle = row_position.reshape(-1).astype(F32)[:, None] * frequency
            table = jnp.where(lanes < ROT, jnp.cos(angle), jnp.sin(angle))
            pack_segment = segment.transpose(1, 0, 2).reshape(MICRO * 2, ROWS)
            pack_places = jnp.broadcast_to(places, (MICRO * 2, ROWS))
            row_info = jnp.stack([pack_segment, pack_places], axis=2)
            col_info = jnp.stack([pack_segment, pack_places], axis=1)
            V["table"] = lax.optimization_barrier((table, row_info, col_info))
            worked(*V["table"])

        def run_feed(i, k):
            bias = bias_in[:, i * half_h : (i + 1) * half_h]
            V["active", i], V["slope", i] = feed(info, turn_of(V["mlp"]), full(k), bias)
            worked(V["active", i])

        def sums_of(j, *groups):
            V["sum", j] = weight_grad(info, list(groups))
            worked(V["sum", j][0])

        def halves_of(value):
            rows = turn_of(V["gmine"]), V["gc"]
            return [(rows[0], value, 0), (rows[1], value, 1)]

        def run_back(i, k):
            rows = turn_of(V["gmine"]), V["gc"]
            V["dhidden", i], V["dsum", i] = feed_back(info, rows, full(k), V["slope", i])
            worked(V["dhidden", i])

        def heads():
            V["mixed"] = project_heads(
                info, turn_of(V["attn"]), full(2), bias_qkv[:, : 2 * HD], V["table"][0]
            )
            worked(V["mixed"])

        def val():
            V["value"], V["dcontext"] = project_values(
                info, turn_of(V["attn"]), (V["gmine"], V["gc"]), full(3), bias_qkv[:, 2 * HD :]
            )
            worked(V["value"])

        def att():
            V["context"], V["dmixed"], V["dvalue"], V["dmixed sum"] = attend(
                turn_of(V["mixed"]), V["value"], V["dcontext"], *V["table"]
            )
            worked(V["context"])

        def run_out(keep):
            parts = [(turn_of(V["context"]), 0, HD), (V["active", 0], 1, 0), (V["active", 1], 2, 0)]
            got = turn_of(*V["oc"]) if keep else ()
            outs = out_rows(info, parts, (full(3), full(1), full(5)), got)
            V["okeep" if keep else "ogive"] = outs
            worked(outs[0])

        def run_rows(keep):
            parts = [
                (turn_of(V["dmixed"]), 0, 0), (V["dvalue"], 1, 0),
                (V["dhidden", 0], 2, 0), (V["dhidden", 1], 3, 0),
            ]
            got = turn_of(*V["hc"]) if keep else ()
            outs = back_rows(
                info, parts, (full(2), full(3), full(0), full(4)), 2,
                V["xmine"] if keep else V["xc"], V["small"], got,
            )
            V["hkeep" if keep else "hgive"] = outs[:-1]
            V["sums", keep] = outs[-1]
            worked(outs[0])

        def vector_total():
            g_sum = jnp.sum(turn_of(g_own), axis=(0, 1))[None]
            sums = jnp.concatenate([turn_of(V["sums", True]) + V["sums", False], g_sum])
            sums = sums.reshape(5, n_dev, -1).transpose(1, 0, 2).reshape(n_dev, -1)
            dhidden_sum = jnp.concatenate([V["dsum", 0], V["dsum", 1]], axis=1)
            bias_sums = jnp.concatenate(
                [
                    dhidden_sum.reshape(n_dp // 2, -1),
                    V["dmixed sum"].reshape(n_dp // 2, -1),
                ],
                axis=-1,
            )
            spread_bias = jnp.zeros((n_dp, n_tensor, bias_sums.shape[-1]), F32)
            spread_bias = lax.dynamic_update_slice(
                spread_bias, bias_sums[:, None], (y * (n_dp // 2), tensor, 0)
            ).reshape(n_dev, -1)
            total = jnp.concatenate([sums, spread_bias], axis=-1)
            V["total"] = total.reshape(n_z, 2, 2, 2, -1)
            worked(V["total"])

        def result_output():
            small = V["small"]
            V["output"] = (x_own + sum_result("o") + small[4] + small[5]).astype(BF)
            worked(V["output"])

        def result_tokens():
            back = sum_result("h")
            own_plain, own_spread = plain_of(x_own)
            V["grad tokens"] = g_own + own_spread * (
                back
                - jnp.mean(back, axis=-1, keepdims=True)
                - own_plain * jnp.mean(back * own_plain, axis=-1, keepdims=True)
            )
            worked(V["grad tokens"])

        def result_weights():
            rest = half_h
            V["weights"] = place_columns(
                info,
                [
                    (w_qkv.shape, False), (w_proj.shape, True),
                    (w_in.shape, False), (w_out.shape, True),
                ],
                [
                    (V["mine", "f01"], turn_of(V["f01"]),
                     [(0, rest, 3, 0, h_cols), (rest, rest, 2, 0, h_cols)]),
                    (V["mine", "f23"], turn_of(V["f23"]),
                     [(0, 2 * HD, 0, 0, q_cols), (2 * HD, HD, 0, 2 * HD, q_cols),
                      (3 * HD, p_cols, 1, 0, p_cols)]),
                    (V["mine", "f45"], turn_of(V["f45"]),
                     [(0, rest, 3, half_h, h_cols), (rest, rest, 2, half_h, h_cols)]),
                ],
            )
            worked(V["weights"][0])

        def result_vectors():
            total = V["row"]
            for got in V["vz"]:
                total = total + turn_of(got)
            V["vector sums"] = total.reshape(-1)

        steps = {
            "y01": lambda: send_y("y01", (0, 1)),
            "y2": lambda: send_y("y2", (2,)),
            "y3": lambda: send_y("y3", (3,)),
            "y45": lambda: send_y("y45", (4, 5)),
            "vy": send_vectors,
            "vz1": lambda: send_vectors_z("vz1", zbit, even),
            "vz2": lambda: send_vectors_z("vz2", 2 * zbit, ~upper),
            "xx": send_part("xx", x_low, flip_x),
            "xy": send_part("xy", x_low, flip_y),
            "xd1": send_part("xd1", "xx", flip_y, 0),
            "xd2": send_part("xd2", "xy", flip_x, 1),
            "xs": lambda: plane_rows("x"),
            "gx": send_part("gx", g_low, flip_x),
            "gy": send_part("gy", g_low, flip_y),
            "gd1": send_part("gd1", "gx", flip_y, 0),
            "gd2": send_part("gd2", "gy", flip_x, 1),
            "gs": lambda: plane_rows("g"),
            "norm": norm, "tab": tab, "heads": heads, "val": val, "att": att,
            "feed0": lambda: run_feed(0, 0),
            "feed1": lambda: run_feed(1, 4),
            "fb0": lambda: run_back(0, 1),
            "fb1": lambda: run_back(1, 5),
            "go0": lambda: sums_of(0, halves_of(V["active", 0])),
            "gi0": lambda: sums_of(1, [(turn_of(V["mlp"]), V["dhidden", 0], 0)]),
            "gqk": lambda: sums_of(2, [(turn_of(V["attn"]), V["dmixed"], 0)]),
            "gvp": lambda: sums_of(
                3, [(turn_of(V["attn"]), V["dvalue"], 0)], halves_of(V["context"])
            ),
            "go1": lambda: sums_of(4, halves_of(V["active", 1])),
            "gi1": lambda: sums_of(5, [(turn_of(V["mlp"]), V["dhidden", 1], 0)]),
            "og": lambda: run_out(False), "ok": lambda: run_out(True),
            "bg": lambda: run_rows(False), "bk": lambda: run_rows(True),
            "f01": lambda: step_f(0, 1, "f01"),
            "f23": lambda: step_f(2, 3, "f23"),
            "f45": lambda: step_f(4, 5, "f45"),
            "vs": vector_total, "vc": send_sums_c, "vx": send_sums_x,
            "vyy": send_sums_y, "vz": send_sums_z, "fv": result_vectors,
            "fo": result_output, "fr": result_tokens, "fw": result_weights,
        }
        for g in "oh":
            steps[g + "c"] = lambda g=g: send_core(g + "c", V[g + "give"])
            steps[g + "1y"] = lambda g=g: sum_first(g, "1y", flip_y, 0)
            steps[g + "1x"] = lambda g=g: sum_first(g, "1x", flip_x, 1)
            steps[g + "2x"] = lambda g=g: sum_second(g, "2x", flip_x, 0)
            steps[g + "2y"] = lambda g=g: sum_second(g, "2y", flip_y, 1)
        for k in range(4):
            steps["xc%d" % k] = lambda k=k: plane_core("xc%d" % k, k, x_low)
            steps["gc%d" % k] = lambda k=k: plane_core("gc%d" % k, k, g_low)
        for k in range(6):
            steps["a%d" % k] = lambda k=k: step_a(k)
            steps["b%d" % k] = lambda k=k: step_b(k)
            steps["c%d" % k] = lambda k=k: cross(k, None, "c%d" % k)
            steps["r%d" % k] = lambda k=k: cross(None, k, "r%d" % k)
            steps["p%d" % k] = lambda k=k: step_p(k)
            steps["q%d" % k] = lambda k=k: step_q(k)
            for j in range(6):
                name = "c%dr%d" % (k, j)
                steps[name] = lambda k=k, j=j, name=name: cross(k, j, name)
        for word in ORDER:
            if word[0] == "-":
                value = V[word[1:]]
                extra = (V["lengths"],) if word == "-vy" else ()
                passed(*(value if isinstance(value, tuple) else (value,)), *extra)
            else:
                steps[word]()

        piece = width // n_dev
        sums = V["vector sums"]
        pieces = [sums[k * piece : (k + 1) * piece] for k in range(5)]
        bias_piece = sums[5 * piece :]
        in_piece = b_in.shape[0] // n_dp
        grad_qkv, grad_proj, grad_in, grad_out = V["weights"]
        return (
            V["output"], V["grad tokens"], pieces[0], pieces[1], pieces[2], pieces[3],
            grad_qkv, bias_piece[in_piece:].reshape(1, -1), grad_proj, pieces[4],
            grad_in, bias_piece[:in_piece].reshape(1, -1), grad_out, pieces[4],
        )

    return per_device


def solution(mesh):
    n_dp, n_tensor = mesh.shape["dp"], mesh.shape["tensor"]
    rows = P(None, AXES, None)
    in_specs = (
        rows, P(None, "dp", None), rows, P("dp"), P("dp"), P("dp"), P("dp"),
        P("dp", "tensor"), P("tensor"), P("tensor", "dp"), P("dp"),
        P("dp", "tensor"), P("tensor"), P("tensor", "dp"), P("dp"),
    )
    vector = P(AXES)
    out_specs = (
        rows, rows, vector, vector, vector, vector,
        P("dp", "tensor"), P("tensor", "dp"), P("tensor", "dp"), vector,
        P("dp", "tensor"), P("tensor", "dp"), P("tensor", "dp"), vector,
    )
    return jax.shard_map(
        layer_program(n_dp, n_tensor), mesh=mesh,
        in_specs=in_specs, out_specs=out_specs, check_vma=False,
    )
```

```python
import jax
import jax.numpy as jnp
from jax import lax
from jax.experimental import pallas as pl
from jax.experimental.pallas import tpu as pltpu
from jax.sharding import PartitionSpec as P

HD = 256
ROT = 64
MICRO = 2
ROWS = 512
SEGS = 8
AXES = ("dp", "tensor")
BF = jnp.bfloat16
F32 = jnp.float32
MIB = 1 << 20
SCALE = HD ** (-0.5)
ANY = pl.BlockSpec(memory_space=pl.ANY)


def swap(value, perm):
    return lax.ppermute(value, AXES, perm)


def dot_nn(a, b):
    return jnp.dot(a, b, preferred_element_type=F32)


def dot_nt(a, b):
    return lax.dot_general(a, b, (((1,), (1,)), ((), ())), preferred_element_type=F32)


def dot_tn(a, b):
    return lax.dot_general(a, b, (((0,), (0,)), ((), ())), preferred_element_type=F32)


def ordered(first, low, high, axis=0):
    return jnp.where(
        first,
        jnp.concatenate([low, high], axis=axis),
        jnp.concatenate([high, low], axis=axis),
    )


def shape_of(shape, dtype):
    return jax.ShapeDtypeStruct(shape, dtype)


def call(body, grid, in_specs, out_specs, out_shape, scratch, prefetch, flops, nbytes, vmem):
    return pl.pallas_call(
        body,
        out_shape=out_shape,
        grid_spec=pltpu.PrefetchScalarGridSpec(
            num_scalar_prefetch=prefetch,
            grid=grid,
            in_specs=in_specs,
            out_specs=out_specs,
            scratch_shapes=scratch,
        ),
        compiler_params=pltpu.CompilerParams(
            dimension_semantics=("arbitrary",) * len(grid), vmem_limit_bytes=vmem * MIB
        ),
        cost_estimate=pl.CostEstimate(
            flops=int(flops) * 7 // 10, bytes_accessed=0, transcendentals=0
        ),
    )


class Gathered:
    def __init__(self, arrays):
        self.arrays = arrays
        self.block, self.other = arrays[0].shape
        self.shape = (4 * self.block, self.other)


def fetch(info, refs, scratch, sem, block):
    def part(ref, index, place):
        source = ref.at[pl.ds(index * block, block), :]
        target = scratch.at[pl.ds(pl.multiple_of(place * block, block), block), :]
        return pltpu.make_async_copy(source, target, sem)

    own, partner, far_mid, far_out = refs
    part(own, 0, info[0]).start()
    part(partner, 0, info[1]).start()

    @pl.when(info[4] == 1)
    def _():
        part(far_mid, 0, info[2]).start()
        part(far_mid, 1, info[3]).start()

    @pl.when(info[4] == 0)
    def _():
        part(far_out, 0, info[2]).start()
        part(far_out, 1, info[3]).start()

    part(own, 0, info[0]).wait()
    part(partner, 0, info[1]).wait()
    part(far_out, 0, info[2]).wait()
    part(far_out, 1, info[3]).wait()


def plain_of(rows):
    center = rows - jnp.mean(rows, axis=-1, keepdims=True)
    spread = lax.rsqrt(jnp.mean(center * center, axis=-1, keepdims=True) + 1e-05)
    return center * spread, spread


def norm_rows(mine, sibling, vectors):
    n, width = mine.shape
    tile = 256
    steps = n // tile

    def body(x_ref, y_ref, v_ref, a_ref, m_ref):
        def write(rows):
            plain, _ = plain_of(rows.astype(F32))
            a_ref[...] = (plain * v_ref[0:1] + v_ref[1:2]).astype(BF)
            m_ref[...] = (plain * v_ref[2:3] + v_ref[3:4]).astype(BF)

        @pl.when(pl.program_id(0) < steps)
        def _():
            write(x_ref[...])

        @pl.when(pl.program_id(0) >= steps)
        def _():
            write(y_ref[...])

    rows = pl.BlockSpec((tile, width), lambda i: (i, 0))
    return call(
        body, (2 * steps,),
        [
            pl.BlockSpec((tile, width), lambda i: (jnp.minimum(i, steps - 1), 0)),
            pl.BlockSpec((tile, width), lambda i: (jnp.maximum(i - steps, 0), 0)),
            pl.BlockSpec(vectors.shape, lambda i: (0, 0)),
        ],
        [rows, rows],
        [shape_of((2 * n, width), BF)] * 2, [], 0, 2 * n * width * 600, 2 * n * width * 6, 16,
    )(mine, sibling, vectors)


def stack_rows(parts):
    rows, width = parts[0].shape
    half = len(parts) // 2

    def body(*refs):
        ins, outs, sem = refs[: 2 * half], refs[2 * half : -1], refs[-1]
        copies = [
            pltpu.make_async_copy(
                ins[k], outs[k // half].at[pl.ds((k % half) * rows, rows), :], sem.at[k]
            )
            for k in range(2 * half)
        ]
        for copy in copies:
            copy.start()
        for copy in copies:
            copy.wait()

    return call(
        body, (1,), [ANY] * (2 * half), [ANY] * 2, [shape_of((half * rows, width), BF)] * 2,
        [pltpu.SemaphoreType.DMA((2 * half,))], 0, 1000, 1000, 4,
    )(*parts)


def feed(info, rows, weight, bias):
    n, width = rows.shape
    cols = weight.other
    tile = 512

    def body(info_ref, x_ref, b_ref, p0, p1, p2, p3, active_ref, slope_ref, w, sem):
        @pl.when(pl.program_id(0) == 0)
        def _():
            fetch(info_ref, (p0, p1, p2, p3), w, sem, weight.block)

        hidden = dot_nn(x_ref[...], w[...]) + b_ref[...]
        cdf = 0.5 * (1.0 + lax.erf(hidden * 0.7071067811865476))
        active_ref[...] = (hidden * cdf).astype(BF)
        slope_ref[...] = cdf + hidden * jnp.exp(-0.5 * hidden * hidden) * 0.3989422804014327

    out = pl.BlockSpec((tile, cols), lambda i, s: (i, 0))
    return call(
        body, (n // tile,),
        [
            pl.BlockSpec((tile, width), lambda i, s: (i, 0)),
            pl.BlockSpec((1, cols), lambda i, s: (0, 0)),
        ] + [ANY] * 4,
        [out, out],
        [shape_of((n, cols), BF), shape_of((n, cols), F32)],
        [pltpu.VMEM(weight.shape, BF), pltpu.SemaphoreType.DMA],
        1, 2 * n * width * cols, 2 * n * width + 6 * n * cols, 18,
    )(info, rows, bias, *weight.arrays)


def halves_specs(tile, width, steps):
    return [
        pl.BlockSpec((tile, width), lambda i, s: (jnp.minimum(i, steps - 1), 0)),
        pl.BlockSpec((tile, width), lambda i, s: (jnp.maximum(i - steps, 0), 0)),
    ]


def feed_back(info, rows, weight, slope):
    n, width = rows[0].shape
    cols = weight.other
    tile = 512
    steps = n // tile

    def body(info_ref, g_ref, h_ref, s_ref, p0, p1, p2, p3, out_ref, sum_ref, w, sem):
        step = pl.program_id(0)

        @pl.when(step == 0)
        def _():
            fetch(info_ref, (p0, p1, p2, p3), w, sem, weight.block)
            sum_ref[...] = jnp.zeros_like(sum_ref)

        def write(ref):
            low = (dot_nn(ref[...], w[...]) * s_ref[...]).astype(BF)
            out_ref[...] = low
            sum_ref[...] += jnp.sum(low.astype(F32), axis=0, keepdims=True)

        @pl.when(step < steps)
        def _():
            write(g_ref)

        @pl.when(step >= steps)
        def _():
            write(h_ref)

    block = lambda width_of: pl.BlockSpec((tile, width_of), lambda i, s: (i, 0))
    return call(
        body, (2 * steps,), halves_specs(tile, width, steps) + [block(cols)] + [ANY] * 4,
        [block(cols), pl.BlockSpec((1, cols), lambda i, s: (0, 0))],
        [shape_of((2 * n, cols), BF), shape_of((1, cols), F32)],
        [pltpu.VMEM(weight.shape, BF), pltpu.SemaphoreType.DMA],
        1, 4 * n * width * cols, 4 * n * width + 12 * n * cols, 20,
    )(info, *rows, slope, *weight.arrays)


def weight_grad(info, groups):
    flat = [pair for group in groups for pair in group]
    width = flat[0][0].shape[1]
    tile = width // 4
    counts = [group[0][1].shape[1] for group in groups]
    cols = sum(counts)

    def body(info_ref, *refs):
        lefts, rights = refs[: len(flat)], refs[len(flat) : 2 * len(flat)]
        far_ref, near_ref = refs[2 * len(flat) :]

        def write(out_ref):
            at, start = 0, 0
            for group, count in zip(groups, counts):
                total = dot_tn(lefts[at][...], rights[at][...])
                for k in range(1, len(group)):
                    total += dot_tn(lefts[at + k][...], rights[at + k][...])
                out_ref[:, start : start + count] = total.astype(BF)
                at, start = at + len(group), start + count

        @pl.when(pl.program_id(0) < 2)
        def _():
            write(far_ref)

        @pl.when(pl.program_id(0) >= 2)
        def _():
            write(near_ref)

    return call(
        body, (4,),
        [pl.BlockSpec((left.shape[0], tile), lambda i, s: (0, s[5 + i])) for left, _, _ in flat]
        + [
            pl.BlockSpec((left.shape[0], right.shape[1]), lambda i, s, k=k: (k, 0))
            for left, right, k in flat
        ],
        [
            pl.BlockSpec((tile, cols), lambda i, s: (jnp.minimum(i, 1), 0)),
            pl.BlockSpec((tile, cols), lambda i, s: (jnp.maximum(i - 2, 0), 0)),
        ],
        [shape_of((width // 2, cols), BF)] * 2,
        [], 1, sum(2 * width * left.shape[0] * right.shape[1] for left, right, _ in flat),
        sum(2 * left.shape[0] * (width + right.shape[1]) for left, right, _ in flat), 24,
    )(info, *[pair[0] for pair in flat], *[pair[1] for pair in flat])


def turn(values, table, sign):
    lane = lax.broadcasted_iota(jnp.int32, values.shape, 1)
    half = ROT // 2
    partner = jnp.where(
        lane < half, -pltpu.roll(values, 128 - half, 1), pltpu.roll(values, half, 1)
    )
    cosine = jnp.where(lane < ROT, table, 1.0)
    sine = jnp.where(lane < ROT, pltpu.roll(table, ROT, 1), 0.0)
    return values * cosine + partner * (sign * sine)


def project_heads(info, rows, weight, bias, table):
    n, width = rows.shape
    cols = weight.other
    tile = 512

    def body(info_ref, x_ref, b_ref, t_ref, p0, p1, p2, p3, out_ref, w, sem):
        @pl.when(pl.program_id(0) == 0)
        def _():
            fetch(info_ref, (p0, p1, p2, p3), w, sem, weight.block)

        mixed = dot_nn(x_ref[...], w[...]) + b_ref[...]
        for start in range(0, cols, HD):
            head = mixed[:, start : start + 128]
            out_ref[:, start : start + 128] = turn(head, t_ref[...], 1.0).astype(BF)
            out_ref[:, start + 128 : start + HD] = mixed[:, start + 128 : start + HD].astype(BF)

    block = lambda width_of: pl.BlockSpec((tile, width_of), lambda i, s: (i, 0))
    return call(
        body, (n // tile,),
        [block(width), pl.BlockSpec((1, cols), lambda i, s: (0, 0)), block(128)] + [ANY] * 4,
        block(cols), shape_of((n, cols), BF),
        [pltpu.VMEM(weight.shape, BF), pltpu.SemaphoreType.DMA],
        1, 2 * n * width * cols, 2 * n * width + 4 * n * cols, 18,
    )(info, rows, bias, table, *weight.arrays)


def project_values(info, rows, grads, weight, bias):
    n, width = rows.shape
    cols = weight.other
    tile = 512
    steps = n // tile // 2

    def body(info_ref, x_ref, g_ref, h_ref, b_ref, p0, p1, p2, p3, v_ref, d_ref, w, sem):
        step = pl.program_id(0)

        @pl.when(step == 0)
        def _():
            fetch(info_ref, (p0, p1, p2, p3), w, sem, weight.block)

        v_ref[...] = (dot_nn(x_ref[...], w[:, :HD]) + b_ref[...]).astype(BF)

        @pl.when(step < steps)
        def _():
            d_ref[...] = dot_nn(g_ref[...], w[:, HD:]).astype(BF)

        @pl.when(step >= steps)
        def _():
            d_ref[...] = dot_nn(h_ref[...], w[:, HD:]).astype(BF)

    block = lambda width_of: pl.BlockSpec((tile, width_of), lambda i, s: (i, 0))
    return call(
        body, (2 * steps,),
        [block(width)] + halves_specs(tile, width, steps)
        + [pl.BlockSpec((1, HD), lambda i, s: (0, 0))] + [ANY] * 4,
        [block(HD), block(HD)], [shape_of((n, HD), BF)] * 2,
        [pltpu.VMEM(weight.shape, BF), pltpu.SemaphoreType.DMA],
        1, 2 * n * width * cols, 4 * n * width + 2 * n * cols, 24,
    )(info, rows, *grads, bias, *weight.arrays)


def attend(mixed, value, dcontext, table, row_info, col_info):
    n, cols = mixed.shape
    share = n // 16
    lead = (2, 2, 2, MICRO, share)

    def body(q_ref, v_ref, d_ref, t_ref, r_ref, k_ref, ctx_ref, dm_ref, dv_ref, sum_ref):
        @pl.when(pl.program_id(0) == 0)
        def _():
            sum_ref[...] = jnp.zeros_like(sum_ref)

        load = lambda ref: ref[...].reshape(ROWS, ref.shape[-1])
        mixed = load(q_ref)
        query, key, value = mixed[:, :HD], mixed[:, HD:], load(v_ref)
        dctx = load(d_ref)
        angles = load(t_ref)
        allowed = (r_ref[0, :, 0:1] == k_ref[0, 0:1, :]) & (k_ref[0, 1:2, :] <= r_ref[0, :, 1:2])
        scores = jnp.where(allowed, dot_nt(query, key) * SCALE, -1e30)
        expos = jnp.exp(scores - jnp.max(scores, axis=-1, keepdims=True))
        soft = expos / jnp.sum(expos, axis=-1, keepdims=True)
        probs = soft.astype(BF)
        ctx_ref[...] = dot_nn(probs, value).astype(BF).reshape(ctx_ref.shape)
        dprobs = dot_nt(dctx, value)
        dscores = soft * (dprobs - jnp.sum(soft * dprobs, axis=-1, keepdims=True))
        dscores = dscores.astype(BF)
        dvalue = dot_tn(probs, dctx)
        dquery = dot_nn(dscores, key) * SCALE
        dkey = dot_tn(dscores, query) * SCALE
        pieces = []
        for part in (dquery, dkey):
            pieces += [turn(part[:, :128], angles, -1.0), part[:, 128:]]
        low = jnp.concatenate(pieces, axis=1).astype(BF)
        low_value = dvalue.astype(BF)
        dm_ref[...] = low.reshape(dm_ref.shape)
        dv_ref[...] = low_value.reshape(dv_ref.shape)
        sum_ref[:, : 2 * HD] += jnp.sum(low.astype(F32), axis=0, keepdims=True)
        sum_ref[:, 2 * HD :] += jnp.sum(low_value.astype(F32), axis=0, keepdims=True)

    view = lambda a: a.reshape(lead + (a.shape[-1],))
    block = lambda w: pl.BlockSpec(
        (2, 1, 2, 1, share, w), lambda p: (0, p % 2, 0, p // 2, 0, 0)
    )
    info = lambda a: pl.BlockSpec((1,) + a.shape[1:], lambda p: (p, 0, 0))
    packs = MICRO * 2
    context, dmixed, dvalue, sums = call(
        body, (packs,),
        [block(cols), block(HD), block(HD), block(128), info(row_info), info(col_info)],
        [block(HD), block(cols), block(HD), pl.BlockSpec((1, 3 * HD), lambda p: (0, 0))],
        [
            shape_of(lead + (HD,), BF), shape_of(lead + (cols,), BF),
            shape_of(lead + (HD,), BF), shape_of((1, 3 * HD), F32),
        ],
        [], 0, packs * 7 * 2 * ROWS * ROWS * HD, n * cols * 6, 60,
    )(
        view(mixed), view(value), view(dcontext), view(table), row_info, col_info
    )
    return context.reshape(n, HD), dmixed.reshape(n, cols), dvalue.reshape(n, HD), sums


def near_rows(info, near, got):
    rows, cols = near.shape
    half = rows // 2

    def body(info_ref, near_ref, got_ref, own_ref, give_ref):
        def part(k):
            start = pl.multiple_of((info_ref[9] ^ k) * half, half)
            got = got_ref[pl.ds(start, half), :].astype(F32)
            return jnp.where(info_ref[4] == 1, got, 0.0)

        own_ref[...] = near_ref[half:, :].astype(F32) + part(0)
        give_ref[...] = (near_ref[:half, :].astype(F32) + part(1)).astype(BF)

    whole = pl.BlockSpec((rows, cols), lambda i, s: (0, 0))
    out = pl.BlockSpec((half, cols), lambda i, s: (0, 0))
    return call(
        body, (1,), [whole, whole], [out, out],
        [shape_of((half, cols), F32), shape_of((half, cols), BF)],
        [], 1, rows * cols, rows * cols * 4, 14,
    )(info, near, got)


def own_rows(info, owns, gots):
    rows, cols = owns[0].shape
    half = rows // 2
    count = len(owns)

    def body(info_ref, *refs):
        own_refs, got_refs = refs[:count], refs[count : 2 * count]
        mine_ref, give_ref = refs[2 * count :]

        def part(k, i):
            start = pl.multiple_of((info_ref[10] ^ k) * half, half)
            at = pl.ds(start, half)
            return own_refs[i][at, :] + got_refs[i][at, :].astype(F32)

        for i in range(count):
            mine_ref[:, i * cols : (i + 1) * cols] = part(0, i)
            give_ref[:, i * cols : (i + 1) * cols] = part(1, i).astype(BF)

    whole = pl.BlockSpec((rows, cols), lambda i, s: (0, 0))
    out = pl.BlockSpec((half, count * cols), lambda i, s: (0, 0))
    return call(
        body, (1,), [whole] * (2 * count), [out, out],
        [shape_of((half, count * cols), F32), shape_of((half, count * cols), BF)],
        [], 1, rows * cols, count * rows * cols * 6, 16,
    )(info, *owns, *gots)


def place_columns(info, outs, pieces):
    flat = [array for mine, theirs, _ in pieces for array in (mine, theirs)]

    def body(info_ref, *refs):
        ins, out_refs = refs[: len(flat)], refs[len(flat) :]
        for i, (_, _, cuts) in enumerate(pieces):
            for side in (0, 1):
                ref = ins[2 * i + side]
                for first, count, out, offset, stride in cuts:
                    start = pl.multiple_of((info_ref[10] ^ side) * stride + offset, 128)
                    value = ref[:, first : first + count].astype(F32)
                    if outs[out][1]:
                        out_refs[out][pl.ds(start, count), :] = value.T
                    else:
                        out_refs[out][:, pl.ds(start, count)] = value

    return call(
        body, (1,),
        [pl.BlockSpec(array.shape, lambda i, s: (0, 0)) for array in flat],
        [pl.BlockSpec(shape, lambda i, s: (0, 0)) for shape, _ in outs],
        [shape_of(shape, F32) for shape, _ in outs],
        [], 1, 1000, 1000, 30,
    )(info, *flat)


def row_kernel(info, got, parts, weights, rows_in, whole_in, sums, finish, vmem):
    keep = len(got) > 0
    n = parts[0][0].shape[0] // 2
    width = weights[0].shape[0]
    tile = 256
    half_tile = n // 8
    steps = n // tile
    n_rows, n_whole = len(rows_in), len(whole_in)
    n_parts, n_weights = len(parts), len(weights)
    n_outs = 4 if keep else 2

    def body(info_ref, *refs):
        def pairs(count, refs):
            return [(refs[2 * i], refs[2 * i + 1]) for i in range(count)], refs[2 * count :]

        row_refs, refs = pairs(n_rows, refs)
        part_refs, refs = pairs(n_parts, refs)
        whole_refs, refs = refs[:n_whole], refs[n_whole:]
        got_refs, refs = refs[: len(got)], refs[len(got) :]
        w_refs, refs = refs[: 4 * n_weights], refs[4 * n_weights :]
        outs, refs = refs[:n_outs], refs[n_outs:]
        sum_refs, scratch, sem = refs[: len(sums)], refs[len(sums) : -1], refs[-1]
        step = pl.program_id(0)
        first = step == 0
        load = lambda pair: jnp.concatenate([pair[0][...], pair[1][...]])

        @pl.when(first)
        def _():
            for i, weight in enumerate(weights):
                fetch(info_ref, w_refs[4 * i : 4 * i + 4], scratch[i], sem, weight.block)

        def product(i):
            array, index, start = parts[i]
            return dot_nt(load(part_refs[i]), scratch[index][:, start : start + array.shape[1]])

        rows = [load(pair) for pair in row_refs]
        total = finish(first, rows, whole_refs, product, sum_refs)
        if keep:
            for k in range(4):

                @pl.when(step == k)
                def _(k=k):
                    outs[k][...] = (total + got_refs[k // 2][...].astype(F32)).astype(BF)

        else:
            for k in range(2):

                @pl.when(step // 2 == k)
                def _(k=k):
                    outs[k][...] = total.astype(BF)

    def row(w, local):
        base = 0 if keep or local else 8
        return [
            pl.BlockSpec((half_tile, w), lambda i, s: (base + s[11 + i], 0)),
            pl.BlockSpec((half_tile, w), lambda i, s: (base + s[15 + i], 0)),
        ]

    twice = lambda arrays: [array for array in arrays for _ in range(2)]
    ks = sum(part[0].shape[1] for part in parts)
    fixed = pl.BlockSpec((tile, width), lambda i, s: (0, 0))
    pair = [
        pl.BlockSpec((tile, width), lambda i, s: (jnp.minimum(i, 1), 0)),
        pl.BlockSpec((tile, width), lambda i, s: (jnp.maximum(i - 2, 0), 0)),
    ]
    if keep:
        out_specs, out_shape = [fixed] * 4, [shape_of((tile, width), BF)] * 4
    else:
        out_specs, out_shape = pair, [shape_of((2 * tile, width), BF)] * 2
    return call(
        body, (steps,),
        [spec for array in rows_in for spec in row(array.shape[1], True)]
        + [spec for part in parts for spec in row(part[0].shape[1], False)]
        + [pl.BlockSpec(array.shape, lambda i, s: (0, 0)) for array in whole_in]
        + pair[: len(got)] + [ANY] * (4 * n_weights),
        out_specs + [pl.BlockSpec(shape, lambda i, s: (0, 0)) for shape in sums],
        out_shape + [shape_of(shape, F32) for shape in sums],
        [pltpu.VMEM(weight.shape, BF) for weight in weights] + [pltpu.SemaphoreType.DMA],
        1, 2 * n * width * ks, 2 * n * (2 * width + ks), vmem,
    )(
        info, *twice(rows_in), *twice([part[0] for part in parts]), *whole_in, *got,
        *[array for weight in weights for array in weight.arrays],
    )


def out_rows(info, parts, weights, got):
    def finish(first, rows, whole, product, sums):
        total = product(0)
        for i in range(1, len(parts)):
            total += product(i)
        return total

    return row_kernel(info, got, parts, weights, [], [], [], finish, 60 if got else 60)


def back_rows(info, parts, weights, n_attn, x, vectors, got):
    def finish(first, rows, whole, product, sums):
        v_ref, sum_ref = whole[0], sums[0]

        @pl.when(first)
        def _():
            sum_ref[...] = jnp.zeros_like(sum_ref)

        plain, _ = plain_of(rows[-1].astype(F32))
        dattn = product(0)
        for i in range(1, n_attn):
            dattn += product(i)
        dmlp = product(n_attn)
        for i in range(n_attn + 1, len(parts)):
            dmlp += product(i)
        for i, grad in enumerate((dattn, dmlp)):
            sum_ref[2 * i : 2 * i + 1] += jnp.sum(grad * plain, axis=0, keepdims=True)
            sum_ref[2 * i + 1 : 2 * i + 2] += jnp.sum(grad, axis=0, keepdims=True)
        return dattn * v_ref[0:1] + dmlp * v_ref[2:3]

    return row_kernel(
        info, got, parts, weights, [x], [vectors], [(4, vectors.shape[1])], finish,
        60 if got else 60,
    )


class Names:

    def __init__(self, mark):
        self.mark = mark

    def __getattr__(self, name):
        return self.mark + name


RUN, WAIT = Names(""), Names("-")
ORDER = [
    RUN.vy, RUN.y01, RUN.xx, RUN.xc0, WAIT.vy, RUN.vz1, RUN.tab,
    WAIT.y01, RUN.a0, RUN.xy, WAIT.vz1, RUN.vz2, RUN.a1, WAIT.xx,
    RUN.xc1, RUN.xd1, WAIT.a0, RUN.b0, WAIT.vz2, RUN.y2, WAIT.xy,
    RUN.xc2, RUN.xd2, WAIT.a1, WAIT.b0, RUN.c0, RUN.b1, RUN.gx,
    WAIT.xc0, WAIT.xc1, WAIT.xc2, WAIT.xd1, WAIT.xd2, RUN.xc3, WAIT.y2,
    RUN.a2, RUN.gy, WAIT.xc3, RUN.xs, RUN.norm, WAIT.gx, RUN.gc1,
    RUN.y3, WAIT.c0, WAIT.b1, RUN.c1, RUN.feed0, WAIT.y3, RUN.a3,
    WAIT.a2, RUN.b2, WAIT.gy, RUN.gc2, RUN.gd1, RUN.gd2, RUN.gc0,
    WAIT.c1, WAIT.gd1, WAIT.gd2, RUN.gc3, RUN.y45, WAIT.b2, WAIT.a3,
    RUN.b3, WAIT.gc0, WAIT.gc1, WAIT.gc2, WAIT.gc3, RUN.gs, RUN.go0,
    RUN.c2r0, WAIT.y45, RUN.a4, RUN.fb0, RUN.gi0, WAIT.b3, RUN.c3r1,
    WAIT.c2r0, RUN.p0, RUN.heads, WAIT.c3r1, RUN.val, WAIT.p0, RUN.q0,
    WAIT.a4, RUN.b4, RUN.a5, RUN.att, WAIT.q0, RUN.gqk, WAIT.b4,
    RUN.c4r2, RUN.p1, WAIT.a5, RUN.b5, RUN.gvp, WAIT.b5, RUN.c5r3,
    WAIT.c4r2, RUN.p2, RUN.feed1, RUN.go1, RUN.r4, WAIT.p1, RUN.q1,
    WAIT.c5r3, RUN.p3, RUN.fb1, RUN.gi1, RUN.og, RUN.oc, WAIT.q1,
    RUN.f01, WAIT.p2, RUN.q2, RUN.r5, RUN.bg, RUN.hc, WAIT.r4,
    RUN.p4, WAIT.oc, RUN.ok, WAIT.p3, RUN.q3, RUN.o1y, RUN.o1x,
    WAIT.hc, WAIT.f01, WAIT.r5, RUN.p5, RUN.bk, RUN.h1y, RUN.h1x,
    WAIT.p4, RUN.q4, WAIT.p5, RUN.q5, WAIT.o1y, WAIT.o1x, RUN.o2x,
    RUN.o2y, WAIT.q2, WAIT.q3, RUN.f23, RUN.vs, RUN.vc, WAIT.vc,
    RUN.vx, WAIT.h1y, WAIT.h1x, RUN.h2x, RUN.h2y, WAIT.q4, WAIT.q5,
    RUN.f45, WAIT.vx, RUN.vyy, WAIT.o2x, WAIT.o2y, RUN.fo, WAIT.vyy,
    RUN.vz, WAIT.f23, WAIT.h2x, WAIT.h2y, RUN.fr, WAIT.vz, RUN.fv,
    WAIT.f45, RUN.fw,
]


def layer_program(n_dp, n_tensor):
    n_z = n_dp // 2
    n_dev = n_dp * n_tensor
    core, xbit, ybit, zbit = 1, 2, 4, 8
    ids = range(n_dev)
    flip = lambda bit: [(i, i ^ bit) for i in ids]
    flip_c, flip_x, flip_y, flip_z = flip(core), flip(xbit), flip(ybit), flip(zbit)
    mirror = {0: 0, 1: 2, 2: 1, 3: 3}
    mid = [
        (i, mirror[i // zbit] * zbit + (i % zbit if i // zbit in (1, 2) else i % zbit ^ core))
        for i in ids if n_z == 4
    ]
    columns = [[z * 2 + y for z in range(n_z)] for y in range(2)]

    def per_device(
        tokens, lengths, out_grad, attn_gain, attn_shift, mlp_gain, mlp_shift,
        w_qkv, b_qkv, w_proj, b_proj, w_in, b_in, w_out, b_out,
    ):
        dp = lax.axis_index("dp")
        tensor = lax.axis_index("tensor")
        z, y = dp // 2, dp % 2
        x, c = tensor // 2, tensor % 2
        share = tokens.shape[1]
        width = tokens.shape[2]
        upper = z >= 2
        even = z % 2 == 0
        token = []
        is_mid = (z == 1) | (z == 2)

        def turn_of(*values):
            out = lax.optimization_barrier(values + tuple(token))[: len(values)] if token else values
            return out if len(out) > 1 else out[0]

        def passed(*values):
            token.extend(values)

        def worked(*values):
            token[:] = values

        if n_z == 4:
            far = jnp.where(upper, 1, 2)
            low_far = jnp.where(upper, 0, 2)
            places_z = [z, z ^ 1, far, far ^ 1, is_mid, low_far, low_far + 1, z ^ 1, z]
        else:
            places_z = [0, 1, 2, 3, 1, 0, 1, 2, 3]
        info = jnp.stack(
            [jnp.asarray(v, jnp.int32) for v in places_z + [z % 2, y, 4, 3, 0, 1, 6, 7, 2, 5]]
        )

        h_cols = w_in.shape[1] // 2
        half_h = h_cols // 2
        q_cols = w_qkv.shape[1] // 2
        p_cols = w_proj.shape[0] // 2

        w_out_t, w_proj_t = w_out.T, w_proj.T
        cuts = [
            [(w_in, h_cols, 0, half_h)],
            [(w_out_t, h_cols, 0, half_h)],
            [(w_qkv, q_cols, 0, 2 * HD)],
            [(w_qkv, q_cols, 2 * HD, HD), (w_proj_t, p_cols, 0, p_cols)],
            [(w_in, h_cols, half_h, half_h)],
            [(w_out_t, h_cols, half_h, half_h)],
        ]
        V = {}

        def side_of(k, side):
            parts = [
                lax.dynamic_slice_in_dim(weight, side * sub + start, count, 1)
                for weight, sub, start, count in cuts[k]
            ]
            return parts[0] if len(parts) == 1 else jnp.concatenate(parts, axis=1)

        def send_y(name, chunks):
            theirs = jnp.concatenate([side_of(k, 1 - y) for k in chunks], axis=1)
            V[name] = swap(turn_of(theirs), flip_y)
            start = 0
            for k in chunks:
                mine = side_of(k, y)
                V[RUN.source, k] = (name, mine, start)
                start += mine.shape[1]

        def step_a(k):
            name, mine, start = V[RUN.source, k]
            got = turn_of(V[name])
            pair = ordered(y == 0, mine, got[:, start : start + mine.shape[1]])
            V[RUN.pair, k] = pair
            V["a%d" % k] = swap(pair, flip_z) if n_z == 4 else pair

        def step_b(k):
            both = jnp.concatenate(turn_of(V[RUN.pair, k], V["a%d" % k]))
            V["b%d" % k] = swap(both, mid) if n_z == 4 else both

        def cross(k, j, name):
            if n_z == 4:
                if j is None:
                    payload = turn_of(V["b%d" % k])
                elif k is None:
                    payload = turn_of(V[RUN.sum, j][0])
                else:
                    payload = jnp.where(is_mid, *turn_of(V["b%d" % k], V[RUN.sum, j][0]))
                got = swap(payload, flip_z)
            else:
                got = turn_of(V["b%d" % k] if j is None else V[RUN.sum, j][0])
            V[name] = got
            if k is not None:
                V[RUN.arrived, k] = name
            if j is not None:
                V[RUN.crossed, j] = name

        def full(k):
            if n_z == 4:
                arrays = (
                    V[RUN.pair, k], V["a%d" % k], V["b%d" % k], V[V[RUN.arrived, k]]
                )
            else:
                whole = lax.all_gather(
                    V[RUN.pair, k], "dp", axis_index_groups=columns, tiled=True
                )
                quarter = jnp.split(whole, 4)
                half = jnp.concatenate(quarter[2:])
                arrays = (quarter[0], quarter[1], half, half)
            return Gathered(arrays)

        def step_p(j):
            far, got = turn_of(V[RUN.sum, j][0], V[V[RUN.crossed, j]])
            far = (far.astype(F32) + got.astype(F32)).astype(BF)
            V["p%d" % j] = swap(far, mid) if n_z == 4 else far

        def step_q(j):
            near, got = turn_of(V[RUN.sum, j][1], V["p%d" % j])
            if n_z == 4:
                V[RUN.own, j], give = near_rows(info, near, got)
                V["q%d" % j] = swap(give, flip_z)
            else:
                own = lax.psum_scatter(
                    jnp.concatenate([V[RUN.sum, j][0], near]), "dp", scatter_dimension=0,
                    axis_index_groups=columns, tiled=True,
                ).astype(F32)
                V[RUN.own, j], V["q%d" % j] = own, jnp.zeros_like(own, BF)

        def step_f(a, b, name):
            values = turn_of(V[RUN.own, a], V[RUN.own, b], V["q%d" % a], V["q%d" % b])
            V[RUN.mine, name], give = own_rows(info, values[:2], values[2:])
            V[name] = swap(give, flip_y)

        def plane_core(name, k, own):
            g = name[0]
            part = own if k == 0 else V[g + "xy"[k - 1]] if k < 3 else None
            if k == 3:
                part = jnp.concatenate(turn_of(V[g + "d1"], V[g + "d2"]))
            else:
                part = turn_of(part)
            V[g + "part", k] = part.reshape(-1, width)
            V[name] = swap(V[g + "part", k], flip_c)

        def plane_rows(g):
            parts = [V[g + "part", k] for k in range(4)] + [V["%sc%d" % (g, k)] for k in range(4)]
            V[g + "mine"], V[g + "c"] = stack_rows(turn_of(*parts))
            worked(V[g + "mine"])

        def send_core(name, parts):
            V[name] = tuple(swap(part, flip_c) for part in turn_of(*parts))

        def sum_first(g, name, perm, at):
            value = turn_of(V[g + "keep"][at]).reshape(2, share, width)
            V[g + name] = swap(value, perm)

        def sum_second(g, name, perm, at):
            got = turn_of(V[g + ("1y", "1x")[at]])
            total = V[g + "keep"][2 + at].reshape(2, share, width).astype(F32) + got.astype(F32)
            V[g + "left", at] = total[0]
            V[g + name] = swap(total[1].astype(BF), perm)

        def sum_result(g):
            got = turn_of(V[g + "2x"], V[g + "2y"])
            return jnp.stack([V[g + "left", at] + got[at].astype(F32) for at in (0, 1)])

        own_places = tensor * share + jnp.arange(share, dtype=jnp.int32)
        own_ends = jnp.cumsum(lengths[:, 0], axis=-1)
        own_segment = jnp.sum((own_places[:, None] >= own_ends[:, None, :]).astype(jnp.int32), axis=-1)
        valid = (own_segment < SEGS - 1).astype(F32)[..., None]
        x_own = tokens.astype(F32)
        g_own = out_grad.astype(F32) * valid
        g_low = g_own.astype(BF).reshape(MICRO, share, width)
        x_low = tokens.reshape(MICRO, share, width)
        bias_in = lax.dynamic_slice_in_dim(b_in, y * h_cols, h_cols).astype(F32)[None]
        bias_qkv = lax.dynamic_slice_in_dim(b_qkv, y * q_cols, q_cols).astype(F32)[None]
        pair_bits = jnp.arange(2, dtype=jnp.int32)
        t_of = (x ^ pair_bits)[None, :] * 2 + (c ^ pair_bits)[:, None]
        places = (t_of[..., None] * share + jnp.arange(share, dtype=jnp.int32)).reshape(-1)

        def send_vectors():
            vectors = jnp.stack([attn_gain, attn_shift, mlp_gain, mlp_shift, b_proj, b_out])
            V[RUN.vectors] = vectors
            V[RUN.vy] = swap(turn_of(vectors), flip_y)
            V[RUN.lengths] = swap(turn_of(lengths[:, 0]), flip_y)

        def send_vectors_z(name, bit, low_first):
            if name == "vz1":
                pair = ordered(y == 0, V[RUN.vectors][None], turn_of(V[RUN.vy])[None])
                if n_z != 4:
                    V[RUN.vz1] = V[RUN.vz2] = pair
                    V[RUN.small] = lax.all_gather(
                        pair, "dp", axis_index_groups=columns, tiled=True
                    )
                    return
            elif n_z != 4:
                return
            else:
                pair = ordered(even, V[RUN.vectors_y], turn_of(V[RUN.vz1]))
            V["vectors_y" if name == "vz1" else "vectors_z"] = pair
            V[name] = swap(pair, flip(bit))

        def send_part(name, value, perm, index=None):
            def run():
                part = turn_of(value if index is None else V[value])
                V[name] = swap(part if index is None else part[index], perm)

            return run

        def send_sums_c():
            V[RUN.vc] = swap_half("total", 3, c, flip_c, "vc")

        def swap_half(source, axis, bit, perm, name):
            total = turn_of(V[source])
            low, high = jnp.split(total, 2, axis=axis)
            got = swap(jnp.where(bit == 0, high, low), perm)
            V["half " + name] = jnp.where(bit == 0, low, high)
            return got

        def send_sums_x():
            V["total x"] = V["half vc"] + turn_of(V[RUN.vc])
            V[RUN.vx] = swap_half("total x", 2, x, flip_x, "vx")

        def send_sums_y():
            V["total y"] = V["half vx"] + turn_of(V[RUN.vx])
            V[RUN.vyy] = swap_half("total y", 1, y, flip_y, "vyy")

        def send_sums_z():
            total = (V["half vyy"] + turn_of(V[RUN.vyy])).reshape(n_z, -1)
            if n_z == 4:
                row = lambda k: lax.dynamic_slice_in_dim(total, z ^ k, 1, 0)
                V[RUN.row] = row(0)
                V[RUN.vz] = tuple(swap(row(k), flip(zbit * k)) for k in (1, 2, 3))
            else:
                V[RUN.row] = lax.psum_scatter(
                    total.reshape(-1), "dp", axis_index_groups=columns, tiled=True
                )
                V[RUN.vz] = ()

        def norm():
            if n_z == 4:
                small = ordered(~upper, V[RUN.vectors_z], turn_of(V[RUN.vz2]))
            else:
                small = V[RUN.small]
            small = small.transpose(1, 0, 2).reshape(6, width).astype(F32)
            V[RUN.small] = jnp.concatenate([small, jnp.zeros((2, width), F32)])
            V[RUN.attn], V[RUN.mlp] = norm_rows(turn_of(V[RUN.xmine]), V[RUN.xc], V[RUN.small])
            worked(V[RUN.attn])

        def tab():
            lengths_all = jnp.stack([lengths[:, 0], turn_of(V[RUN.lengths])])
            ends = jnp.cumsum(lengths_all, axis=-1)
            gone = (places[:, None] >= ends[..., None, :]).astype(jnp.int32)
            segment = jnp.sum(gone, axis=-1)
            position = places - jnp.sum(gone * lengths_all[..., None, :], axis=-1)
            row_position = position.reshape(2, MICRO, 2, 2, share).transpose(2, 0, 3, 1, 4)
            lanes = jnp.arange(2 * ROT)
            frequency = 10000.0 ** (-2.0 * (lanes % (ROT // 2)).astype(F32) / ROT)
            angle = row_position.reshape(-1).astype(F32)[:, None] * frequency
            table = jnp.where(lanes < ROT, jnp.cos(angle), jnp.sin(angle))
            pack_segment = segment.transpose(1, 0, 2).reshape(MICRO * 2, ROWS)
            pack_places = jnp.broadcast_to(places, (MICRO * 2, ROWS))
            row_info = jnp.stack([pack_segment, pack_places], axis=2)
            col_info = jnp.stack([pack_segment, pack_places], axis=1)
            V[RUN.table] = lax.optimization_barrier((table, row_info, col_info))
            worked(*V[RUN.table])

        def run_feed(i, k):
            bias = bias_in[:, i * half_h : (i + 1) * half_h]
            V[RUN.active, i], V[RUN.slope, i] = feed(info, turn_of(V[RUN.mlp]), full(k), bias)
            worked(V[RUN.active, i])

        def sums_of(j, *groups):
            V[RUN.sum, j] = weight_grad(info, list(groups))
            worked(V[RUN.sum, j][0])

        def halves_of(value):
            rows = turn_of(V[RUN.gmine]), V[RUN.gc]
            return [(rows[0], value, 0), (rows[1], value, 1)]

        def run_back(i, k):
            rows = turn_of(V[RUN.gmine]), V[RUN.gc]
            V[RUN.dhidden, i], V[RUN.dsum, i] = feed_back(info, rows, full(k), V[RUN.slope, i])
            worked(V[RUN.dhidden, i])

        def heads():
            V[RUN.mixed] = project_heads(
                info, turn_of(V[RUN.attn]), full(2), bias_qkv[:, : 2 * HD], V[RUN.table][0]
            )
            worked(V[RUN.mixed])

        def val():
            V[RUN.value], V[RUN.dcontext] = project_values(
                info, turn_of(V[RUN.attn]), (V[RUN.gmine], V[RUN.gc]), full(3), bias_qkv[:, 2 * HD :]
            )
            worked(V[RUN.value])

        def att():
            V[RUN.context], V[RUN.dmixed], V[RUN.dvalue], V["dmixed sum"] = attend(
                turn_of(V[RUN.mixed]), V[RUN.value], V[RUN.dcontext], *V[RUN.table]
            )
            worked(V[RUN.context])

        def run_out(keep):
            parts = [(turn_of(V[RUN.context]), 0, HD), (V[RUN.active, 0], 1, 0), (V[RUN.active, 1], 2, 0)]
            got = turn_of(*V[RUN.oc]) if keep else ()
            outs = out_rows(info, parts, (full(3), full(1), full(5)), got)
            V["okeep" if keep else "ogive"] = outs
            worked(outs[0])

        def run_rows(keep):
            parts = [
                (turn_of(V[RUN.dmixed]), 0, 0), (V[RUN.dvalue], 1, 0),
                (V[RUN.dhidden, 0], 2, 0), (V[RUN.dhidden, 1], 3, 0),
            ]
            got = turn_of(*V[RUN.hc]) if keep else ()
            outs = back_rows(
                info, parts, (full(2), full(3), full(0), full(4)), 2,
                V[RUN.xmine] if keep else V[RUN.xc], V[RUN.small], got,
            )
            V["hkeep" if keep else "hgive"] = outs[:-1]
            V[RUN.sums, keep] = outs[-1]
            worked(outs[0])

        def vector_total():
            g_sum = jnp.sum(turn_of(g_own), axis=(0, 1))[None]
            sums = jnp.concatenate([turn_of(V[RUN.sums, True]) + V[RUN.sums, False], g_sum])
            sums = sums.reshape(5, n_dev, -1).transpose(1, 0, 2).reshape(n_dev, -1)
            dhidden_sum = jnp.concatenate([V[RUN.dsum, 0], V[RUN.dsum, 1]], axis=1)
            bias_sums = jnp.concatenate(
                [
                    dhidden_sum.reshape(n_dp // 2, -1),
                    V["dmixed sum"].reshape(n_dp // 2, -1),
                ],
                axis=-1,
            )
            spread_bias = jnp.zeros((n_dp, n_tensor, bias_sums.shape[-1]), F32)
            spread_bias = lax.dynamic_update_slice(
                spread_bias, bias_sums[:, None], (y * (n_dp // 2), tensor, 0)
            ).reshape(n_dev, -1)
            total = jnp.concatenate([sums, spread_bias], axis=-1)
            V[RUN.total] = total.reshape(n_z, 2, 2, 2, -1)
            worked(V[RUN.total])

        def result_output():
            small = V[RUN.small]
            V[RUN.output] = (x_own + sum_result("o") + small[4] + small[5]).astype(BF)
            worked(V[RUN.output])

        def result_tokens():
            back = sum_result("h")
            own_plain, own_spread = plain_of(x_own)
            V["grad tokens"] = g_own + own_spread * (
                back
                - jnp.mean(back, axis=-1, keepdims=True)
                - own_plain * jnp.mean(back * own_plain, axis=-1, keepdims=True)
            )
            worked(V["grad tokens"])

        def result_weights():
            rest = half_h
            V[RUN.weights] = place_columns(
                info,
                [
                    (w_qkv.shape, False), (w_proj.shape, True),
                    (w_in.shape, False), (w_out.shape, True),
                ],
                [
                    (V[RUN.mine, "f01"], turn_of(V[RUN.f01]),
                     [(0, rest, 3, 0, h_cols), (rest, rest, 2, 0, h_cols)]),
                    (V[RUN.mine, "f23"], turn_of(V[RUN.f23]),
                     [(0, 2 * HD, 0, 0, q_cols), (2 * HD, HD, 0, 2 * HD, q_cols),
                      (3 * HD, p_cols, 1, 0, p_cols)]),
                    (V[RUN.mine, "f45"], turn_of(V[RUN.f45]),
                     [(0, rest, 3, half_h, h_cols), (rest, rest, 2, half_h, h_cols)]),
                ],
            )
            worked(V[RUN.weights][0])

        def result_vectors():
            total = V[RUN.row]
            for got in V[RUN.vz]:
                total = total + turn_of(got)
            V["vector sums"] = total.reshape(-1)

        steps = dict(
            y01=lambda: send_y("y01", (0, 1)),
            y2=lambda: send_y("y2", (2,)),
            y3=lambda: send_y("y3", (3,)),
            y45=lambda: send_y("y45", (4, 5)),
            vy=send_vectors,
            vz1=lambda: send_vectors_z("vz1", zbit, even),
            vz2=lambda: send_vectors_z("vz2", 2 * zbit, ~upper),
            xx=send_part("xx", x_low, flip_x),
            xy=send_part("xy", x_low, flip_y),
            xd1=send_part("xd1", "xx", flip_y, 0),
            xd2=send_part("xd2", "xy", flip_x, 1),
            xs=lambda: plane_rows("x"),
            gx=send_part("gx", g_low, flip_x),
            gy=send_part("gy", g_low, flip_y),
            gd1=send_part("gd1", "gx", flip_y, 0),
            gd2=send_part("gd2", "gy", flip_x, 1),
            gs=lambda: plane_rows("g"),
            norm=norm, tab=tab, heads=heads, val=val, att=att,
            feed0=lambda: run_feed(0, 0),
            feed1=lambda: run_feed(1, 4),
            fb0=lambda: run_back(0, 1),
            fb1=lambda: run_back(1, 5),
            go0=lambda: sums_of(0, halves_of(V[RUN.active, 0])),
            gi0=lambda: sums_of(1, [(turn_of(V[RUN.mlp]), V[RUN.dhidden, 0], 0)]),
            gqk=lambda: sums_of(2, [(turn_of(V[RUN.attn]), V[RUN.dmixed], 0)]),
            gvp=lambda: sums_of(
                3, [(turn_of(V[RUN.attn]), V[RUN.dvalue], 0)], halves_of(V[RUN.context])
            ),
            go1=lambda: sums_of(4, halves_of(V[RUN.active, 1])),
            gi1=lambda: sums_of(5, [(turn_of(V[RUN.mlp]), V[RUN.dhidden, 1], 0)]),
            og=lambda: run_out(False), ok=lambda: run_out(True),
            bg=lambda: run_rows(False), bk=lambda: run_rows(True),
            f01=lambda: step_f(0, 1, "f01"),
            f23=lambda: step_f(2, 3, "f23"),
            f45=lambda: step_f(4, 5, "f45"),
            vs=vector_total, vc=send_sums_c, vx=send_sums_x,
            vyy=send_sums_y, vz=send_sums_z, fv=result_vectors,
            fo=result_output, fr=result_tokens, fw=result_weights,
        )
        for g in "oh":
            steps[g + "c"] = lambda g=g: send_core(g + "c", V[g + "give"])
            steps[g + "1y"] = lambda g=g: sum_first(g, "1y", flip_y, 0)
            steps[g + "1x"] = lambda g=g: sum_first(g, "1x", flip_x, 1)
            steps[g + "2x"] = lambda g=g: sum_second(g, "2x", flip_x, 0)
            steps[g + "2y"] = lambda g=g: sum_second(g, "2y", flip_y, 1)
        for k in range(4):
            steps["xc%d" % k] = lambda k=k: plane_core("xc%d" % k, k, x_low)
            steps["gc%d" % k] = lambda k=k: plane_core("gc%d" % k, k, g_low)
        for k in range(6):
            steps["a%d" % k] = lambda k=k: step_a(k)
            steps["b%d" % k] = lambda k=k: step_b(k)
            steps["c%d" % k] = lambda k=k: cross(k, None, "c%d" % k)
            steps["r%d" % k] = lambda k=k: cross(None, k, "r%d" % k)
            steps["p%d" % k] = lambda k=k: step_p(k)
            steps["q%d" % k] = lambda k=k: step_q(k)
            for j in range(6):
                name = "c%dr%d" % (k, j)
                steps[name] = lambda k=k, j=j, name=name: cross(k, j, name)
        for word in ORDER:
            if word[0] == "-":
                value = V[word[1:]]
                extra = (V[RUN.lengths],) if word == "-vy" else ()
                passed(*(value if isinstance(value, tuple) else (value,)), *extra)
            else:
                steps[word]()

        piece = width // n_dev
        sums = V["vector sums"]
        pieces = [sums[k * piece : (k + 1) * piece] for k in range(5)]
        bias_piece = sums[5 * piece :]
        in_piece = b_in.shape[0] // n_dp
        grad_qkv, grad_proj, grad_in, grad_out = V[RUN.weights]
        return (
            V[RUN.output], V["grad tokens"], pieces[0], pieces[1], pieces[2], pieces[3],
            grad_qkv, bias_piece[in_piece:].reshape(1, -1), grad_proj, pieces[4],
            grad_in, bias_piece[:in_piece].reshape(1, -1), grad_out, pieces[4],
        )

    return per_device


def solution(mesh):
    n_dp, n_tensor = mesh.shape["dp"], mesh.shape["tensor"]
    rows = P(None, AXES, None)
    in_specs = (
        rows, P(None, "dp", None), rows, P("dp"), P("dp"), P("dp"), P("dp"),
        P("dp", "tensor"), P("tensor"), P("tensor", "dp"), P("dp"),
        P("dp", "tensor"), P("tensor"), P("tensor", "dp"), P("dp"),
    )
    vector = P(AXES)
    out_specs = (
        rows, rows, vector, vector, vector, vector,
        P("dp", "tensor"), P("tensor", "dp"), P("tensor", "dp"), vector,
        P("dp", "tensor"), P("tensor", "dp"), P("tensor", "dp"), vector,
    )
    return jax.shard_map(
        layer_program(n_dp, n_tensor), mesh=mesh,
        in_specs=in_specs, out_specs=out_specs, check_vma=False,
    )
```

```python
import jax
import jax.numpy as jnp
from jax import lax
from jax.experimental import pallas as pl
from jax.experimental.pallas import tpu as pltpu
from jax.sharding import PartitionSpec as P

HD = 256
ROT = 64
MICRO = 2
ROWS = 512
SEGS = 8
AXES = ("dp", "tensor")
BF = jnp.bfloat16
F32 = jnp.float32
MIB = 1 << 20
SCALE = HD ** (-0.5)
ANY = pl.BlockSpec(memory_space=pl.ANY)


def swap(value, perm):
    return lax.ppermute(value, AXES, perm)


def dot_nn(a, b):
    return jnp.dot(a, b, preferred_element_type=F32)


def dot_nt(a, b):
    return lax.dot_general(a, b, (((1,), (1,)), ((), ())), preferred_element_type=F32)


def dot_tn(a, b):
    return lax.dot_general(a, b, (((0,), (0,)), ((), ())), preferred_element_type=F32)


def ordered(first, low, high, axis=0):
    return jnp.where(
        first,
        jnp.concatenate([low, high], axis=axis),
        jnp.concatenate([high, low], axis=axis),
    )


def shape_of(shape, dtype):
    return jax.ShapeDtypeStruct(shape, dtype)


def call(body, grid, in_specs, out_specs, out_shape, scratch, prefetch, flops, nbytes, vmem):
    return pl.pallas_call(
        body,
        out_shape=out_shape,
        grid_spec=pltpu.PrefetchScalarGridSpec(
            num_scalar_prefetch=prefetch,
            grid=grid,
            in_specs=in_specs,
            out_specs=out_specs,
            scratch_shapes=scratch,
        ),
        compiler_params=pltpu.CompilerParams(
            dimension_semantics=("arbitrary",) * len(grid), vmem_limit_bytes=vmem * MIB
        ),
        cost_estimate=pl.CostEstimate(
            flops=int(flops) * 7 // 10, bytes_accessed=0, transcendentals=0
        ),
    )


class Gathered:
    def __init__(self, arrays):
        self.arrays = arrays
        self.block, self.other = arrays[0].shape
        self.shape = (4 * self.block, self.other)


def fetch(info, refs, scratch, sem, block):
    def part(ref, index, place):
        source = ref.at[pl.ds(index * block, block), :]
        target = scratch.at[pl.ds(pl.multiple_of(place * block, block), block), :]
        return pltpu.make_async_copy(source, target, sem)

    own, partner, far_mid, far_out = refs
    part(own, 0, info[0]).start()
    part(partner, 0, info[1]).start()

    @pl.when(info[4] == 1)
    def _():
        part(far_mid, 0, info[2]).start()
        part(far_mid, 1, info[3]).start()

    @pl.when(info[4] == 0)
    def _():
        part(far_out, 0, info[2]).start()
        part(far_out, 1, info[3]).start()

    part(own, 0, info[0]).wait()
    part(partner, 0, info[1]).wait()
    part(far_out, 0, info[2]).wait()
    part(far_out, 1, info[3]).wait()


def plain_of(rows):
    center = rows - jnp.mean(rows, axis=-1, keepdims=True)
    spread = lax.rsqrt(jnp.mean(center * center, axis=-1, keepdims=True) + 1e-05)
    return center * spread, spread


def norm_rows(mine, sibling, vectors):
    n, width = mine.shape
    tile = 256
    steps = n // tile

    def body(x_ref, y_ref, v_ref, a_ref, m_ref):
        def write(rows):
            plain, _ = plain_of(rows.astype(F32))
            a_ref[...] = (plain * v_ref[0:1] + v_ref[1:2]).astype(BF)
            m_ref[...] = (plain * v_ref[2:3] + v_ref[3:4]).astype(BF)

        @pl.when(pl.program_id(0) < steps)
        def _():
            write(x_ref[...])

        @pl.when(pl.program_id(0) >= steps)
        def _():
            write(y_ref[...])

    rows = pl.BlockSpec((tile, width), lambda i: (i, 0))
    return call(
        body, (2 * steps,),
        [
            pl.BlockSpec((tile, width), lambda i: (jnp.minimum(i, steps - 1), 0)),
            pl.BlockSpec((tile, width), lambda i: (jnp.maximum(i - steps, 0), 0)),
            pl.BlockSpec(vectors.shape, lambda i: (0, 0)),
        ],
        [rows, rows],
        [shape_of((2 * n, width), BF)] * 2, [], 0, 2 * n * width * 600, 2 * n * width * 6, 16,
    )(mine, sibling, vectors)


def stack_rows(parts):
    rows, width = parts[0].shape
    half = len(parts) // 2

    def body(*refs):
        ins, outs, sem = refs[: 2 * half], refs[2 * half : -1], refs[-1]
        copies = [
            pltpu.make_async_copy(
                ins[k], outs[k // half].at[pl.ds((k % half) * rows, rows), :], sem.at[k]
            )
            for k in range(2 * half)
        ]
        for copy in copies:
            copy.start()
        for copy in copies:
            copy.wait()

    return call(
        body, (1,), [ANY] * (2 * half), [ANY] * 2, [shape_of((half * rows, width), BF)] * 2,
        [pltpu.SemaphoreType.DMA((2 * half,))], 0, 1000, 1000, 4,
    )(*parts)


def feed(info, rows, weight, bias):
    n, width = rows.shape
    cols = weight.other
    tile = 512

    def body(info_ref, x_ref, b_ref, p0, p1, p2, p3, active_ref, slope_ref, w, sem):
        @pl.when(pl.program_id(0) == 0)
        def _():
            fetch(info_ref, (p0, p1, p2, p3), w, sem, weight.block)

        hidden = dot_nn(x_ref[...], w[...]) + b_ref[...]
        cdf = 0.5 * (1.0 + lax.erf(hidden * 0.7071067811865476))
        active_ref[...] = (hidden * cdf).astype(BF)
        density = jnp.exp(-0.5 * hidden * hidden) * 0.3989422804014327
        slope_ref[...] = (cdf + hidden * density).astype(BF)

    out = pl.BlockSpec((tile, cols), lambda i, s: (i, 0))
    return call(
        body, (n // tile,),
        [
            pl.BlockSpec((tile, width), lambda i, s: (i, 0)),
            pl.BlockSpec((1, cols), lambda i, s: (0, 0)),
        ] + [ANY] * 4,
        [out, out],
        [shape_of((n, cols), BF), shape_of((n, cols), BF)],
        [pltpu.VMEM(weight.shape, BF), pltpu.SemaphoreType.DMA],
        1, 2 * n * width * cols, 2 * n * width + 6 * n * cols, 18,
    )(info, rows, bias, *weight.arrays)


def halves_specs(tile, width, steps):
    return [
        pl.BlockSpec((tile, width), lambda i, s: (jnp.minimum(i, steps - 1), 0)),
        pl.BlockSpec((tile, width), lambda i, s: (jnp.maximum(i - steps, 0), 0)),
    ]


def feed_back(info, rows, weight, slope):
    n, width = rows[0].shape
    cols = weight.other
    tile = 512
    steps = n // tile

    def body(info_ref, g_ref, h_ref, s_ref, p0, p1, p2, p3, out_ref, sum_ref, w, sem):
        step = pl.program_id(0)

        @pl.when(step == 0)
        def _():
            fetch(info_ref, (p0, p1, p2, p3), w, sem, weight.block)
            sum_ref[...] = jnp.zeros_like(sum_ref)

        def write(ref):
            low = (dot_nn(ref[...], w[...]) * s_ref[...].astype(F32)).astype(BF)
            out_ref[...] = low
            sum_ref[...] += jnp.sum(low.astype(F32), axis=0, keepdims=True)

        @pl.when(step < steps)
        def _():
            write(g_ref)

        @pl.when(step >= steps)
        def _():
            write(h_ref)

    block = lambda width_of: pl.BlockSpec((tile, width_of), lambda i, s: (i, 0))
    return call(
        body, (2 * steps,), halves_specs(tile, width, steps) + [block(cols)] + [ANY] * 4,
        [block(cols), pl.BlockSpec((1, cols), lambda i, s: (0, 0))],
        [shape_of((2 * n, cols), BF), shape_of((1, cols), F32)],
        [pltpu.VMEM(weight.shape, BF), pltpu.SemaphoreType.DMA],
        1, 4 * n * width * cols, 4 * n * width + 12 * n * cols, 20,
    )(info, *rows, slope, *weight.arrays)


def weight_grad(info, groups):
    flat = [pair for group in groups for pair in group]
    width = flat[0][0].shape[1]
    tile = width // 4
    counts = [group[0][1].shape[1] for group in groups]
    cols = sum(counts)

    def body(info_ref, *refs):
        lefts, rights = refs[: len(flat)], refs[len(flat) : 2 * len(flat)]
        far_ref, near_ref = refs[2 * len(flat) :]

        def write(out_ref):
            at, start = 0, 0
            for group, count in zip(groups, counts):
                total = dot_tn(lefts[at][...], rights[at][...])
                for k in range(1, len(group)):
                    total += dot_tn(lefts[at + k][...], rights[at + k][...])
                out_ref[:, start : start + count] = total.astype(BF)
                at, start = at + len(group), start + count

        @pl.when(pl.program_id(0) < 2)
        def _():
            write(far_ref)

        @pl.when(pl.program_id(0) >= 2)
        def _():
            write(near_ref)

    return call(
        body, (4,),
        [pl.BlockSpec((left.shape[0], tile), lambda i, s: (0, s[5 + i])) for left, _, _ in flat]
        + [
            pl.BlockSpec((left.shape[0], right.shape[1]), lambda i, s, k=k: (k, 0))
            for left, right, k in flat
        ],
        [
            pl.BlockSpec((tile, cols), lambda i, s: (jnp.minimum(i, 1), 0)),
            pl.BlockSpec((tile, cols), lambda i, s: (jnp.maximum(i - 2, 0), 0)),
        ],
        [shape_of((width // 2, cols), BF)] * 2,
        [], 1, sum(2 * width * left.shape[0] * right.shape[1] for left, right, _ in flat),
        sum(2 * left.shape[0] * (width + right.shape[1]) for left, right, _ in flat), 24,
    )(info, *[pair[0] for pair in flat], *[pair[1] for pair in flat])


def turn(values, table, sign):
    lane = lax.broadcasted_iota(jnp.int32, values.shape, 1)
    half = ROT // 2
    partner = jnp.where(
        lane < half, -pltpu.roll(values, 128 - half, 1), pltpu.roll(values, half, 1)
    )
    cosine = jnp.where(lane < ROT, table, 1.0)
    sine = jnp.where(lane < ROT, pltpu.roll(table, ROT, 1), 0.0)
    return values * cosine + partner * (sign * sine)


def project_heads(info, rows, weight, bias, table):
    n, width = rows.shape
    cols = weight.other
    tile = 512

    def body(info_ref, x_ref, b_ref, t_ref, p0, p1, p2, p3, out_ref, w, sem):
        @pl.when(pl.program_id(0) == 0)
        def _():
            fetch(info_ref, (p0, p1, p2, p3), w, sem, weight.block)

        mixed = dot_nn(x_ref[...], w[...]) + b_ref[...]
        for start in range(0, cols, HD):
            head = mixed[:, start : start + 128]
            out_ref[:, start : start + 128] = turn(head, t_ref[...], 1.0).astype(BF)
            out_ref[:, start + 128 : start + HD] = mixed[:, start + 128 : start + HD].astype(BF)

    block = lambda width_of: pl.BlockSpec((tile, width_of), lambda i, s: (i, 0))
    return call(
        body, (n // tile,),
        [block(width), pl.BlockSpec((1, cols), lambda i, s: (0, 0)), block(128)] + [ANY] * 4,
        block(cols), shape_of((n, cols), BF),
        [pltpu.VMEM(weight.shape, BF), pltpu.SemaphoreType.DMA],
        1, 2 * n * width * cols, 2 * n * width + 4 * n * cols, 18,
    )(info, rows, bias, table, *weight.arrays)


def project_values(info, rows, grads, weight, bias):
    n, width = rows.shape
    cols = weight.other
    tile = 512
    steps = n // tile // 2

    def body(info_ref, x_ref, g_ref, h_ref, b_ref, p0, p1, p2, p3, v_ref, d_ref, w, sem):
        step = pl.program_id(0)

        @pl.when(step == 0)
        def _():
            fetch(info_ref, (p0, p1, p2, p3), w, sem, weight.block)

        v_ref[...] = (dot_nn(x_ref[...], w[:, :HD]) + b_ref[...]).astype(BF)

        @pl.when(step < steps)
        def _():
            d_ref[...] = dot_nn(g_ref[...], w[:, HD:]).astype(BF)

        @pl.when(step >= steps)
        def _():
            d_ref[...] = dot_nn(h_ref[...], w[:, HD:]).astype(BF)

    block = lambda width_of: pl.BlockSpec((tile, width_of), lambda i, s: (i, 0))
    return call(
        body, (2 * steps,),
        [block(width)] + halves_specs(tile, width, steps)
        + [pl.BlockSpec((1, HD), lambda i, s: (0, 0))] + [ANY] * 4,
        [block(HD), block(HD)], [shape_of((n, HD), BF)] * 2,
        [pltpu.VMEM(weight.shape, BF), pltpu.SemaphoreType.DMA],
        1, 2 * n * width * cols, 4 * n * width + 2 * n * cols, 24,
    )(info, rows, *grads, bias, *weight.arrays)


def attend(mixed, value, dcontext, table, row_info, col_info):
    n, cols = mixed.shape
    share = n // 16
    lead = (2, 2, 2, MICRO, share)

    def body(q_ref, v_ref, d_ref, t_ref, r_ref, k_ref, ctx_ref, dm_ref, dv_ref, sum_ref):
        @pl.when(pl.program_id(0) == 0)
        def _():
            sum_ref[...] = jnp.zeros_like(sum_ref)

        load = lambda ref: ref[...].reshape(ROWS, ref.shape[-1])
        mixed = load(q_ref)
        query, key, value = mixed[:, :HD], mixed[:, HD:], load(v_ref)
        dctx = load(d_ref)
        angles = load(t_ref)
        allowed = (r_ref[0, :, 0:1] == k_ref[0, 0:1, :]) & (k_ref[0, 1:2, :] <= r_ref[0, :, 1:2])
        scores = jnp.where(allowed, dot_nt(query, key) * SCALE, -1e30)
        expos = jnp.exp(scores - jnp.max(scores, axis=-1, keepdims=True))
        soft = expos / jnp.sum(expos, axis=-1, keepdims=True)
        probs = soft.astype(BF)
        ctx_ref[...] = dot_nn(probs, value).astype(BF).reshape(ctx_ref.shape)
        dprobs = dot_nt(dctx, value)
        dscores = soft * (dprobs - jnp.sum(soft * dprobs, axis=-1, keepdims=True))
        dscores = dscores.astype(BF)
        dvalue = dot_tn(probs, dctx)
        dquery = dot_nn(dscores, key) * SCALE
        dkey = dot_tn(dscores, query) * SCALE
        pieces = []
        for part in (dquery, dkey):
            pieces += [turn(part[:, :128], angles, -1.0), part[:, 128:]]
        low = jnp.concatenate(pieces, axis=1).astype(BF)
        low_value = dvalue.astype(BF)
        dm_ref[...] = low.reshape(dm_ref.shape)
        dv_ref[...] = low_value.reshape(dv_ref.shape)
        sum_ref[:, : 2 * HD] += jnp.sum(low.astype(F32), axis=0, keepdims=True)
        sum_ref[:, 2 * HD :] += jnp.sum(low_value.astype(F32), axis=0, keepdims=True)

    view = lambda a: a.reshape(lead + (a.shape[-1],))
    block = lambda w: pl.BlockSpec(
        (2, 1, 2, 1, share, w), lambda p: (0, p % 2, 0, p // 2, 0, 0)
    )
    info = lambda a: pl.BlockSpec((1,) + a.shape[1:], lambda p: (p, 0, 0))
    packs = MICRO * 2
    context, dmixed, dvalue, sums = call(
        body, (packs,),
        [block(cols), block(HD), block(HD), block(128), info(row_info), info(col_info)],
        [block(HD), block(cols), block(HD), pl.BlockSpec((1, 3 * HD), lambda p: (0, 0))],
        [
            shape_of(lead + (HD,), BF), shape_of(lead + (cols,), BF),
            shape_of(lead + (HD,), BF), shape_of((1, 3 * HD), F32),
        ],
        [], 0, packs * 7 * 2 * ROWS * ROWS * HD, n * cols * 6, 60,
    )(
        view(mixed), view(value), view(dcontext), view(table), row_info, col_info
    )
    return context.reshape(n, HD), dmixed.reshape(n, cols), dvalue.reshape(n, HD), sums


def near_rows(info, near, got):
    rows, cols = near.shape
    half = rows // 2

    def body(info_ref, near_ref, got_ref, own_ref, give_ref):
        def part(k):
            start = pl.multiple_of((info_ref[9] ^ k) * half, half)
            got = got_ref[pl.ds(start, half), :].astype(F32)
            return jnp.where(info_ref[4] == 1, got, 0.0)

        own_ref[...] = near_ref[half:, :].astype(F32) + part(0)
        give_ref[...] = (near_ref[:half, :].astype(F32) + part(1)).astype(BF)

    whole = pl.BlockSpec((rows, cols), lambda i, s: (0, 0))
    out = pl.BlockSpec((half, cols), lambda i, s: (0, 0))
    return call(
        body, (1,), [whole, whole], [out, out],
        [shape_of((half, cols), F32), shape_of((half, cols), BF)],
        [], 1, rows * cols, rows * cols * 4, 14,
    )(info, near, got)


def own_rows(info, owns, gots):
    rows, cols = owns[0].shape
    half = rows // 2
    count = len(owns)

    def body(info_ref, *refs):
        own_refs, got_refs = refs[:count], refs[count : 2 * count]
        mine_ref, give_ref = refs[2 * count :]

        def part(k, i):
            start = pl.multiple_of((info_ref[10] ^ k) * half, half)
            at = pl.ds(start, half)
            return own_refs[i][at, :] + got_refs[i][at, :].astype(F32)

        for i in range(count):
            mine_ref[:, i * cols : (i + 1) * cols] = part(0, i)
            give_ref[:, i * cols : (i + 1) * cols] = part(1, i).astype(BF)

    whole = pl.BlockSpec((rows, cols), lambda i, s: (0, 0))
    out = pl.BlockSpec((half, count * cols), lambda i, s: (0, 0))
    return call(
        body, (1,), [whole] * (2 * count), [out, out],
        [shape_of((half, count * cols), F32), shape_of((half, count * cols), BF)],
        [], 1, rows * cols, count * rows * cols * 6, 16,
    )(info, *owns, *gots)


def place_columns(info, outs, pieces):
    flat = [array for mine, theirs, _ in pieces for array in (mine, theirs)]

    def body(info_ref, *refs):
        ins, out_refs = refs[: len(flat)], refs[len(flat) :]
        for i, (_, _, cuts) in enumerate(pieces):
            for side in (0, 1):
                ref = ins[2 * i + side]
                for first, count, out, offset, stride in cuts:
                    start = pl.multiple_of((info_ref[10] ^ side) * stride + offset, 128)
                    value = ref[:, first : first + count].astype(F32)
                    if outs[out][1]:
                        out_refs[out][pl.ds(start, count), :] = value.T
                    else:
                        out_refs[out][:, pl.ds(start, count)] = value

    return call(
        body, (1,),
        [pl.BlockSpec(array.shape, lambda i, s: (0, 0)) for array in flat],
        [pl.BlockSpec(shape, lambda i, s: (0, 0)) for shape, _ in outs],
        [shape_of(shape, F32) for shape, _ in outs],
        [], 1, 1000, 1000, 30,
    )(info, *flat)


def row_kernel(info, got, parts, weights, rows_in, whole_in, sums, finish, vmem):
    keep = len(got) > 0
    n = parts[0][0].shape[0] // 2
    width = weights[0].shape[0]
    tile = 256
    half_tile = n // 8
    steps = n // tile
    n_rows, n_whole = len(rows_in), len(whole_in)
    n_parts, n_weights = len(parts), len(weights)
    n_outs = 4 if keep else 2

    def body(info_ref, *refs):
        def pairs(count, refs):
            return [(refs[2 * i], refs[2 * i + 1]) for i in range(count)], refs[2 * count :]

        row_refs, refs = pairs(n_rows, refs)
        part_refs, refs = pairs(n_parts, refs)
        whole_refs, refs = refs[:n_whole], refs[n_whole:]
        got_refs, refs = refs[: len(got)], refs[len(got) :]
        w_refs, refs = refs[: 4 * n_weights], refs[4 * n_weights :]
        outs, refs = refs[:n_outs], refs[n_outs:]
        sum_refs, scratch, sem = refs[: len(sums)], refs[len(sums) : -1], refs[-1]
        step = pl.program_id(0)
        first = step == 0
        load = lambda pair: jnp.concatenate([pair[0][...], pair[1][...]])

        @pl.when(first)
        def _():
            for i, weight in enumerate(weights):
                fetch(info_ref, w_refs[4 * i : 4 * i + 4], scratch[i], sem, weight.block)

        def product(i):
            array, index, start = parts[i]
            return dot_nt(load(part_refs[i]), scratch[index][:, start : start + array.shape[1]])

        rows = [load(pair) for pair in row_refs]
        total = finish(first, rows, whole_refs, product, sum_refs)
        if keep:
            for k in range(4):

                @pl.when(step == k)
                def _(k=k):
                    outs[k][...] = (total + got_refs[k // 2][...].astype(F32)).astype(BF)

        else:
            for k in range(2):

                @pl.when(step // 2 == k)
                def _(k=k):
                    outs[k][...] = total.astype(BF)

    def row(w, local):
        base = 0 if keep or local else 8
        return [
            pl.BlockSpec((half_tile, w), lambda i, s: (base + s[11 + i], 0)),
            pl.BlockSpec((half_tile, w), lambda i, s: (base + s[15 + i], 0)),
        ]

    twice = lambda arrays: [array for array in arrays for _ in range(2)]
    ks = sum(part[0].shape[1] for part in parts)
    fixed = pl.BlockSpec((tile, width), lambda i, s: (0, 0))
    pair = [
        pl.BlockSpec((tile, width), lambda i, s: (jnp.minimum(i, 1), 0)),
        pl.BlockSpec((tile, width), lambda i, s: (jnp.maximum(i - 2, 0), 0)),
    ]
    if keep:
        out_specs, out_shape = [fixed] * 4, [shape_of((tile, width), BF)] * 4
    else:
        out_specs, out_shape = pair, [shape_of((2 * tile, width), BF)] * 2
    return call(
        body, (steps,),
        [spec for array in rows_in for spec in row(array.shape[1], True)]
        + [spec for part in parts for spec in row(part[0].shape[1], False)]
        + [pl.BlockSpec(array.shape, lambda i, s: (0, 0)) for array in whole_in]
        + pair[: len(got)] + [ANY] * (4 * n_weights),
        out_specs + [pl.BlockSpec(shape, lambda i, s: (0, 0)) for shape in sums],
        out_shape + [shape_of(shape, F32) for shape in sums],
        [pltpu.VMEM(weight.shape, BF) for weight in weights] + [pltpu.SemaphoreType.DMA],
        1, 2 * n * width * ks, 2 * n * (2 * width + ks), vmem,
    )(
        info, *twice(rows_in), *twice([part[0] for part in parts]), *whole_in, *got,
        *[array for weight in weights for array in weight.arrays],
    )


def out_rows(info, parts, weights, got):
    def finish(first, rows, whole, product, sums):
        total = product(0)
        for i in range(1, len(parts)):
            total += product(i)
        return total

    return row_kernel(info, got, parts, weights, [], [], [], finish, 60 if got else 60)


def back_rows(info, parts, weights, n_attn, x, vectors, got):
    def finish(first, rows, whole, product, sums):
        v_ref, sum_ref = whole[0], sums[0]

        @pl.when(first)
        def _():
            sum_ref[...] = jnp.zeros_like(sum_ref)

        plain, _ = plain_of(rows[-1].astype(F32))
        dattn = product(0)
        for i in range(1, n_attn):
            dattn += product(i)
        dmlp = product(n_attn)
        for i in range(n_attn + 1, len(parts)):
            dmlp += product(i)
        for i, grad in enumerate((dattn, dmlp)):
            sum_ref[2 * i : 2 * i + 1] += jnp.sum(grad * plain, axis=0, keepdims=True)
            sum_ref[2 * i + 1 : 2 * i + 2] += jnp.sum(grad, axis=0, keepdims=True)
        return dattn * v_ref[0:1] + dmlp * v_ref[2:3]

    return row_kernel(
        info, got, parts, weights, [x], [vectors], [(4, vectors.shape[1])], finish,
        60 if got else 60,
    )


class Names:

    def __init__(self, mark):
        self.mark = mark

    def __getattr__(self, name):
        return self.mark + name


RUN, WAIT = Names(""), Names("-")
ORDER = [
    RUN.vy, RUN.y01, RUN.xx, RUN.xc0, WAIT.vy, RUN.vz1, RUN.tab,
    WAIT.y01, RUN.a0, RUN.xy, WAIT.vz1, RUN.vz2, RUN.a1, WAIT.xx,
    RUN.xc1, RUN.xd1, WAIT.a0, RUN.b0, WAIT.vz2, RUN.y2, WAIT.xy,
    RUN.xc2, RUN.xd2, WAIT.a1, WAIT.b0, RUN.c0, RUN.b1, RUN.gx,
    WAIT.xc0, WAIT.xc1, WAIT.xc2, WAIT.xd1, WAIT.xd2, RUN.xc3, WAIT.y2,
    RUN.a2, RUN.gy, WAIT.xc3, RUN.xs, RUN.norm, WAIT.gx, RUN.gc1,
    RUN.y3, WAIT.c0, WAIT.b1, RUN.c1, RUN.feed0, WAIT.y3, RUN.a3,
    WAIT.a2, RUN.b2, WAIT.gy, RUN.gc2, RUN.gd1, RUN.gd2, RUN.gc0,
    WAIT.c1, WAIT.gd1, WAIT.gd2, RUN.gc3, RUN.y45, WAIT.b2, WAIT.a3,
    RUN.b3, WAIT.gc0, WAIT.gc1, WAIT.gc2, WAIT.gc3, RUN.gs, RUN.go0,
    RUN.c2r0, WAIT.y45, RUN.a4, RUN.fb0, RUN.gi0, WAIT.b3, RUN.c3r1,
    WAIT.c2r0, RUN.p0, RUN.heads, WAIT.c3r1, RUN.val, WAIT.p0, RUN.q0,
    WAIT.a4, RUN.b4, RUN.a5, RUN.att, WAIT.q0, RUN.gqk, WAIT.b4,
    RUN.c4r2, RUN.p1, WAIT.a5, RUN.b5, RUN.gvp, WAIT.b5, RUN.c5r3,
    WAIT.c4r2, RUN.p2, RUN.feed1, RUN.go1, RUN.r4, WAIT.p1, RUN.q1,
    WAIT.c5r3, RUN.p3, RUN.fb1, RUN.gi1, RUN.og, RUN.oc, WAIT.q1,
    RUN.f01, WAIT.p2, RUN.q2, RUN.r5, RUN.bg, RUN.hc, WAIT.r4,
    RUN.p4, WAIT.oc, RUN.ok, WAIT.p3, RUN.q3, RUN.o1y, RUN.o1x,
    WAIT.hc, WAIT.f01, WAIT.r5, RUN.p5, RUN.bk, RUN.h1y, RUN.h1x,
    WAIT.p4, RUN.q4, WAIT.p5, RUN.q5, WAIT.o1y, WAIT.o1x, RUN.o2x,
    RUN.o2y, WAIT.q2, WAIT.q3, RUN.f23, RUN.vs, RUN.vc, WAIT.vc,
    RUN.vx, WAIT.h1y, WAIT.h1x, RUN.h2x, RUN.h2y, WAIT.q4, WAIT.q5,
    RUN.f45, WAIT.vx, RUN.vyy, WAIT.o2x, WAIT.o2y, RUN.fo, WAIT.vyy,
    RUN.vz, WAIT.f23, WAIT.h2x, WAIT.h2y, RUN.fr, WAIT.vz, RUN.fv,
    WAIT.f45, RUN.fw,
]


def layer_program(n_dp, n_tensor):
    n_z = n_dp // 2
    n_dev = n_dp * n_tensor
    core, xbit, ybit, zbit = 1, 2, 4, 8
    ids = range(n_dev)
    flip = lambda bit: [(i, i ^ bit) for i in ids]
    flip_c, flip_x, flip_y, flip_z = flip(core), flip(xbit), flip(ybit), flip(zbit)
    mirror = {0: 0, 1: 2, 2: 1, 3: 3}
    mid = [
        (i, mirror[i // zbit] * zbit + (i % zbit if i // zbit in (1, 2) else i % zbit ^ core))
        for i in ids if n_z == 4
    ]
    columns = [[z * 2 + y for z in range(n_z)] for y in range(2)]

    def per_device(
        tokens, lengths, out_grad, attn_gain, attn_shift, mlp_gain, mlp_shift,
        w_qkv, b_qkv, w_proj, b_proj, w_in, b_in, w_out, b_out,
    ):
        dp = lax.axis_index("dp")
        tensor = lax.axis_index("tensor")
        z, y = dp // 2, dp % 2
        x, c = tensor // 2, tensor % 2
        share = tokens.shape[1]
        width = tokens.shape[2]
        upper = z >= 2
        even = z % 2 == 0
        token = []
        is_mid = (z == 1) | (z == 2)

        def turn_of(*values):
            out = lax.optimization_barrier(values + tuple(token))[: len(values)] if token else values
            return out if len(out) > 1 else out[0]

        def passed(*values):
            token.extend(values)

        def worked(*values):
            token[:] = values

        if n_z == 4:
            far = jnp.where(upper, 1, 2)
            low_far = jnp.where(upper, 0, 2)
            places_z = [z, z ^ 1, far, far ^ 1, is_mid, low_far, low_far + 1, z ^ 1, z]
        else:
            places_z = [0, 1, 2, 3, 1, 0, 1, 2, 3]
        info = jnp.stack(
            [jnp.asarray(v, jnp.int32) for v in places_z + [z % 2, y, 4, 3, 0, 1, 6, 7, 2, 5]]
        )

        h_cols = w_in.shape[1] // 2
        half_h = h_cols // 2
        q_cols = w_qkv.shape[1] // 2
        p_cols = w_proj.shape[0] // 2

        w_out_t, w_proj_t = w_out.T, w_proj.T
        cuts = [
            [(w_in, h_cols, 0, half_h)],
            [(w_out_t, h_cols, 0, half_h)],
            [(w_qkv, q_cols, 0, 2 * HD)],
            [(w_qkv, q_cols, 2 * HD, HD), (w_proj_t, p_cols, 0, p_cols)],
            [(w_in, h_cols, half_h, half_h)],
            [(w_out_t, h_cols, half_h, half_h)],
        ]
        V = {}

        def side_of(k, side):
            parts = [
                lax.dynamic_slice_in_dim(weight, side * sub + start, count, 1)
                for weight, sub, start, count in cuts[k]
            ]
            return parts[0] if len(parts) == 1 else jnp.concatenate(parts, axis=1)

        def send_y(name, chunks):
            theirs = jnp.concatenate([side_of(k, 1 - y) for k in chunks], axis=1)
            V[name] = swap(turn_of(theirs), flip_y)
            start = 0
            for k in chunks:
                mine = side_of(k, y)
                V[RUN.source, k] = (name, mine, start)
                start += mine.shape[1]

        def step_a(k):
            name, mine, start = V[RUN.source, k]
            got = turn_of(V[name])
            pair = ordered(y == 0, mine, got[:, start : start + mine.shape[1]])
            V[RUN.pair, k] = pair
            V["a%d" % k] = swap(pair, flip_z) if n_z == 4 else pair

        def step_b(k):
            both = jnp.concatenate(turn_of(V[RUN.pair, k], V["a%d" % k]))
            V["b%d" % k] = swap(both, mid) if n_z == 4 else both

        def cross(k, j, name):
            if n_z == 4:
                if j is None:
                    payload = turn_of(V["b%d" % k])
                elif k is None:
                    payload = turn_of(V[RUN.sum, j][0])
                else:
                    payload = jnp.where(is_mid, *turn_of(V["b%d" % k], V[RUN.sum, j][0]))
                got = swap(payload, flip_z)
            else:
                got = turn_of(V["b%d" % k] if j is None else V[RUN.sum, j][0])
            V[name] = got
            if k is not None:
                V[RUN.arrived, k] = name
            if j is not None:
                V[RUN.crossed, j] = name

        def full(k):
            if n_z == 4:
                arrays = (
                    V[RUN.pair, k], V["a%d" % k], V["b%d" % k], V[V[RUN.arrived, k]]
                )
            else:
                whole = lax.all_gather(
                    V[RUN.pair, k], "dp", axis_index_groups=columns, tiled=True
                )
                quarter = jnp.split(whole, 4)
                half = jnp.concatenate(quarter[2:])
                arrays = (quarter[0], quarter[1], half, half)
            return Gathered(arrays)

        def step_p(j):
            far, got = turn_of(V[RUN.sum, j][0], V[V[RUN.crossed, j]])
            far = (far.astype(F32) + got.astype(F32)).astype(BF)
            V["p%d" % j] = swap(far, mid) if n_z == 4 else far

        def step_q(j):
            near, got = turn_of(V[RUN.sum, j][1], V["p%d" % j])
            if n_z == 4:
                V[RUN.own, j], give = near_rows(info, near, got)
                V["q%d" % j] = swap(give, flip_z)
            else:
                own = lax.psum_scatter(
                    jnp.concatenate([V[RUN.sum, j][0], near]), "dp", scatter_dimension=0,
                    axis_index_groups=columns, tiled=True,
                ).astype(F32)
                V[RUN.own, j], V["q%d" % j] = own, jnp.zeros_like(own, BF)

        def step_f(a, b, name):
            values = turn_of(V[RUN.own, a], V[RUN.own, b], V["q%d" % a], V["q%d" % b])
            V[RUN.mine, name], give = own_rows(info, values[:2], values[2:])
            V[name] = swap(give, flip_y)

        def plane_core(name, k, own):
            g = name[0]
            part = own if k == 0 else V[g + "xy"[k - 1]] if k < 3 else None
            if k == 3:
                part = jnp.concatenate(turn_of(V[g + "d1"], V[g + "d2"]))
            else:
                part = turn_of(part)
            V[g + "part", k] = part.reshape(-1, width)
            V[name] = swap(V[g + "part", k], flip_c)

        def plane_rows(g):
            parts = [V[g + "part", k] for k in range(4)] + [V["%sc%d" % (g, k)] for k in range(4)]
            V[g + "mine"], V[g + "c"] = stack_rows(turn_of(*parts))
            worked(V[g + "mine"])

        def send_core(name, parts):
            V[name] = tuple(swap(part, flip_c) for part in turn_of(*parts))

        def sum_first(g, name, perm, at):
            value = turn_of(V[g + "keep"][at]).reshape(2, share, width)
            V[g + name] = swap(value, perm)

        def sum_second(g, name, perm, at):
            got = turn_of(V[g + ("1y", "1x")[at]])
            total = V[g + "keep"][2 + at].reshape(2, share, width).astype(F32) + got.astype(F32)
            V[g + "left", at] = total[0]
            V[g + name] = swap(total[1].astype(BF), perm)

        def sum_result(g):
            got = turn_of(V[g + "2x"], V[g + "2y"])
            return jnp.stack([V[g + "left", at] + got[at].astype(F32) for at in (0, 1)])

        own_places = tensor * share + jnp.arange(share, dtype=jnp.int32)
        own_ends = jnp.cumsum(lengths[:, 0], axis=-1)
        own_segment = jnp.sum((own_places[:, None] >= own_ends[:, None, :]).astype(jnp.int32), axis=-1)
        valid = (own_segment < SEGS - 1).astype(F32)[..., None]
        x_own = tokens.astype(F32)
        g_own = out_grad.astype(F32) * valid
        g_low = g_own.astype(BF).reshape(MICRO, share, width)
        x_low = tokens.reshape(MICRO, share, width)
        bias_in = lax.dynamic_slice_in_dim(b_in, y * h_cols, h_cols).astype(F32)[None]
        bias_qkv = lax.dynamic_slice_in_dim(b_qkv, y * q_cols, q_cols).astype(F32)[None]
        pair_bits = jnp.arange(2, dtype=jnp.int32)
        t_of = (x ^ pair_bits)[None, :] * 2 + (c ^ pair_bits)[:, None]
        places = (t_of[..., None] * share + jnp.arange(share, dtype=jnp.int32)).reshape(-1)

        def send_vectors():
            vectors = jnp.stack([attn_gain, attn_shift, mlp_gain, mlp_shift, b_proj, b_out])
            V[RUN.vectors] = vectors
            V[RUN.vy] = swap(turn_of(vectors), flip_y)
            V[RUN.lengths] = swap(turn_of(lengths[:, 0]), flip_y)

        def send_vectors_z(name, bit, low_first):
            if name == "vz1":
                pair = ordered(y == 0, V[RUN.vectors][None], turn_of(V[RUN.vy])[None])
                if n_z != 4:
                    V[RUN.vz1] = V[RUN.vz2] = pair
                    V[RUN.small] = lax.all_gather(
                        pair, "dp", axis_index_groups=columns, tiled=True
                    )
                    return
            elif n_z != 4:
                return
            else:
                pair = ordered(even, V[RUN.vectors_y], turn_of(V[RUN.vz1]))
            V["vectors_y" if name == "vz1" else "vectors_z"] = pair
            V[name] = swap(pair, flip(bit))

        def send_part(name, value, perm, index=None):
            def run():
                part = turn_of(value if index is None else V[value])
                V[name] = swap(part if index is None else part[index], perm)

            return run

        def send_sums_c():
            V[RUN.vc] = swap_half("total", 3, c, flip_c, "vc")

        def swap_half(source, axis, bit, perm, name):
            total = turn_of(V[source])
            low, high = jnp.split(total, 2, axis=axis)
            got = swap(jnp.where(bit == 0, high, low), perm)
            V["half " + name] = jnp.where(bit == 0, low, high)
            return got

        def send_sums_x():
            V["total x"] = V["half vc"] + turn_of(V[RUN.vc])
            V[RUN.vx] = swap_half("total x", 2, x, flip_x, "vx")

        def send_sums_y():
            V["total y"] = V["half vx"] + turn_of(V[RUN.vx])
            V[RUN.vyy] = swap_half("total y", 1, y, flip_y, "vyy")

        def send_sums_z():
            total = (V["half vyy"] + turn_of(V[RUN.vyy])).reshape(n_z, -1)
            if n_z == 4:
                row = lambda k: lax.dynamic_slice_in_dim(total, z ^ k, 1, 0)
                V[RUN.row] = row(0)
                V[RUN.vz] = tuple(swap(row(k), flip(zbit * k)) for k in (1, 2, 3))
            else:
                V[RUN.row] = lax.psum_scatter(
                    total.reshape(-1), "dp", axis_index_groups=columns, tiled=True
                )
                V[RUN.vz] = ()

        def norm():
            if n_z == 4:
                small = ordered(~upper, V[RUN.vectors_z], turn_of(V[RUN.vz2]))
            else:
                small = V[RUN.small]
            small = small.transpose(1, 0, 2).reshape(6, width).astype(F32)
            V[RUN.small] = jnp.concatenate([small, jnp.zeros((2, width), F32)])
            V[RUN.attn], V[RUN.mlp] = norm_rows(turn_of(V[RUN.xmine]), V[RUN.xc], V[RUN.small])
            worked(V[RUN.attn])

        def tab():
            lengths_all = jnp.stack([lengths[:, 0], turn_of(V[RUN.lengths])])
            ends = jnp.cumsum(lengths_all, axis=-1)
            gone = (places[:, None] >= ends[..., None, :]).astype(jnp.int32)
            segment = jnp.sum(gone, axis=-1)
            position = places - jnp.sum(gone * lengths_all[..., None, :], axis=-1)
            row_position = position.reshape(2, MICRO, 2, 2, share).transpose(2, 0, 3, 1, 4)
            lanes = jnp.arange(2 * ROT)
            frequency = 10000.0 ** (-2.0 * (lanes % (ROT // 2)).astype(F32) / ROT)
            angle = row_position.reshape(-1).astype(F32)[:, None] * frequency
            table = jnp.where(lanes < ROT, jnp.cos(angle), jnp.sin(angle))
            pack_segment = segment.transpose(1, 0, 2).reshape(MICRO * 2, ROWS)
            pack_places = jnp.broadcast_to(places, (MICRO * 2, ROWS))
            row_info = jnp.stack([pack_segment, pack_places], axis=2)
            col_info = jnp.stack([pack_segment, pack_places], axis=1)
            V[RUN.table] = lax.optimization_barrier((table, row_info, col_info))
            worked(*V[RUN.table])

        def run_feed(i, k):
            bias = bias_in[:, i * half_h : (i + 1) * half_h]
            V[RUN.active, i], V[RUN.slope, i] = feed(info, turn_of(V[RUN.mlp]), full(k), bias)
            worked(V[RUN.active, i])

        def sums_of(j, *groups):
            V[RUN.sum, j] = weight_grad(info, list(groups))
            worked(V[RUN.sum, j][0])

        def halves_of(value):
            rows = turn_of(V[RUN.gmine]), V[RUN.gc]
            return [(rows[0], value, 0), (rows[1], value, 1)]

        def run_back(i, k):
            rows = turn_of(V[RUN.gmine]), V[RUN.gc]
            V[RUN.dhidden, i], V[RUN.dsum, i] = feed_back(info, rows, full(k), V[RUN.slope, i])
            worked(V[RUN.dhidden, i])

        def heads():
            V[RUN.mixed] = project_heads(
                info, turn_of(V[RUN.attn]), full(2), bias_qkv[:, : 2 * HD], V[RUN.table][0]
            )
            worked(V[RUN.mixed])

        def val():
            V[RUN.value], V[RUN.dcontext] = project_values(
                info, turn_of(V[RUN.attn]), (V[RUN.gmine], V[RUN.gc]), full(3), bias_qkv[:, 2 * HD :]
            )
            worked(V[RUN.value])

        def att():
            V[RUN.context], V[RUN.dmixed], V[RUN.dvalue], V["dmixed sum"] = attend(
                turn_of(V[RUN.mixed]), V[RUN.value], V[RUN.dcontext], *V[RUN.table]
            )
            worked(V[RUN.context])

        def run_out(keep):
            parts = [(turn_of(V[RUN.context]), 0, HD), (V[RUN.active, 0], 1, 0), (V[RUN.active, 1], 2, 0)]
            got = turn_of(*V[RUN.oc]) if keep else ()
            outs = out_rows(info, parts, (full(3), full(1), full(5)), got)
            V["okeep" if keep else "ogive"] = outs
            worked(outs[0])

        def run_rows(keep):
            parts = [
                (turn_of(V[RUN.dmixed]), 0, 0), (V[RUN.dvalue], 1, 0),
                (V[RUN.dhidden, 0], 2, 0), (V[RUN.dhidden, 1], 3, 0),
            ]
            got = turn_of(*V[RUN.hc]) if keep else ()
            outs = back_rows(
                info, parts, (full(2), full(3), full(0), full(4)), 2,
                V[RUN.xmine] if keep else V[RUN.xc], V[RUN.small], got,
            )
            V["hkeep" if keep else "hgive"] = outs[:-1]
            V[RUN.sums, keep] = outs[-1]
            worked(outs[0])

        def vector_total():
            g_sum = jnp.sum(turn_of(g_own), axis=(0, 1))[None]
            sums = jnp.concatenate([turn_of(V[RUN.sums, True]) + V[RUN.sums, False], g_sum])
            sums = sums.reshape(5, n_dev, -1).transpose(1, 0, 2).reshape(n_dev, -1)
            dhidden_sum = jnp.concatenate([V[RUN.dsum, 0], V[RUN.dsum, 1]], axis=1)
            bias_sums = jnp.concatenate(
                [
                    dhidden_sum.reshape(n_dp // 2, -1),
                    V["dmixed sum"].reshape(n_dp // 2, -1),
                ],
                axis=-1,
            )
            spread_bias = jnp.zeros((n_dp, n_tensor, bias_sums.shape[-1]), F32)
            spread_bias = lax.dynamic_update_slice(
                spread_bias, bias_sums[:, None], (y * (n_dp // 2), tensor, 0)
            ).reshape(n_dev, -1)
            total = jnp.concatenate([sums, spread_bias], axis=-1)
            V[RUN.total] = total.reshape(n_z, 2, 2, 2, -1)
            worked(V[RUN.total])

        def result_output():
            small = V[RUN.small]
            V[RUN.output] = (x_own + sum_result("o") + small[4] + small[5]).astype(BF)
            worked(V[RUN.output])

        def result_tokens():
            back = sum_result("h")
            own_plain, own_spread = plain_of(x_own)
            V["grad tokens"] = g_own + own_spread * (
                back
                - jnp.mean(back, axis=-1, keepdims=True)
                - own_plain * jnp.mean(back * own_plain, axis=-1, keepdims=True)
            )
            worked(V["grad tokens"])

        def result_weights():
            rest = half_h
            V[RUN.weights] = place_columns(
                info,
                [
                    (w_qkv.shape, False), (w_proj.shape, True),
                    (w_in.shape, False), (w_out.shape, True),
                ],
                [
                    (V[RUN.mine, "f01"], turn_of(V[RUN.f01]),
                     [(0, rest, 3, 0, h_cols), (rest, rest, 2, 0, h_cols)]),
                    (V[RUN.mine, "f23"], turn_of(V[RUN.f23]),
                     [(0, 2 * HD, 0, 0, q_cols), (2 * HD, HD, 0, 2 * HD, q_cols),
                      (3 * HD, p_cols, 1, 0, p_cols)]),
                    (V[RUN.mine, "f45"], turn_of(V[RUN.f45]),
                     [(0, rest, 3, half_h, h_cols), (rest, rest, 2, half_h, h_cols)]),
                ],
            )
            worked(V[RUN.weights][0])

        def result_vectors():
            total = V[RUN.row]
            for got in V[RUN.vz]:
                total = total + turn_of(got)
            V["vector sums"] = total.reshape(-1)

        steps = dict(
            y01=lambda: send_y("y01", (0, 1)),
            y2=lambda: send_y("y2", (2,)),
            y3=lambda: send_y("y3", (3,)),
            y45=lambda: send_y("y45", (4, 5)),
            vy=send_vectors,
            vz1=lambda: send_vectors_z("vz1", zbit, even),
            vz2=lambda: send_vectors_z("vz2", 2 * zbit, ~upper),
            xx=send_part("xx", x_low, flip_x),
            xy=send_part("xy", x_low, flip_y),
            xd1=send_part("xd1", "xx", flip_y, 0),
            xd2=send_part("xd2", "xy", flip_x, 1),
            xs=lambda: plane_rows("x"),
            gx=send_part("gx", g_low, flip_x),
            gy=send_part("gy", g_low, flip_y),
            gd1=send_part("gd1", "gx", flip_y, 0),
            gd2=send_part("gd2", "gy", flip_x, 1),
            gs=lambda: plane_rows("g"),
            norm=norm, tab=tab, heads=heads, val=val, att=att,
            feed0=lambda: run_feed(0, 0),
            feed1=lambda: run_feed(1, 4),
            fb0=lambda: run_back(0, 1),
            fb1=lambda: run_back(1, 5),
            go0=lambda: sums_of(0, halves_of(V[RUN.active, 0])),
            gi0=lambda: sums_of(1, [(turn_of(V[RUN.mlp]), V[RUN.dhidden, 0], 0)]),
            gqk=lambda: sums_of(2, [(turn_of(V[RUN.attn]), V[RUN.dmixed], 0)]),
            gvp=lambda: sums_of(
                3, [(turn_of(V[RUN.attn]), V[RUN.dvalue], 0)], halves_of(V[RUN.context])
            ),
            go1=lambda: sums_of(4, halves_of(V[RUN.active, 1])),
            gi1=lambda: sums_of(5, [(turn_of(V[RUN.mlp]), V[RUN.dhidden, 1], 0)]),
            og=lambda: run_out(False), ok=lambda: run_out(True),
            bg=lambda: run_rows(False), bk=lambda: run_rows(True),
            f01=lambda: step_f(0, 1, "f01"),
            f23=lambda: step_f(2, 3, "f23"),
            f45=lambda: step_f(4, 5, "f45"),
            vs=vector_total, vc=send_sums_c, vx=send_sums_x,
            vyy=send_sums_y, vz=send_sums_z, fv=result_vectors,
            fo=result_output, fr=result_tokens, fw=result_weights,
        )
        for g in "oh":
            steps[g + "c"] = lambda g=g: send_core(g + "c", V[g + "give"])
            steps[g + "1y"] = lambda g=g: sum_first(g, "1y", flip_y, 0)
            steps[g + "1x"] = lambda g=g: sum_first(g, "1x", flip_x, 1)
            steps[g + "2x"] = lambda g=g: sum_second(g, "2x", flip_x, 0)
            steps[g + "2y"] = lambda g=g: sum_second(g, "2y", flip_y, 1)
        for k in range(4):
            steps["xc%d" % k] = lambda k=k: plane_core("xc%d" % k, k, x_low)
            steps["gc%d" % k] = lambda k=k: plane_core("gc%d" % k, k, g_low)
        for k in range(6):
            steps["a%d" % k] = lambda k=k: step_a(k)
            steps["b%d" % k] = lambda k=k: step_b(k)
            steps["c%d" % k] = lambda k=k: cross(k, None, "c%d" % k)
            steps["r%d" % k] = lambda k=k: cross(None, k, "r%d" % k)
            steps["p%d" % k] = lambda k=k: step_p(k)
            steps["q%d" % k] = lambda k=k: step_q(k)
            for j in range(6):
                name = "c%dr%d" % (k, j)
                steps[name] = lambda k=k, j=j, name=name: cross(k, j, name)
        for word in ORDER:
            if word[0] == "-":
                value = V[word[1:]]
                extra = (V[RUN.lengths],) if word == "-vy" else ()
                passed(*(value if isinstance(value, tuple) else (value,)), *extra)
            else:
                steps[word]()

        piece = width // n_dev
        sums = V["vector sums"]
        pieces = [sums[k * piece : (k + 1) * piece] for k in range(5)]
        bias_piece = sums[5 * piece :]
        in_piece = b_in.shape[0] // n_dp
        grad_qkv, grad_proj, grad_in, grad_out = V[RUN.weights]
        return (
            V[RUN.output], V["grad tokens"], pieces[0], pieces[1], pieces[2], pieces[3],
            grad_qkv, bias_piece[in_piece:].reshape(1, -1), grad_proj, pieces[4],
            grad_in, bias_piece[:in_piece].reshape(1, -1), grad_out, pieces[4],
        )

    return per_device


def solution(mesh):
    n_dp, n_tensor = mesh.shape["dp"], mesh.shape["tensor"]
    rows = P(None, AXES, None)
    in_specs = (
        rows, P(None, "dp", None), rows, P("dp"), P("dp"), P("dp"), P("dp"),
        P("dp", "tensor"), P("tensor"), P("tensor", "dp"), P("dp"),
        P("dp", "tensor"), P("tensor"), P("tensor", "dp"), P("dp"),
    )
    vector = P(AXES)
    out_specs = (
        rows, rows, vector, vector, vector, vector,
        P("dp", "tensor"), P("tensor", "dp"), P("tensor", "dp"), vector,
        P("dp", "tensor"), P("tensor", "dp"), P("tensor", "dp"), vector,
    )
    return jax.shard_map(
        layer_program(n_dp, n_tensor), mesh=mesh,
        in_specs=in_specs, out_specs=out_specs, check_vma=False,
    )
```
